32 devices in a mesh: dp: 16 (over z, y, x), mp: 2 (over core).
Axes of the slice: x: 2, y: 2, z: 4, core: 2. Of those that a mesh axis runs over, the one named last changes fastest.
Arguments:
- layer_input_rows: bfloat16 [20480, 768], P(('dp', 'mp')), may hold values from -6 to 6
- resolution: int32 [32], P(('dp', 'mp')), may hold values from 0 to 1
- attn_gain: float32 [768], replicated, may hold values from 0.1 to 1.9
- attn_bias: float32 [768], replicated, may hold values from -3 to 3
- qkv_weight: bfloat16 [768, 2304], replicated, may hold values from -0.3125 to 0.3125
- qv_bias: float32 [2, 768], replicated, may hold values from -3 to 3
- out_weight: bfloat16 [768, 768], replicated, may hold values from -0.875 to 0.875
- out_bias: float32 [768], replicated, may hold values from -3 to 3
- attn_scale: float32 [768], replicated, may hold values from 0.5 to 1.5
- ffn_scale: float32 [768], replicated, may hold values from 0.5 to 1.5
- ffn_gain: float32 [2, 768], replicated, may hold values from 0.1 to 1.9
- ffn_bias: float32 [2, 768], replicated, may hold values from -3 to 3
- up_weight: bfloat16 [2, 768, 3072], P(None, 'dp', 'mp'), may hold values from -0.21875 to 0.21875
- up_bias: float32 [2, 3072], P(None, 'mp'), may hold values from -3 to 3
- down_weight: bfloat16 [2, 768, 3072], P(None, 'dp', 'mp'), may hold values from -0.109375 to 0.109375
- down_bias: float32 [2, 768], replicated, may hold values from -3 to 3
- output_gradient: bfloat16 [20480, 768], P(('dp', 'mp')), may hold values from -6 to 6
Outputs:
- block_output: bfloat16 [20480, 768], P(('dp', 'mp'))
- input_grad: bfloat16 [20480, 768], P(('dp', 'mp'))
- attn_gain_grad: float32 [768], replicated
- attn_bias_grad: float32 [768], replicated
- qkv_weight_grad: float32 [768, 2304], P(('dp', 'mp'))
- qv_bias_grad: float32 [2, 768], replicated
- out_weight_grad: float32 [768, 768], P(('dp', 'mp'))
- out_bias_grad: float32 [768], replicated
- attn_scale_grad: float32 [768], replicated
- ffn_scale_grad: float32 [768], replicated
- ffn_gain_grad: float32 [2, 768], replicated
- ffn_bias_grad: float32 [2, 768], replicated
- up_weight_grad: float32 [2, 768, 3072], P(None, 'dp', 'mp')
- up_bias_grad: float32 [2, 3072], replicated
- down_weight_grad: float32 [2, 768, 3072], P(None, 'dp', 'mp')
- down_bias_grad: float32 [2, 768], replicated
The draws below stay inside these ranges and needn't reach their ends.
All inputs are finite; a program needn't handle non-finite values.
Results may differ from the reference program's by a relative error of at most 0.014.
The reference program's roundings to bfloat16 on the way count: a program that leaves them out, or rounds other values in their place, can miss the bound.
Values may be sent and summed in bfloat16 or wider, within the bound.
A program may use at most 256 MiB of HBM per device.

```python
import jax
import jax.numpy as jnp
from jax import lax

MODEL_WIDTH = 768
HEADS = 12
HEAD = 64
FF = 3072
PATCH_SMALL = 197
PATCH_LARGE = 577
CAPTION = 40
ROWS_PER_SLOT = 640
SLOT_TOTAL = 32
ROWS = 20480


def plant(drawn, rng, least, top_value):
    longest = drawn.shape.index(max(drawn.shape))
    spots = []
    for shift in (0, 1):
        where = [jax.random.randint(jax.random.fold_in(rng, axis), (), 0, length) for axis, length in enumerate(drawn.shape)]
        where[longest] = (where[longest] + shift) % drawn.shape[longest]
        spots.append(tuple(where))
    return drawn.at[spots[0]].set(least).at[spots[1]].set(top_value)


def levels(rng, extent, cuts, smallest, largest):
    def one(dim, blocks):
        draws = jax.random.uniform(jax.random.fold_in(jax.random.fold_in(rng, 6), dim), (blocks,), jnp.float32, smallest / len(cuts), largest / len(cuts))
        return jnp.repeat(jnp.exp(draws), extent[dim] // blocks).reshape((-1,) + (1,) * (len(extent) - dim - 1))

    factor_of = one(*cuts[0])
    for cut in cuts[1:]:
        factor_of = factor_of * one(*cut)
    return factor_of


def normal_values(rng, extent, scale, limit, cuts=(), held_as=jnp.bfloat16):
    level = levels(rng, extent, cuts, -0.22, 0.18) if cuts else 1.0
    array = jax.random.normal(rng, extent, jnp.float32) * scale * level
    return jnp.minimum(jnp.maximum(array, -limit), limit).astype(held_as)


def setup_inputs(seed: int = 0) -> dict:
    streams_of = jax.random.split(jax.random.key(seed), 18)
    layer_input_rows = normal_values(streams_of[0], (ROWS, MODEL_WIDTH), 1.0, 6.0, ((0, 32),))
    resolution = plant(jax.random.randint(streams_of[1], (SLOT_TOTAL,), 0, 2), jax.random.fold_in(streams_of[1], 1), 0, 1).astype(jnp.int32)
    attn_gain = jnp.clip(1.0 + 0.18 * jax.random.normal(streams_of[2], (MODEL_WIDTH,), jnp.float32), 0.1, 1.9)
    attn_bias = normal_values(streams_of[3], (MODEL_WIDTH,), 0.3, 3.0, (), jnp.float32)
    qkv_weight = normal_values(streams_of[4], (MODEL_WIDTH, 3 * MODEL_WIDTH), (MODEL_WIDTH // 2) ** -0.5, 0.3125)
    qv_bias = normal_values(streams_of[5], (2, MODEL_WIDTH), 0.3, 3.0, (), jnp.float32)
    out_weight = normal_values(streams_of[6], (MODEL_WIDTH, MODEL_WIDTH), (MODEL_WIDTH // 16) ** -0.5, 0.875)
    out_bias = normal_values(streams_of[7], (MODEL_WIDTH,), 0.3, 3.0, (), jnp.float32)
    attn_scale = jnp.clip(jax.random.uniform(streams_of[8], (MODEL_WIDTH,), jnp.float32, 0.5, 1.5), 0.5, 1.5)
    ffn_scale = jnp.clip(jax.random.uniform(streams_of[9], (MODEL_WIDTH,), jnp.float32, 0.5, 1.5), 0.5, 1.5)
    ffn_gain = jnp.clip(1.0 + 0.18 * jax.random.normal(streams_of[10], (2, MODEL_WIDTH), jnp.float32), 0.1, 1.9)
    ffn_bias = normal_values(streams_of[11], (2, MODEL_WIDTH), 0.3, 3.0, (), jnp.float32)
    up_weight = normal_values(streams_of[12], (2, MODEL_WIDTH, FF), MODEL_WIDTH ** -0.5, 0.21875, ((1, 16), (2, 2)))
    up_bias = normal_values(streams_of[13], (2, FF), 0.3, 3.0, ((1, 2),), jnp.float32)
    down_weight = normal_values(streams_of[14], (2, MODEL_WIDTH, FF), FF ** -0.5, 0.109375, ((1, 16), (2, 2)))
    down_bias = normal_values(streams_of[15], (2, MODEL_WIDTH), 0.3, 3.0, (), jnp.float32)
    output_gradient = normal_values(streams_of[16], (ROWS, MODEL_WIDTH), 1.0, 6.0, ((0, 32),))
    return dict(layer_input_rows=layer_input_rows, resolution=resolution, attn_gain=attn_gain, attn_bias=attn_bias, qkv_weight=qkv_weight, qv_bias=qv_bias, out_weight=out_weight, out_bias=out_bias, attn_scale=attn_scale, ffn_scale=ffn_scale, ffn_gain=ffn_gain, ffn_bias=ffn_bias, up_weight=up_weight, up_bias=up_bias, down_weight=down_weight, down_bias=down_bias, output_gradient=output_gradient)


@jax.custom_vjp
def low(v):
    return lax.optimization_barrier(v.astype(jnp.bfloat16)).astype(jnp.float32)

@jax.custom_vjp
def low_back(v):
    return v

def low_keep(v):
    return (low(v), None)

def low_pass(kept, grad):
    return (grad,)

def back_keep(v):
    return (v, None)

def back_low(kept, grad):
    return (low(grad),)
low.defvjp(low_keep, low_pass)
low_back.defvjp(back_keep, back_low)
NORM_EPS = 1e-06
HIGH = lax.Precision.HIGHEST

def layer_norm(field, gain, shift):
    center = field - lax.optimization_barrier(jnp.mean(field, axis=-1, keepdims=True))
    spread = lax.optimization_barrier(jnp.mean(center * center, axis=-1, keepdims=True))
    return center * lax.rsqrt(spread + NORM_EPS) * gain + shift

def slot_layout(res_group, row_count):
    position = jnp.arange(row_count, dtype=jnp.int32)
    small_len = PATCH_SMALL + CAPTION
    large_kind = jnp.where(position < PATCH_LARGE, 1, jnp.where(position < PATCH_LARGE + CAPTION, 0, 2))
    large_segment = jnp.where(position < PATCH_LARGE + CAPTION, 0, 2)
    within = position % small_len
    small_kind = jnp.where(position < 2 * small_len, jnp.where(within < PATCH_SMALL, 1, 0), 2)
    small_segment = jnp.where(position < 2 * small_len, position // small_len, 2)
    row_kind = jnp.where(res_group == 1, large_kind, small_kind).astype(jnp.int32)
    segment = jnp.where(res_group == 1, large_segment, small_segment).astype(jnp.int32)
    return (row_kind, segment)

def slot_forward(params, slot_rows, res_group):
    row_kind, segment = slot_layout(res_group, ROWS_PER_SLOT)
    live_rows = (row_kind != 2).astype(jnp.float32)[:, None]
    vision = (row_kind == 1)[:, None]
    normed = layer_norm(slot_rows, params['attn_gain'], params['attn_bias'])
    activ = low(normed)
    projected = jnp.dot(activ, params['qkv_weight'], precision=HIGH)
    query = low(low_back(projected[:, :MODEL_WIDTH] + params['qv_bias'][0]))
    keys = low(low_back(projected[:, MODEL_WIDTH:2 * MODEL_WIDTH]))
    values = low(low_back(projected[:, 2 * MODEL_WIDTH:] + params['qv_bias'][1]))
    query_heads = query.reshape(ROWS_PER_SLOT, HEADS, HEAD)
    key_heads = keys.reshape(ROWS_PER_SLOT, HEADS, HEAD)
    value_heads = values.reshape(ROWS_PER_SLOT, HEADS, HEAD)
    raw_scores = low_back(jnp.einsum('qhd,khd->hqk', query_heads, key_heads, precision=HIGH) * HEAD ** (-0.5))
    same_seq = (segment[:, None] == segment[None, :])[None]
    masked = jnp.where(same_seq, raw_scores, -1000000000.0)
    attn_probs = low(jax.nn.softmax(masked, axis=-1))
    attn_mixed = jnp.einsum('hqk,khd->qhd', attn_probs, value_heads, precision=HIGH).reshape(ROWS_PER_SLOT, MODEL_WIDTH)
    attn_mixed = low(low_back(attn_mixed))
    branch = low_back(jnp.dot(attn_mixed, params['out_weight'], precision=HIGH) + params['out_bias'])
    after_attn = slot_rows + live_rows * params['attn_scale'] * branch
    gain_rows = jnp.where(vision, params['ffn_gain'][1], params['ffn_gain'][0])
    shift_rows = jnp.where(vision, params['ffn_bias'][1], params['ffn_bias'][0])
    ffn_normed = low(low_back(layer_norm(after_attn, gain_rows, shift_rows)))

    def expert(index):
        preact = jnp.dot(ffn_normed, params['up_weight'][index], precision=HIGH) + params['up_bias'][index]
        hidden = low(jax.nn.gelu(low_back(preact), approximate=False))
        summed = jnp.dot(hidden, params['down_weight'][index].T, precision=HIGH) + params['down_bias'][index]
        return low(low_back(summed))
    expert_out = jnp.where(vision, expert(1), expert(0))
    return after_attn + live_rows * params['ffn_scale'] * expert_out

def reference(layer_input_rows, resolution, attn_gain, attn_bias, qkv_weight, qv_bias, out_weight, out_bias, attn_scale, ffn_scale, ffn_gain, ffn_bias, up_weight, up_bias, down_weight, down_bias, output_gradient):
    params = {'attn_gain': attn_gain.astype(jnp.float32), 'attn_bias': attn_bias.astype(jnp.float32), 'qkv_weight': qkv_weight.astype(jnp.float32), 'qv_bias': qv_bias.astype(jnp.float32), 'out_weight': out_weight.astype(jnp.float32), 'out_bias': out_bias.astype(jnp.float32), 'attn_scale': attn_scale.astype(jnp.float32), 'ffn_scale': ffn_scale.astype(jnp.float32), 'ffn_gain': ffn_gain.astype(jnp.float32), 'ffn_bias': ffn_bias.astype(jnp.float32), 'up_weight': up_weight.astype(jnp.float32), 'up_bias': up_bias.astype(jnp.float32), 'down_weight': down_weight.astype(jnp.float32), 'down_bias': down_bias.astype(jnp.float32)}
    input_rows = layer_input_rows.astype(jnp.float32).reshape(SLOT_TOTAL, ROWS_PER_SLOT, MODEL_WIDTH)
    upstream_gradient = output_gradient.astype(jnp.float32).reshape(SLOT_TOTAL, ROWS_PER_SLOT, MODEL_WIDTH)

    def forward(weights, rows):

        def one_slot(block_item):
            return jax.checkpoint(slot_forward)(weights, block_item[0], block_item[1])
        return lax.map(one_slot, (rows, resolution))
    outputs, pullback = jax.vjp(forward, params, input_rows)
    grads, input_grad = pullback(upstream_gradient)
    return (outputs.reshape(ROWS, MODEL_WIDTH).astype(jnp.bfloat16), input_grad.reshape(ROWS, MODEL_WIDTH).astype(jnp.bfloat16), grads['attn_gain'], grads['attn_bias'], grads['qkv_weight'], grads['qv_bias'], grads['out_weight'], grads['out_bias'], grads['attn_scale'], grads['ffn_scale'], grads['ffn_gain'], grads['ffn_bias'], grads['up_weight'], grads['up_bias'], grads['down_weight'], grads['down_bias'])
```

```python
import functools

import jax
import jax.numpy as jnp
from jax import lax
from jax.experimental import pallas as pl
from jax.experimental.pallas import tpu as pltpu
from jax.sharding import PartitionSpec as P

MESHID = pl.DeviceIdType.MESH
BF = jnp.bfloat16
F32 = jnp.float32

HEADS = 12
PATCH_SMALL = 197
PATCH_LARGE = 577
CAPTION = 40


NORM_EPS = 1e-06
HIGH = lax.Precision.HIGHEST


def layer_norm(field, gain, shift):
    center = field - jnp.mean(field, axis=-1, keepdims=True)
    spread = jnp.mean(center * center, axis=-1, keepdims=True)
    return center * lax.rsqrt(spread + NORM_EPS) * gain + shift


def exact_gelu(field):
    return jax.nn.gelu(field, approximate=False)


def ceil_div(numer, denom):
    return -(-numer // denom)


def slot_layout(res_group, row_count):
    position = jnp.arange(row_count, dtype=jnp.int32)
    small_len = PATCH_SMALL + CAPTION
    large_kind = jnp.where(
        position < PATCH_LARGE, 1, jnp.where(position < PATCH_LARGE + CAPTION, 0, 2)
    )
    large_segment = jnp.where(position < PATCH_LARGE + CAPTION, 0, 2)
    within = position % small_len
    small_kind = jnp.where(position < 2 * small_len, jnp.where(within < PATCH_SMALL, 1, 0), 2)
    small_segment = jnp.where(position < 2 * small_len, position // small_len, 2)
    row_kind = jnp.where(res_group == 1, large_kind, small_kind).astype(jnp.int32)
    segment = jnp.where(res_group == 1, large_segment, small_segment)
    return (row_kind, segment)


def contract_rows(left, right):
    return lax.dot_general(
        left, right, (((0,), (0,)), ((), ())), preferred_element_type=jnp.float32
    )


def contract_cols(left, right):
    return lax.dot_general(
        left, right, (((1,), (1,)), ((), ())), preferred_element_type=jnp.float32
    )


def shards(
    layer_input_rows,
    resolution,
    attn_gain,
    attn_bias,
    qkv_weight,
    qv_bias,
    out_weight,
    out_bias,
    attn_scale,
    ffn_scale,
    ffn_gain,
    ffn_bias,
    up_weight,
    up_bias,
    down_weight,
    down_bias,
    output_gradient,
):
    model_width = layer_input_rows.shape[1]
    slot_count = resolution.shape[0]
    slot_rows = layer_input_rows.shape[0] // slot_count
    head_count = HEADS
    head_width = model_width // head_count
    score_scale = head_width ** (-0.5)
    hidden_part = up_weight.shape[2]
    dp_count = lax.axis_size("dp")
    mp_count = lax.axis_size("mp")
    dp_index = lax.axis_index("dp")
    mp_index = lax.axis_index("mp")
    lang_count = dp_count // 4
    vis_count = dp_count - lang_count
    capacity = max(
        ceil_div(slot_count * PATCH_LARGE, vis_count),
        ceil_div(2 * slot_count * CAPTION, lang_count),
    )
    recv_rows = dp_count * capacity
    kinds, segments = jax.vmap(lambda res_group: slot_layout(res_group, slot_rows))(resolution)
    row_kind = kinds.reshape(-1)
    live_rows = (row_kind != 2).astype(jnp.float32)[:, None]
    vision = (row_kind == 1)[:, None]
    kind_onehot = jnp.stack([row_kind == 0, row_kind == 1], axis=1).astype(jnp.float32)
    rank_vis = jnp.cumsum((row_kind == 1).astype(jnp.int32)) - 1
    rank_txt = jnp.cumsum((row_kind == 0).astype(jnp.int32)) - 1
    target = jnp.where(
        row_kind == 1,
        (rank_vis + dp_index) % vis_count,
        vis_count + (rank_txt + dp_index) % lang_count,
    )
    position = jnp.where(row_kind == 1, rank_vis // vis_count, rank_txt // lang_count)
    slot_index = jnp.where(row_kind == 2, recv_rows, target * capacity + position)

    def to_slots(row_values):
        buffer = (
            jnp.zeros((recv_rows, model_width), row_values.dtype)
            .at[slot_index]
            .set(row_values, mode="drop")
        )
        return buffer.reshape(dp_count, capacity, model_width)

    def from_slots(buffer):
        return jnp.take(
            buffer.reshape(recv_rows, model_width), slot_index, axis=0, mode="fill", fill_value=0
        )

    my_expert = jnp.where(dp_index < vis_count, 1, 0)
    full_up, full_down = (
        lax.all_gather(up_weight, "dp", axis=1, tiled=True),
        lax.all_gather(down_weight, "dp", axis=1, tiled=True),
    )
    own_up = jnp.where(my_expert == 1, full_up[1], full_up[0])
    own_down = jnp.where(my_expert == 1, full_down[1], full_down[0])
    own_up_bias = jnp.where(my_expert == 1, up_bias[1], up_bias[0])
    own_down_bias = jnp.where(my_expert == 1, down_bias[1], down_bias[0])
    x_float = layer_input_rows.astype(jnp.float32)
    normed, norm_pull = jax.vjp(layer_norm, x_float, attn_gain, attn_bias)
    activ = normed.astype(jnp.bfloat16)
    projected = jnp.dot(activ, qkv_weight, preferred_element_type=jnp.float32)
    query = (projected[:, :model_width] + qv_bias[0]).astype(jnp.bfloat16)
    keys = projected[:, model_width : 2 * model_width].astype(jnp.bfloat16)
    values = (projected[:, 2 * model_width :] + qv_bias[1]).astype(jnp.bfloat16)
    query_slots = query.reshape(slot_count, slot_rows, head_count, head_width)
    key_slots = keys.reshape(slot_count, slot_rows, head_count, head_width)
    value_slots = values.reshape(slot_count, slot_rows, head_count, head_width)

    def slot_scores(query_heads, key_heads, segment):
        raw_scores = (
            jnp.einsum("qhd,khd->hqk", query_heads, key_heads, preferred_element_type=jnp.float32)
            * score_scale
        )
        same_seq = (segment[:, None] == segment[None, :])[None]
        return jnp.where(same_seq, raw_scores, -1000000000.0)

    def attend(block_item):
        query_heads, key_heads, value_heads, segment = block_item
        masked = slot_scores(query_heads, key_heads, segment)
        row_max = jnp.max(masked, axis=-1, keepdims=True)
        weights_exp = jnp.exp(masked - row_max)
        row_total = jnp.sum(weights_exp, axis=-1, keepdims=True)
        attn_probs = (weights_exp / row_total).astype(jnp.bfloat16)
        attn_mixed = jnp.einsum(
            "hqk,khd->qhd", attn_probs, value_heads, preferred_element_type=jnp.float32
        )
        log_total = (row_max + jnp.log(row_total))[..., 0]
        return (attn_mixed.reshape(slot_rows, model_width).astype(jnp.bfloat16), log_total)

    attn_mixed, log_totals = lax.map(attend, (query_slots, key_slots, value_slots, segments))
    attn_mixed = attn_mixed.reshape(-1, model_width)
    branch = jnp.dot(attn_mixed, out_weight, preferred_element_type=jnp.float32) + out_bias
    after_attn = x_float + live_rows * attn_scale * branch
    gain_rows = jnp.where(vision, ffn_gain[1], ffn_gain[0])
    shift_rows = jnp.where(vision, ffn_bias[1], ffn_bias[0])
    ffn_normed, norm2_pull = jax.vjp(layer_norm, after_attn, gain_rows, shift_rows)
    sent_rows = ffn_normed.astype(jnp.bfloat16)
    arrived = lax.all_to_all(
        to_slots(sent_rows), "dp", split_axis=0, concat_axis=0, tiled=True
    ).reshape(recv_rows, model_width)
    paired = lax.all_gather(arrived, "mp", axis=0, tiled=True)
    preact = jnp.dot(paired, own_up, preferred_element_type=jnp.float32) + own_up_bias
    hidden, gelu_pull = jax.vjp(exact_gelu, preact)
    hidden_low = hidden.astype(jnp.bfloat16)
    partial_out = contract_cols(hidden_low, own_down)
    expert_sum = (
        lax.psum_scatter(
            partial_out.astype(jnp.bfloat16), "mp", scatter_dimension=0, tiled=True
        ).astype(jnp.float32)
        + own_down_bias
    )
    returned = lax.all_to_all(
        expert_sum.astype(jnp.bfloat16).reshape(dp_count, capacity, model_width),
        "dp",
        split_axis=0,
        concat_axis=0,
        tiled=True,
    )
    expert_rows = from_slots(returned).astype(jnp.float32)
    block_output = (after_attn + live_rows * ffn_scale * expert_rows).astype(jnp.bfloat16)
    grad_float = output_gradient.astype(jnp.float32)
    d_expert = (live_rows * ffn_scale * grad_float).astype(jnp.bfloat16)
    ffn_scale_grad = jnp.sum(live_rows * expert_rows * grad_float, axis=0)
    down_bias_grad = jnp.dot(kind_onehot.T, d_expert.astype(jnp.float32), precision=HIGH)
    arrived_grad = lax.all_to_all(
        to_slots(d_expert), "dp", split_axis=0, concat_axis=0, tiled=True
    ).reshape(recv_rows, model_width)
    paired_grad = lax.all_gather(arrived_grad, "mp", axis=0, tiled=True)
    d_hidden = jnp.dot(paired_grad, own_down, preferred_element_type=jnp.float32)
    d_preact = gelu_pull(d_hidden)[0].astype(jnp.bfloat16)
    own_down_grad = contract_rows(paired_grad, hidden_low)
    own_up_grad = contract_rows(paired, d_preact)
    own_bias_grad = jnp.sum(d_preact.astype(jnp.float32), axis=0)
    d_normed_part = contract_cols(d_preact, own_up)
    d_normed = lax.psum_scatter(
        d_normed_part.astype(jnp.bfloat16), "mp", scatter_dimension=0, tiled=True
    )
    back_grad = lax.all_to_all(
        d_normed.reshape(dp_count, capacity, model_width),
        "dp",
        split_axis=0,
        concat_axis=0,
        tiled=True,
    )
    d_ffn_normed = from_slots(back_grad).astype(jnp.float32)
    d_after_part, gain_grad_rows, shift_grad_rows = norm2_pull(d_ffn_normed)
    ffn_gain_grad = jnp.dot(kind_onehot.T, gain_grad_rows, precision=HIGH)
    ffn_bias_grad = jnp.dot(kind_onehot.T, shift_grad_rows, precision=HIGH)
    d_after = grad_float + d_after_part
    d_branch = (live_rows * attn_scale * d_after).astype(jnp.bfloat16)
    attn_scale_grad = jnp.sum(live_rows * branch * d_after, axis=0)
    out_bias_grad = jnp.sum(d_branch.astype(jnp.float32), axis=0)
    out_weight_grad = contract_rows(attn_mixed, d_branch)
    d_mixed = contract_cols(d_branch, out_weight).astype(jnp.bfloat16)
    d_mixed_slots = d_mixed.reshape(slot_count, slot_rows, head_count, head_width)

    def attend_back(block_item):
        query_heads, key_heads, value_heads, segment, log_total, d_heads = block_item
        masked = slot_scores(query_heads, key_heads, segment)
        probs_full = jnp.exp(masked - log_total[..., None])
        d_probs = jnp.einsum(
            "qhd,khd->hqk", d_heads, value_heads, preferred_element_type=jnp.float32
        )
        row_delta = jnp.sum(probs_full * d_probs, axis=-1, keepdims=True)
        d_scores = (probs_full * (d_probs - row_delta)).astype(jnp.bfloat16)
        probs_low = probs_full.astype(jnp.bfloat16)
        grad_value = jnp.einsum(
            "hqk,qhd->khd", probs_low, d_heads, preferred_element_type=jnp.float32
        )
        grad_query = (
            jnp.einsum("hqk,khd->qhd", d_scores, key_heads, preferred_element_type=jnp.float32)
            * score_scale
        )
        grad_key = (
            jnp.einsum("hqk,qhd->khd", d_scores, query_heads, preferred_element_type=jnp.float32)
            * score_scale
        )
        joined = jnp.concatenate(
            [
                grad_query.reshape(slot_rows, model_width),
                grad_key.reshape(slot_rows, model_width),
                grad_value.reshape(slot_rows, model_width),
            ],
            axis=1,
        )
        return joined.astype(jnp.bfloat16)

    d_projected = lax.map(
        attend_back, (query_slots, key_slots, value_slots, segments, log_totals, d_mixed_slots)
    ).reshape(-1, 3 * model_width)
    qkv_weight_grad = contract_rows(activ, d_projected)
    d_proj_float = d_projected.astype(jnp.float32)
    qv_bias_grad = jnp.stack(
        [
            jnp.sum(d_proj_float[:, :model_width], axis=0),
            jnp.sum(d_proj_float[:, 2 * model_width :], axis=0),
        ]
    )
    d_attn_normed = contract_cols(d_projected, qkv_weight)
    d_input_part, attn_gain_grad, attn_bias_grad = norm_pull(d_attn_normed)
    input_grad = (d_after + d_input_part).astype(jnp.bfloat16)
    expert_pick = (jnp.arange(2) == my_expert).astype(jnp.float32)[:, None, None]
    up_weight_grad, down_weight_grad = (
        lax.psum_scatter(expert_pick * own_up_grad[None], "dp", scatter_dimension=1, tiled=True),
        lax.psum_scatter(expert_pick * own_down_grad[None], "dp", scatter_dimension=1, tiled=True),
    )
    up_bias_full = (
        jnp.zeros((2, mp_count, hidden_part), jnp.float32)
        .at[my_expert, mp_index]
        .set(own_bias_grad)
        .reshape(2, mp_count * hidden_part)
    )
    vector_sums = lax.psum(
        (
            attn_gain_grad,
            attn_bias_grad,
            qv_bias_grad,
            out_bias_grad,
            attn_scale_grad,
            ffn_scale_grad,
            ffn_gain_grad,
            ffn_bias_grad,
            up_bias_full,
            down_bias_grad,
        ),
        ("dp", "mp"),
    )
    matrix_sums = (
        lax.psum_scatter(qkv_weight_grad, ("dp", "mp"), scatter_dimension=0, tiled=True),
        lax.psum_scatter(out_weight_grad, ("dp", "mp"), scatter_dimension=0, tiled=True),
    )
    return (
        block_output,
        input_grad,
        vector_sums[0],
        vector_sums[1],
        matrix_sums[0],
        vector_sums[2],
        matrix_sums[1],
        vector_sums[3],
        vector_sums[4],
        vector_sums[5],
        vector_sums[6],
        vector_sums[7],
        up_weight_grad,
        vector_sums[8],
        down_weight_grad,
        vector_sums[9],
    )


NT = (((1,), (1,)), ((), ()))
TN = (((0,), (0,)), ((), ()))
SMALL = PATCH_SMALL + CAPTION
CAPS = 2 * CAPTION
ANY = pl.BlockSpec(memory_space=pl.ANY)
VM = pl.BlockSpec(memory_space=pltpu.VMEM)
SM = pl.BlockSpec(memory_space=pltpu.SMEM)
DMA = pltpu.SemaphoreType.DMA
CHUNK = 128
V_AG, V_AB, V_QB, V_VB, V_OB, V_AS, V_FS, V_FG, V_FB, V_DB = 0, 1, 2, 3, 4, 5, 6, 7, 9, 11
G_AG, G_AB, G_QB, G_VB, G_OB, G_AS, G_FS, G_FG, G_FB, G_DB, G_UB = 0, 1, 2, 3, 4, 5, 6, 7, 9, 11, 16


def kind_of(res, pos):
    one = lambda c: c.astype(jnp.int32)
    big_seg = 2 * one(pos >= PATCH_LARGE + CAPTION)
    big_kind = 1 - one(pos >= PATCH_LARGE) + big_seg
    small_seg = one(pos >= SMALL) + one(pos >= 2 * SMALL)
    small_pad = one(pos >= 2 * SMALL)
    within = pos - SMALL * small_seg
    small_kind = (1 - small_pad) * one(within < PATCH_SMALL) + 2 * small_pad
    return (
        res * big_kind + (1 - res) * small_kind,
        res * big_seg + (1 - res) * small_seg,
    )


def caption_place(res, slot):
    late = (slot >= CAPTION).astype(jnp.int32)
    big = (1 - late) * (PATCH_LARGE + slot) - late
    small = PATCH_SMALL + slot + late * (SMALL - CAPTION)
    none = (slot >= CAPS).astype(jnp.int32)
    place = res * big + (1 - res) * small
    return (1 - none) * place - none


def iota(shape, dim):
    return lax.broadcasted_iota(jnp.int32, shape, dim)


def fill_bias(res, bias):
    n = bias.shape[0]
    across = kind_of(res, iota((1, n), 1))[1]

    @pl.loop(0, n // CHUNK)
    def _(r):
        base = pl.multiple_of(r * CHUNK, CHUNK)
        down = kind_of(res, iota((CHUNK, 1), 0) + base)[1]
        bias[pl.ds(base, CHUNK), :] = jnp.where(down == across, 0.0, -1000000000.0)


def norm_parts(v):
    center = v - jnp.mean(v, axis=-1, keepdims=True)
    inv = lax.rsqrt(jnp.mean(center * center, axis=-1, keepdims=True) + NORM_EPS)
    return center * inv, inv


def norm_back(xhat, inv, d_hat):
    mean_d = jnp.mean(d_hat, axis=-1, keepdims=True)
    mean_dx = jnp.mean(d_hat * xhat, axis=-1, keepdims=True)
    return inv * (d_hat - mean_d - xhat * mean_dx)


def half_mask(hh, scale):
    lane = iota((1, 128), 1)
    inside = (lane < 64) if hh == 0 else (lane >= 64)
    return jnp.where(inside, scale, 0.0).astype(BF)


def colsum(v):
    return jnp.sum(v, axis=0, keepdims=True)


def dyn_unit(z, k):
    m = k // 2
    zz = z + (z // 2) * (3 - 2 * z)
    u = (1 - m) * (zz + k - 2 * k * zz) + m * k
    w = z // 2
    return u + w * (3 - 2 * u)


class Place:
    def __init__(s):
        s.dp, s.mp = lax.axis_index("dp"), lax.axis_index("mp")
        s.z = s.dp // 4
        s.y = (s.dp // 2) % 2
        s.x = s.dp % 2
        s.xn = s.dp + 1 - 2 * s.x
        s.yn = s.dp + 2 - 4 * s.y
        s.z1 = s.dp + 4 - 8 * (s.z % 2)
        s.z2 = s.dp + 8 - 16 * (s.z // 2)
        s.other = 1 - s.mp

    def barrier(s, far=False):
        bar = pltpu.get_barrier_semaphore()
        dp, z = s.dp, s.z

        def sig(d, m):
            pl.semaphore_signal(bar, inc=1, device_id=(d, m), device_id_type=MESHID)

        sig(s.xn, s.mp)
        sig(s.yn, s.mp)
        sig(dp, s.other)
        if far:
            sig(s.z2, s.mp)

        @pl.when(z > 0)
        def _():
            sig(dp - 4, s.mp)

        @pl.when(z < 3)
        def _():
            sig(dp + 4, s.mp)

        pl.semaphore_wait(bar, 4 + int(far) + ((z + 1) // 2) % 2)


def remote(src, dst, ss, sr, dev, core):
    return pltpu.make_async_remote_copy(
        src_ref=src, dst_ref=dst, send_sem=ss, recv_sem=sr,
        device_id=(dev, core), device_id_type=MESHID,
    )


class AG:
    def __init__(s, place, g, ss, sr, C):
        s.p, s.g, s.ss, s.sr, s.C = place, g, ss, sr, C
        s.rows, s.hid = g.shape[1] // 16, g.shape[2]
        s.ck = s.hid // C
        s.col = place.y * 2 + place.x

    def cp(s, kind, c, u, owner, dev, half=None):
        h = slice(0, 4) if half is None else slice(2 * half, 2 * half + 2)
        at = pl.ds(pl.multiple_of(owner * s.rows, 16), s.rows)
        w = s.g.at[h, at, pl.ds(pl.multiple_of(c * s.ck, 128), s.ck)]
        rk = 0 if kind == 1 else kind
        return remote(w, w, s.ss.at[kind, c, u], s.sr.at[rk, c, u], dev, s.p.mp)

    def send(s, k, c, local):
        p = s.p
        z, dp = p.z, p.dp
        u = dyn_unit(z, k)
        owner = u * 4 + s.col
        if not local:
            s.cp(0, c, u, owner, dp).wait_recv()

        @pl.when((u <= z) & (z < 3))
        def _():
            s.cp(0, c, u, owner, dp + 4).start()

        @pl.when((u >= z) & (z > 0))
        def _():
            s.cp(1, c, u, owner, dp - 4).start()

        s.cp(2, c, u, owner, p.xn).start()
        s.cp(3, c, u, owner, p.yn).start()

    def forward(s, k, c):
        p = s.p
        u = dyn_unit(p.z, k)
        xo = u * 4 + p.y * 2 + 1 - p.x
        yo = u * 4 + 2 - 2 * p.y + p.x
        s.cp(2, c, u, xo, p.dp).wait_recv()
        s.cp(5, c, u, xo, p.yn, half=0).start()
        s.cp(3, c, u, yo, p.dp).wait_recv()
        s.cp(4, c, u, yo, p.xn, half=1).start()

    def tick(s, t):
        c, m = t // 3, t % 3
        s.send(1 + m, c, False)
        s.forward(m, c)
        if isinstance(t, int):
            if m == 0 and c > 0:
                s.forward(3, c - 1)
        else:
            @pl.when((m == 0) & (c > 0))
            def _():
                s.forward(3, c - 1)

    def arrived(s, c):
        for k in range(4):
            u = dyn_unit(s.p.z, k)
            own = u * 4 + s.col
            s.cp(4, c, u, own, s.p.dp, half=1).wait_recv()
            s.cp(5, c, u, own, s.p.dp, half=0).wait_recv()

    def finish(s, k, c):
        p = s.p
        z, dp = p.z, p.dp
        u = dyn_unit(z, k)
        own = u * 4 + s.col
        s.cp(2, c, u, own, dp).wait_send()
        s.cp(3, c, u, own, dp).wait_send()
        s.cp(4, c, u, own, dp, half=1).wait_send()
        s.cp(5, c, u, own, dp, half=0).wait_send()

        @pl.when((u <= z) & (z < 3))
        def _():
            s.cp(0, c, u, own, dp).wait_send()

        @pl.when((u >= z) & (z > 0))
        def _():
            s.cp(1, c, u, own, dp).wait_send()


class RS:
    def __init__(s, place, g, bufs, ss, sr, C, write):
        s.p, s.g, s.write = place, g, write
        s.bx, s.by, s.bdx, s.bdy, s.bzu, s.bzd = bufs
        s.ss, s.sr, s.C = ss, sr, C
        s.M = g.shape[0]
        s.flat = len(g.shape) == 3
        s.rows = g.shape[1] // 16 if s.flat else g.shape[2]
        s.ck = g.shape[-1] // C
        s.h0 = s.M // 2
        x, y = place.x, place.y
        s.oo = y * 2 + x
        s.ox = y * 2 + 1 - x
        s.oy = 2 - 2 * y + x
        s.od = 3 - 2 * y - x

    def cols(s, c):
        return pl.ds(pl.multiple_of(c * s.ck, 128), s.ck)

    def win(s, u, col, c, lo=0, hi=None):
        hi = s.M if hi is None else hi
        if s.flat:
            at = pl.multiple_of((u * 4 + col) * s.rows, 16)
            return s.g.at[lo:hi, pl.ds(at, s.rows), s.cols(c)]
        return s.g.at[lo:hi, u * 4 + col, :, s.cols(c)]

    def cp(s, kind, u, c, src, dst, dev):
        return remote(src, dst, s.ss.at[kind, c, u], s.sr.at[kind, c, u], dev, s.p.mp)

    def bw(s, b, u, c):
        return b.at[u, :, :, s.cols(c)]

    def c_dy(s, u, c):
        return s.cp(0, u, c, s.win(u, s.od, c, 0, s.h0), s.bw(s.bdy, u, c), s.p.yn)

    def c_dx(s, u, c):
        return s.cp(1, u, c, s.win(u, s.od, c, s.h0), s.bw(s.bdx, u, c), s.p.xn)

    def c_x(s, u, c):
        return s.cp(2, u, c, s.win(u, s.ox, c), s.bw(s.bx, u, c), s.p.xn)

    def c_y(s, u, c):
        return s.cp(3, u, c, s.win(u, s.oy, c), s.bw(s.by, u, c), s.p.yn)

    def c_zu(s, u, c):
        return s.cp(4, u, c, s.win(u, s.oo, c), s.bw(s.bzu, u, c), s.p.dp + 4)

    def c_zd(s, u, c):
        return s.cp(5, u, c, s.win(u, s.oo, c), s.bw(s.bzd, u, c), s.p.dp - 4)

    def item(s, t):
        return dyn_unit(s.p.z, 3 - t // s.C), t % s.C

    def s1(s, t):
        u, c = s.item(t)
        s.c_dy(u, c).start()
        s.c_dx(u, c).start()

    def add(s, dst, src):
        dst[...] = (dst[...].astype(F32) + src[...].astype(F32)).astype(BF)

    def s2(s, t):
        u, c = s.item(t)
        s.c_dy(u, c).wait_recv()
        s.add(s.win(u, s.ox, c, 0, s.h0), s.bw(s.bdy, u, c))
        s.c_x(u, c).start()
        s.c_dx(u, c).wait_recv()
        s.add(s.win(u, s.oy, c, s.h0), s.bw(s.bdx, u, c))
        s.c_y(u, c).start()

    def s3(s, t):
        u, c = s.item(t)
        z = s.p.z
        s.c_x(u, c).wait_recv()
        s.c_y(u, c).wait_recv()
        o = s.win(u, s.oo, c)

        def total(*bufs):
            v = o[...].astype(F32)
            for b in (s.bx, s.by) + bufs:
                v = v + s.bw(b, u, c)[...].astype(F32)
            return v

        def go(pred, wu, wd, send):
            @pl.when(pred)
            def _():
                more = ()
                if wu:
                    s.c_zu(u, c).wait_recv()
                    more += (s.bzu,)
                if wd:
                    s.c_zd(u, c).wait_recv()
                    more += (s.bzd,)
                v = total(*more)
                if send is None:
                    s.write(c, v)
                else:
                    o[...] = v.astype(BF)
                    send(u, c).start()

        up, dn, own = u > z, u < z, u == z
        go(up & (z > 0), True, False, s.c_zu)
        go(up & (z == 0), False, False, s.c_zu)
        go(dn & (z < 3), False, True, s.c_zd)
        go(dn & (z == 3), False, False, s.c_zd)
        go(own & (z == 0), False, True, None)
        go(own & (z == 3), True, False, None)
        go(own & (z > 0) & (z < 3), True, True, None)

    def tick(s, t):
        n = 4 * s.C
        if t < n:
            s.s1(t)
        if 0 <= t - 1 < n:
            s.s2(t - 1)
        if 0 <= t - 2 < n:
            s.s3(t - 2)

    def finish(s, t):
        u, c = s.item(t)
        for f in (s.c_dy, s.c_dx, s.c_x, s.c_y):
            f(u, c).wait_send()

        @pl.when(u > s.p.z)
        def _():
            s.c_zu(u, c).wait_send()

        @pl.when(u < s.p.z)
        def _():
            s.c_zd(u, c).wait_send()


def load_all(pairs, sem):
    copies = [pltpu.make_async_copy(a, b, sem.at[i]) for i, (a, b) in enumerate(pairs)]
    for c in copies:
        c.start()
    return copies


def front_kernel(
    C, res_ref, a_gain, a_bias, qv_bias, o_bias, a_scale, f_scale, f_gain, f_bias, dn_bias, up_bias,
    x, og, wqkv, wout, up_ref, down_ref,
    proj, activ, mixed, vec, ub, fsum, bsum, grads,
    g, bias, qkvb, xall, gall, xt, gt, xct, gct, accf, accb, rcv, stage, hid, dpre, ubg,
    lsem, ss, sr, ps, pr,
):
    p = Place()
    n, width = x.shape
    res = res_ref[0]
    ag = AG(p, g, ss, sr, C)
    mine = pl.ds(pl.multiple_of(p.dp * ag.rows, 16), ag.rows)
    loads = load_all([(up_ref, g.at[0:2, mine, :]), (down_ref, g.at[2:4, mine, :])], lsem)
    p.barrier()
    for c in loads:
        c.wait()
    for c in range(C):
        ag.send(0, c, True)

    for row, ref in (
        (V_AG, a_gain), (V_AB, a_bias), (V_OB, o_bias), (V_AS, a_scale), (V_FS, f_scale),
    ):
        vec[row:row + 1, :] = ref[...].reshape(1, width)
    for row, ref in ((V_QB, qv_bias), (V_FG, f_gain), (V_FB, f_bias), (V_DB, dn_bias)):
        vec[row:row + 2, :] = ref[...]
    vec[13:16, :] = jnp.zeros((3, width), F32)

    @pl.loop(0, n // CHUNK)
    def _(r):
        at = pl.ds(pl.multiple_of(r * CHUNK, CHUNK), CHUNK)
        hat, _ = norm_parts(x[at, :].astype(F32))
        activ[at, :] = (hat * vec[V_AG:V_AG + 1, :] + vec[V_AB:V_AB + 1, :]).astype(BF)

    qkvb[:, :width] = vec[V_QB:V_QB + 1, :]
    qkvb[:, width:2 * width] = jnp.zeros((1, width), F32)
    qkvb[:, 2 * width:] = vec[V_VB:V_VB + 1, :]
    part = 384

    @pl.loop(0, 3 * width // part)
    def _(j):
        at = pl.ds(pl.multiple_of(j * part, 128), part)
        v = jnp.dot(activ[...], wqkv[:, at], preferred_element_type=F32)
        proj[:, at] = (v + qkvb[:, at]).astype(BF)

    fill_bias(res, bias)
    masks = [half_mask(0, 0.125), half_mask(1, 0.125)]
    first = iota((1, 128), 1) < 64

    @pl.loop(0, width // 128)
    def _(h):
        def cols(base):
            return pl.ds(pl.multiple_of(base + h * 128, 128), 128)

        @pl.when(h > 0)
        def _():
            ag.tick(h - 1)

        q, k, v = proj[:, cols(0)], proj[:, cols(width)], proj[:, cols(2 * width)]
        outs = []
        for hh in range(2):
            s = lax.dot_general(q * masks[hh], k, NT, preferred_element_type=F32) + bias[...]
            e = jnp.exp(s - jnp.max(s, axis=-1, keepdims=True))
            pr_low = (e * (1.0 / jnp.sum(e, axis=-1, keepdims=True))).astype(BF)
            outs.append(jnp.dot(pr_low, v, preferred_element_type=F32))
        mixed[:, cols(0)] = jnp.where(first, outs[0], outs[1]).astype(BF)

    ag.tick(5)
    half = 256

    @pl.loop(0, width // half)
    def _(j):
        at = pl.ds(pl.multiple_of(j * half, 128), half)
        accf[:n, at] = jnp.dot(mixed[...], wout[:, at], preferred_element_type=F32)

    img = p.mp * n
    caps = 2 * n + p.mp * CAPS

    @pl.loop(0, n // CHUNK)
    def _(r):
        base = pl.multiple_of(r * CHUNK, CHUNK)
        at = pl.ds(base, CHUNK)
        to = pl.ds(pl.multiple_of(img + base, 128), CHUNK)
        kind = kind_of(res, iota((CHUNK, 1), 0) + base)[0]
        live = (kind < 2).astype(F32)
        row = x[at, :].astype(F32)
        row = row + live * vec[V_AS:V_AS + 1, :] * (accf[at, :] + vec[V_OB:V_OB + 1, :])
        hat, _ = norm_parts(row)
        gain = jnp.where(kind == 1, vec[V_FG + 1:V_FG + 2, :], vec[V_FG:V_FG + 1, :])
        shift = jnp.where(kind == 1, vec[V_FB + 1:V_FB + 2, :], vec[V_FB:V_FB + 1, :])
        xall[to, :] = (hat * gain + shift).astype(BF)
        gall[to, :] = (live * vec[V_FS:V_FS + 1, :] * og[at, :].astype(F32)).astype(BF)

    pick = (iota((CAPS, n), 1) == caption_place(res, iota((CAPS, 1), 0))).astype(F32).astype(BF)
    at_img = pl.ds(pl.multiple_of(img, 128), n)
    at_cap = pl.ds(pl.multiple_of(caps, 16), CAPS)
    for ref in (xall, gall):
        ref[at_cap, :] = jnp.dot(pick, ref[at_img, :], preferred_element_type=F32).astype(BF)

    @pl.loop(0, n // CHUNK)
    def _(r):
        base = pl.multiple_of(r * CHUNK, CHUNK)
        to = pl.ds(pl.multiple_of(img + base, 128), CHUNK)
        vis = (kind_of(res, iota((CHUNK, 1), 0) + base)[0] == 1).astype(F32)
        gall[to, :] = (gall[to, :].astype(F32) * vis).astype(BF)

    pairs = []
    for i, (ref, at) in enumerate(((xall, at_img), (xall, at_cap), (gall, at_img), (gall, at_cap))):
        w = ref.at[at, :]
        pairs.append(remote(w, w, ps.at[i], pr.at[i], p.dp, p.other))
        pairs[-1].start()
    ag.tick(6)
    accf[...] = jnp.zeros(accf.shape, F32)
    accb[...] = jnp.zeros(accb.shape, F32)
    ubg[...] = jnp.zeros(ubg.shape, F32)
    for c in pairs:
        c.wait()
    for src, dst in ((xall, xt), (gall, gt)):
        @pl.loop(0, 2 * n // CHUNK)
        def _(r):
            at = pl.ds(pl.multiple_of(r * CHUNK, CHUNK), CHUNK)
            dst[:, at] = src[at, :].T

    xct[...] = xall[2 * n:, :].T
    gct[...] = gall[2 * n:, :].T
    ag.tick(7)
    ck = ag.ck

    def saved(c):
        return pltpu.make_async_copy(stage, grads.at[:, :, c * ck:(c + 1) * ck], lsem.at[2])

    def rows_step(c, expert, at):
        here = slice(c * ck, (c + 1) * ck)
        up, down = g[expert, :, here], g[2 + expert, :, here]
        v = jnp.dot(xall[at, :], up, preferred_element_type=F32) + up_bias[expert:expert + 1, here]
        dh = jnp.dot(gall[at, :], down, preferred_element_type=F32)
        cdf = 0.5 * (1.0 + lax.erf(v * (0.5 ** 0.5)))
        slope = cdf + v * (jnp.exp(v * v * -0.5) * 0.3989422804014327)
        h_low = (v * cdf).astype(BF)
        d_low = (dh * slope).astype(BF)
        hid[at, :] = h_low
        dpre[at, :] = d_low
        accf[at, :] += lax.dot_general(h_low, down, NT, preferred_element_type=F32)
        accb[at, :] += lax.dot_general(d_low, up, NT, preferred_element_type=F32)
        ubg[expert:expert + 1, here] += colsum(d_low.astype(F32))

    back_pairs = []
    for c in range(C):
        ag.arrived(c)

        @pl.loop(0, 2 * n // 256)
        def _(r):
            rows_step(c, 1, pl.ds(pl.multiple_of(r * 256, 256), 256))

        rows_step(c, 0, slice(2 * n, 2 * n + 2 * CAPS))
        if c == 0:
            ag.tick(8)
        if c == C - 1:
            theirs_img = pl.ds(pl.multiple_of(p.other * n, 128), n)
            theirs_cap = pl.ds(pl.multiple_of(2 * n + p.other * CAPS, 16), CAPS)
            for i, (acc, low) in enumerate(((accf, xall), (accb, gall))):
                @pl.loop(0, 9)
                def _(r):
                    at = pl.ds(pl.multiple_of(r * 160, 16), 160)
                    low[at, :] = acc[at, :].astype(BF)

                for j, (at, lo, size) in enumerate(((theirs_img, 0, n), (theirs_cap, n, CAPS))):
                    k = 2 * i + j
                    to = rcv.at[pl.ds(i * (n + CAPS) + lo, size), :]
                    back_pairs.append(
                        remote(low.at[at, :], to, ps.at[4 + k], pr.at[4 + k], p.dp, p.other)
                    )
                    back_pairs[-1].start()
        if c > 0:
            saved(c - 1).wait()

        @pl.loop(0, width // 256)
        def _(r):
            at = pl.ds(pl.multiple_of(r * 256, 256), 256)
            im = slice(0, 2 * n)
            cp = slice(2 * n, 2 * n + 2 * CAPS)
            for i, (l, rr, rows) in enumerate(
                ((xct, dpre, cp), (xt, dpre, im), (gct, hid, cp), (gt, hid, im))
            ):
                stage[i, at, :] = jnp.dot(
                    l[at, :], rr[rows, :], preferred_element_type=F32
                ).astype(BF)

        saved(c).start()
        if c == 0:
            ag.forward(3, C - 1)
    ub[...] = jnp.zeros(ub.shape, F32)
    for e in range(2):
        for j in range(2):
            ub[pl.ds(e * 4 + p.mp * 2 + j, 1), :] = ubg[e:e + 1, j * width:(j + 1) * width]
    for c in back_pairs:
        c.wait()
    for i, (low, out) in enumerate(((xall, fsum), (gall, bsum))):
        off = i * (n + CAPS)

        @pl.loop(0, n // CHUNK)
        def _(r):
            base = r * CHUNK
            at = pl.ds(pl.multiple_of(base, CHUNK), CHUNK)
            own = low[pl.ds(pl.multiple_of(img + base, CHUNK), CHUNK), :].astype(F32)
            got = rcv[pl.ds(pl.multiple_of(off + base, 16), CHUNK), :].astype(F32)
            out[at, :] = (own + got).astype(BF)

        own = low[at_cap, :].astype(F32)
        out[n:, :] = (own + rcv[off + n:off + n + CAPS, :].astype(F32)).astype(BF)
    saved(C - 1).wait()
    for k in range(4):
        for c in range(C):
            ag.finish(k, c)


def front(res, small, up_bias, x, og, wqkv, wout, up, down, C=3):
    n, width = x.shape
    _, rows, hid = up.shape
    ck = hid // C
    sds = jax.ShapeDtypeStruct
    wide = 2 * (n + CAPS)
    return pl.pallas_call(
        functools.partial(front_kernel, C),
        out_shape=(
            sds((n, 3 * width), BF),
            sds((n, width), BF),
            sds((n, width), BF),
            sds((16, width), F32),
            sds((8, width), F32),
            sds((n + CAPS, width), BF),
            sds((n + CAPS, width), BF),
            sds((4, rows * 16, hid), BF),
        ),
        in_specs=[SM] + [VM] * 14 + [ANY, ANY],
        out_specs=(VM,) * 7 + (ANY,),
        scratch_shapes=[
            pltpu.VMEM((4, rows * 16, hid), BF),
            pltpu.VMEM((n, n), F32),
            pltpu.VMEM((1, 3 * width), F32),
            pltpu.VMEM((wide, width), BF),
            pltpu.VMEM((wide, width), BF),
            pltpu.VMEM((width, 2 * n), BF),
            pltpu.VMEM((width, 2 * n), BF),
            pltpu.VMEM((width, 2 * CAPS), BF),
            pltpu.VMEM((width, 2 * CAPS), BF),
            pltpu.VMEM((wide, width), F32),
            pltpu.VMEM((wide, width), F32),
            pltpu.VMEM((wide, width), BF),
            pltpu.VMEM((4, rows * 16, ck), BF),
            pltpu.VMEM((wide, ck), BF),
            pltpu.VMEM((wide, ck), BF),
            pltpu.VMEM((2, hid), F32),
            DMA((3,)), DMA((6, C, 4)), DMA((6, C, 4)), DMA((8,)), DMA((8,)),
        ],
        compiler_params=pltpu.CompilerParams(
            collective_id=0, has_side_effects=True, vmem_limit_bytes=67043328
        ),
        name="front",
    )(res, *small, up_bias, x, og, wqkv, wout, up, down)


def back_kernel(
    C, res_ref, vec, ub, x, og, fsum, bsum, proj_h, mixed_h, wout, grads_h,
    out_up, out_down, block, d_proj, d_branch, d_after, vsum,
    g, bx, by, bdx, bdy, bzu, bzd, proj, mixed, capf, branch, d_mixed, bias,
    lsem, ss, sr,
):
    p = Place()
    n, width = x.shape
    res = res_ref[0]
    loads = load_all([(grads_h, g), (proj_h, proj), (mixed_h, mixed)], lsem)
    p.barrier()

    def write(c, v):
        at = pl.ds(pl.multiple_of(c * (g.shape[2] // C), 128), g.shape[2] // C)
        out_up[:, :, at] = v[:2]
        out_down[:, :, at] = v[2:]

    rs = RS(p, g, (bx, by, bdx, bdy, bzu, bzd), ss, sr, C, write)
    loads[0].wait()
    rs.tick(0)
    loads[1].wait()
    loads[2].wait()
    fill_bias(res, bias)
    half = 256

    @pl.loop(0, width // half)
    def _(j):
        at = pl.ds(pl.multiple_of(j * half, 128), half)
        branch[:, at] = jnp.dot(mixed[...], wout[:, at], preferred_element_type=F32)

    vsum[...] = jnp.zeros(vsum.shape, F32)
    vsum[G_UB:G_UB + 8, :] = ub[...]
    pad = jnp.zeros((128 - CAPS, width), BF)
    for i, ref in enumerate((fsum, bsum)):
        capf[i] = jnp.concatenate([ref[n:, :], pad], axis=0)

    def add(row, v):
        vsum[row:row + 1, :] += colsum(v)

    @pl.loop(0, n // CHUNK)
    def _(r):
        base = pl.multiple_of(r * CHUNK, CHUNK)
        at = pl.ds(base, CHUNK)
        pos = iota((CHUNK, 1), 0) + base
        kind = kind_of(res, pos)[0]
        live = (kind < 2).astype(F32)
        vis = kind == 1
        cap = kind == 0
        pick = (pos == caption_place(res, iota((1, 128), 1))).astype(F32).astype(BF)
        from_cap = jnp.dot(pick, capf[0], preferred_element_type=F32)
        d_cap = jnp.dot(pick, capf[1], preferred_element_type=F32)
        from_img = fsum[at, :].astype(F32)
        d_img = bsum[at, :].astype(F32)
        grad = og[at, :].astype(F32)
        row_branch = branch[at, :] + vec[V_OB:V_OB + 1, :]
        scale = live * vec[V_AS:V_AS + 1, :]
        after = x[at, :].astype(F32) + scale * row_branch
        expert = jnp.where(
            cap, from_cap + vec[V_DB:V_DB + 1, :], from_img + vec[V_DB + 1:V_DB + 2, :]
        ).astype(BF).astype(F32)
        ffn_scale = live * vec[V_FS:V_FS + 1, :]
        block[at, :] = (after + ffn_scale * expert).astype(BF)
        add(G_FS, live * expert * grad)
        d_expert = (ffn_scale * grad).astype(BF).astype(F32)
        add(G_DB, jnp.where(cap, d_expert, 0.0))
        add(G_DB + 1, jnp.where(vis, d_expert, 0.0))
        d_ffn = jnp.where(cap, d_cap, d_img)
        hat, inv = norm_parts(after)
        d_gain = d_ffn * hat
        add(G_FG, jnp.where(cap, d_gain, 0.0))
        add(G_FG + 1, jnp.where(vis, d_gain, 0.0))
        add(G_FB, jnp.where(cap, d_ffn, 0.0))
        add(G_FB + 1, jnp.where(vis, d_ffn, 0.0))
        gain = jnp.where(vis, vec[V_FG + 1:V_FG + 2, :], vec[V_FG:V_FG + 1, :])
        da = grad + norm_back(hat, inv, d_ffn * gain)
        d_after[at, :] = da
        add(G_AS, live * row_branch * da)
        db = (scale * da).astype(BF)
        d_branch[at, :] = db
        add(G_OB, db.astype(F32))

    rs.tick(1)

    @pl.loop(0, width // half)
    def _(j):
        at = pl.ds(pl.multiple_of(j * half, 128), half)
        v = lax.dot_general(d_branch[...], wout[at, :], NT, preferred_element_type=F32)
        d_mixed[:, at] = v.astype(BF)

    ones = [half_mask(0, 1.0), half_mask(1, 1.0)]
    scaled = [half_mask(0, 0.125), half_mask(1, 0.125)]
    first = iota((1, 128), 1) < 64

    @pl.loop(0, width // 128)
    def _(h):
        t = h + 2
        rs.s1(t)
        rs.s2(t - 1)
        rs.s3(t - 2)

        def cols(base):
            return pl.ds(pl.multiple_of(base + h * 128, 128), 128)

        q, k, v = proj[:, cols(0)], proj[:, cols(width)], proj[:, cols(2 * width)]
        do = d_mixed[:, cols(0)]
        q_scaled = q * jnp.full((1, 128), 0.125, BF)
        k_turned = (k.astype(F32) * 0.125).T.astype(BF)
        dq, dk, dv = [], [], []
        for hh in range(2):
            s = lax.dot_general(k * scaled[hh], q, NT, preferred_element_type=F32) + bias[...]
            e = jnp.exp(s - jnp.max(s, axis=0, keepdims=True))
            pt = e * (1.0 / jnp.sum(e, axis=0, keepdims=True))
            dpt = lax.dot_general(v * ones[hh], do, NT, preferred_element_type=F32)
            delta = jnp.sum(pt * dpt, axis=0, keepdims=True)
            dst = (pt * (dpt - delta)).astype(BF)
            dv.append(jnp.dot(pt.astype(BF), do, preferred_element_type=F32))
            dk.append(jnp.dot(dst, q_scaled, preferred_element_type=F32))
            dq.append(jnp.dot(k_turned[64 * hh:64 * hh + 64], dst, preferred_element_type=F32))
        dq_all = jnp.concatenate(dq, axis=0).T.astype(BF)
        dv_all = jnp.where(first, dv[0], dv[1]).astype(BF)
        d_proj[:, cols(0)] = dq_all
        d_proj[:, cols(width)] = jnp.where(first, dk[0], dk[1]).astype(BF)
        d_proj[:, cols(2 * width)] = dv_all
        vsum[G_QB:G_QB + 1, cols(0)] = colsum(dq_all.astype(F32))
        vsum[G_VB:G_VB + 1, cols(0)] = colsum(dv_all.astype(F32))

    rs.tick(4 * C)
    rs.tick(4 * C + 1)
    for t in range(4 * C):
        rs.finish(t)


def back(res, vec, ub, x, og, fsum, bsum, proj, mixed, wout, grads, C=2):
    n, width = x.shape
    M, rows, hid = grads.shape[0], grads.shape[1] // 16, grads.shape[2]
    sds = jax.ShapeDtypeStruct
    full = pltpu.VMEM((4, M, rows, hid), BF)
    part = pltpu.VMEM((4, M // 2, rows, hid), BF)
    return pl.pallas_call(
        functools.partial(back_kernel, C),
        out_shape=(
            sds((2, rows, hid), F32),
            sds((2, rows, hid), F32),
            sds((n, width), BF),
            sds((n, 3 * width), BF),
            sds((n, width), BF),
            sds((n, width), F32),
            sds((24, width), F32),
        ),
        in_specs=[SM] + [VM] * 6 + [ANY, ANY, VM, ANY],
        out_specs=(VM,) * 7,
        scratch_shapes=[
            pltpu.VMEM((M, 16 * rows, hid), BF),
            full, full, part, part, full, full,
            pltpu.VMEM((n, 3 * width), BF),
            pltpu.VMEM((n, width), BF),
            pltpu.VMEM((2, 128, width), BF),
            pltpu.VMEM((n, width), F32),
            pltpu.VMEM((n, width), BF),
            pltpu.VMEM((n, n), F32),
            DMA((3,)), DMA((6, C, 4)), DMA((6, C, 4)),
        ],
        compiler_params=pltpu.CompilerParams(
            collective_id=1, has_side_effects=True, vmem_limit_bytes=63 << 20
        ),
        name="back",
    )(res, vec, ub, x, og, fsum, bsum, proj, mixed, wout, grads)


def tail_kernel(
    C, vec, x, activ, mixed, d_proj, d_branch, d_after, wqkv, vin,
    qkv_out, out_out, d_in, vout,
    full, split, got, g, bx, by, bdx, bdy, bzu, bzd, dn, vs, vr,
    ss, sr, ps, pr, vss, vsr,
):
    p = Place()
    n, width = x.shape
    rows = qkv_out.shape[0]
    p.barrier(far=True)

    def pair(j):
        return remote(split.at[p.other, j], got.at[j], ps.at[j], pr.at[j], p.dp, p.other)

    for j in (0, 2, 1, 3):
        if j < 3:
            full[...] = lax.dot_general(
                activ[...], d_proj[:, j * width:(j + 1) * width], TN, preferred_element_type=F32
            )
        else:
            full[...] = lax.dot_general(mixed[...], d_branch[...], TN, preferred_element_type=F32)

        @pl.loop(0, 16)
        def _(o):
            for core in range(2):
                at = pl.ds(pl.multiple_of((2 * o + core) * rows, 8), rows)
                split[core, j, o] = full[at, :].astype(BF)

        pair(j).start()

    def write(c, v):
        if True:
            at = pl.ds(pl.multiple_of(c * width, 128), width)
            qkv_out[:, at] = v[0]

            @pl.when(c == 0)
            def _():
                qkv_out[:, 2 * width:] = v[1]

            @pl.when(c == 1)
            def _():
                out_out[...] = v[1]

    rs = RS(p, g, (bx, by, bdx, bdy, bzu, bzd), ss, sr, C, write)
    for j in (0, 2, 1, 3):
        pair(j).wait()

        @pl.loop(0, 16)
        def _(o):
            v = split[p.mp, j, o].astype(F32) + got[j, o].astype(F32)
            g[j // 2, o, :, (j % 2) * width:(j % 2 + 1) * width] = v.astype(BF)

    rs.tick(0)
    rs.tick(1)
    half = 256
    vs[0] = vin[...]

    @pl.loop(0, width // half)
    def _(j):
        at = pl.ds(pl.multiple_of(j * half, 128), half)
        dn[:, at] = lax.dot_general(d_proj[...], wqkv[at, :], NT, preferred_element_type=F32)

    rs.tick(2)
    rs.tick(3)

    @pl.loop(0, n // CHUNK)
    def _(r):
        at = pl.ds(pl.multiple_of(r * CHUNK, CHUNK), CHUNK)
        hat, inv = norm_parts(x[at, :].astype(F32))
        d = dn[at, :]
        vs[0, G_AG:G_AG + 1, :] += colsum(d * hat)
        vs[0, G_AB:G_AB + 1, :] += colsum(d)
        d_in[at, :] = (d_after[at, :] + norm_back(hat, inv, d * vec[V_AG:V_AG + 1, :])).astype(BF)

    steps = [(p.dp, p.other), (p.xn, p.mp), (p.yn, p.mp), (p.z1, p.mp), (p.z2, p.mp)]

    def hop(i):
        return remote(vs.at[i], vr.at[i], vss.at[i], vsr.at[i], *steps[i])

    hop(0).start()
    for i in range(5):
        rs.tick(4 + i)
        hop(i).wait()
        v = vs[i] + vr[i]
        if i < 4:
            vs[i + 1] = v
            hop(i + 1).start()
        else:
            vout[...] = v
    for t in range(9, 4 * C + 2):
        rs.tick(t)
    for t in range(4 * C):
        rs.finish(t)


def tail(vec, x, activ, mixed, d_proj, d_branch, d_after, wqkv, vsum, C=2):
    n, width = x.shape
    rows = width // 32
    sds = jax.ShapeDtypeStruct
    full = pltpu.VMEM((4, 2, rows, 2 * width), BF)
    part = pltpu.VMEM((4, 1, rows, 2 * width), BF)
    return pl.pallas_call(
        functools.partial(tail_kernel, C),
        out_shape=(
            sds((rows, 3 * width), F32),
            sds((rows, width), F32),
            sds((n, width), BF),
            sds((24, width), F32),
        ),
        in_specs=[VM] * 9,
        out_specs=(VM,) * 4,
        scratch_shapes=[
            pltpu.VMEM((width, width), F32),
            pltpu.VMEM((2, 4, 16, rows, width), BF),
            pltpu.VMEM((4, 16, rows, width), BF),
            pltpu.VMEM((2, 16, rows, 2 * width), BF),
            full, full, part, part, full, full,
            pltpu.VMEM((n, width), F32),
            pltpu.VMEM((5, 24, width), F32),
            pltpu.VMEM((5, 24, width), F32),
            DMA((6, C, 4)), DMA((6, C, 4)), DMA((4,)), DMA((4,)), DMA((5,)), DMA((5,)),
        ],
        compiler_params=pltpu.CompilerParams(
            collective_id=2, has_side_effects=True, vmem_limit_bytes=60 << 20
        ),
        name="tail",
    )(vec, x, activ, mixed, d_proj, d_branch, d_after, wqkv, vsum)


def local_shards(
    layer_input_rows,
    resolution,
    attn_gain,
    attn_bias,
    qkv_weight,
    qv_bias,
    out_weight,
    out_bias,
    attn_scale,
    ffn_scale,
    ffn_gain,
    ffn_bias,
    up_weight,
    up_bias,
    down_weight,
    down_bias,
    output_gradient,
):
    x, og = layer_input_rows, output_gradient
    width = x.shape[1]
    small = (
        attn_gain, attn_bias, qv_bias, out_bias, attn_scale, ffn_scale, ffn_gain, ffn_bias, down_bias
    )
    proj, activ, mixed, vec, ub, fsum, bsum, grads = front(
        resolution, small, up_bias, x, og, qkv_weight, out_weight, up_weight, down_weight
    )
    up_weight_grad, down_weight_grad, block_output, d_proj, d_branch, d_after, vsum = back(
        resolution, vec, ub, x, og, fsum, bsum, proj, mixed, out_weight, grads
    )
    qkv_out, out_out, input_grad, v = tail(
        vec, x, activ, mixed, d_proj, d_branch, d_after, qkv_weight, vsum
    )
    return (
        block_output,
        input_grad,
        v[G_AG],
        v[G_AB],
        qkv_out,
        v[G_QB:G_QB + 2],
        out_out,
        v[G_OB],
        v[G_AS],
        v[G_FS],
        v[G_FG:G_FG + 2],
        v[G_FB:G_FB + 2],
        up_weight_grad,
        v[G_UB:G_UB + 8].reshape(2, 4 * width),
        down_weight_grad,
        v[G_DB:G_DB + 2],
    )


def solution(mesh):
    placed = (
        P(("dp", "mp"), None),
        P(("dp", "mp")),
        P(),
        P(),
        P(),
        P(),
        P(),
        P(),
        P(),
        P(),
        P(),
        P(),
        P(None, "dp", "mp"),
        P(None, "mp"),
        P(None, "dp", "mp"),
        P(),
        P(("dp", "mp"), None),
    )
    fast = mesh.shape["dp"] == 16 and mesh.shape["mp"] == 2
    return jax.shard_map(
        local_shards if fast else shards,
        mesh=mesh,
        in_specs=placed,
        out_specs=(
            P(("dp", "mp"), None),
            P(("dp", "mp"), None),
            P(),
            P(),
            P(("dp", "mp"), None),
            P(),
            P(("dp", "mp"), None),
            P(),
            P(),
            P(),
            P(),
            P(),
            P(None, "dp", "mp"),
            P(),
            P(None, "dp", "mp"),
            P(),
        ),
        check_vma=False,
    )
```

```python
import functools

import jax
import jax.numpy as jnp
from jax import lax
from jax.experimental import pallas as pl
from jax.experimental.pallas import tpu as pltpu
from jax.sharding import PartitionSpec as P

MESHID = pl.DeviceIdType.MESH
BF = jnp.bfloat16
F32 = jnp.float32

HEADS = 12
PATCH_SMALL = 197
PATCH_LARGE = 577
CAPTION = 40


NORM_EPS = 1e-06
HIGH = lax.Precision.HIGHEST


def layer_norm(field, gain, shift):
    center = field - jnp.mean(field, axis=-1, keepdims=True)
    spread = jnp.mean(center * center, axis=-1, keepdims=True)
    return center * lax.rsqrt(spread + NORM_EPS) * gain + shift


def exact_gelu(field):
    return jax.nn.gelu(field, approximate=False)


def ceil_div(numer, denom):
    return -(-numer // denom)


def slot_layout(res_group, row_count):
    position = jnp.arange(row_count, dtype=jnp.int32)
    small_len = PATCH_SMALL + CAPTION
    large_kind = jnp.where(
        position < PATCH_LARGE, 1, jnp.where(position < PATCH_LARGE + CAPTION, 0, 2)
    )
    large_segment = jnp.where(position < PATCH_LARGE + CAPTION, 0, 2)
    within = position % small_len
    small_kind = jnp.where(position < 2 * small_len, jnp.where(within < PATCH_SMALL, 1, 0), 2)
    small_segment = jnp.where(position < 2 * small_len, position // small_len, 2)
    row_kind = jnp.where(res_group == 1, large_kind, small_kind).astype(jnp.int32)
    segment = jnp.where(res_group == 1, large_segment, small_segment)
    return (row_kind, segment)


def contract_rows(left, right):
    return lax.dot_general(
        left, right, (((0,), (0,)), ((), ())), preferred_element_type=jnp.float32
    )


def contract_cols(left, right):
    return lax.dot_general(
        left, right, (((1,), (1,)), ((), ())), preferred_element_type=jnp.float32
    )


def shards(
    layer_input_rows,
    resolution,
    attn_gain,
    attn_bias,
    qkv_weight,
    qv_bias,
    out_weight,
    out_bias,
    attn_scale,
    ffn_scale,
    ffn_gain,
    ffn_bias,
    up_weight,
    up_bias,
    down_weight,
    down_bias,
    output_gradient,
):
    model_width = layer_input_rows.shape[1]
    slot_count = resolution.shape[0]
    slot_rows = layer_input_rows.shape[0] // slot_count
    head_count = HEADS
    head_width = model_width // head_count
    score_scale = head_width ** (-0.5)
    hidden_part = up_weight.shape[2]
    dp_count = lax.axis_size("dp")
    mp_count = lax.axis_size("mp")
    dp_index = lax.axis_index("dp")
    mp_index = lax.axis_index("mp")
    lang_count = dp_count // 4
    vis_count = dp_count - lang_count
    capacity = max(
        ceil_div(slot_count * PATCH_LARGE, vis_count),
        ceil_div(2 * slot_count * CAPTION, lang_count),
    )
    recv_rows = dp_count * capacity
    kinds, segments = jax.vmap(lambda res_group: slot_layout(res_group, slot_rows))(resolution)
    row_kind = kinds.reshape(-1)
    live_rows = (row_kind != 2).astype(jnp.float32)[:, None]
    vision = (row_kind == 1)[:, None]
    kind_onehot = jnp.stack([row_kind == 0, row_kind == 1], axis=1).astype(jnp.float32)
    rank_vis = jnp.cumsum((row_kind == 1).astype(jnp.int32)) - 1
    rank_txt = jnp.cumsum((row_kind == 0).astype(jnp.int32)) - 1
    target = jnp.where(
        row_kind == 1,
        (rank_vis + dp_index) % vis_count,
        vis_count + (rank_txt + dp_index) % lang_count,
    )
    position = jnp.where(row_kind == 1, rank_vis // vis_count, rank_txt // lang_count)
    slot_index = jnp.where(row_kind == 2, recv_rows, target * capacity + position)

    def to_slots(row_values):
        buffer = (
            jnp.zeros((recv_rows, model_width), row_values.dtype)
            .at[slot_index]
            .set(row_values, mode="drop")
        )
        return buffer.reshape(dp_count, capacity, model_width)

    def from_slots(buffer):
        return jnp.take(
            buffer.reshape(recv_rows, model_width), slot_index, axis=0, mode="fill", fill_value=0
        )

    my_expert = jnp.where(dp_index < vis_count, 1, 0)
    full_up, full_down = (
        lax.all_gather(up_weight, "dp", axis=1, tiled=True),
        lax.all_gather(down_weight, "dp", axis=1, tiled=True),
    )
    own_up = jnp.where(my_expert == 1, full_up[1], full_up[0])
    own_down = jnp.where(my_expert == 1, full_down[1], full_down[0])
    own_up_bias = jnp.where(my_expert == 1, up_bias[1], up_bias[0])
    own_down_bias = jnp.where(my_expert == 1, down_bias[1], down_bias[0])
    x_float = layer_input_rows.astype(jnp.float32)
    normed, norm_pull = jax.vjp(layer_norm, x_float, attn_gain, attn_bias)
    activ = normed.astype(jnp.bfloat16)
    projected = jnp.dot(activ, qkv_weight, preferred_element_type=jnp.float32)
    query = (projected[:, :model_width] + qv_bias[0]).astype(jnp.bfloat16)
    keys = projected[:, model_width : 2 * model_width].astype(jnp.bfloat16)
    values = (projected[:, 2 * model_width :] + qv_bias[1]).astype(jnp.bfloat16)
    query_slots = query.reshape(slot_count, slot_rows, head_count, head_width)
    key_slots = keys.reshape(slot_count, slot_rows, head_count, head_width)
    value_slots = values.reshape(slot_count, slot_rows, head_count, head_width)

    def slot_scores(query_heads, key_heads, segment):
        raw_scores = (
            jnp.einsum("qhd,khd->hqk", query_heads, key_heads, preferred_element_type=jnp.float32)
            * score_scale
        )
        same_seq = (segment[:, None] == segment[None, :])[None]
        return jnp.where(same_seq, raw_scores, -1000000000.0)

    def attend(block_item):
        query_heads, key_heads, value_heads, segment = block_item
        masked = slot_scores(query_heads, key_heads, segment)
        row_max = jnp.max(masked, axis=-1, keepdims=True)
        weights_exp = jnp.exp(masked - row_max)
        row_total = jnp.sum(weights_exp, axis=-1, keepdims=True)
        attn_probs = (weights_exp / row_total).astype(jnp.bfloat16)
        attn_mixed = jnp.einsum(
            "hqk,khd->qhd", attn_probs, value_heads, preferred_element_type=jnp.float32
        )
        log_total = (row_max + jnp.log(row_total))[..., 0]
        return (attn_mixed.reshape(slot_rows, model_width).astype(jnp.bfloat16), log_total)

    attn_mixed, log_totals = lax.map(attend, (query_slots, key_slots, value_slots, segments))
    attn_mixed = attn_mixed.reshape(-1, model_width)
    branch = jnp.dot(attn_mixed, out_weight, preferred_element_type=jnp.float32) + out_bias
    after_attn = x_float + live_rows * attn_scale * branch
    gain_rows = jnp.where(vision, ffn_gain[1], ffn_gain[0])
    shift_rows = jnp.where(vision, ffn_bias[1], ffn_bias[0])
    ffn_normed, norm2_pull = jax.vjp(layer_norm, after_attn, gain_rows, shift_rows)
    sent_rows = ffn_normed.astype(jnp.bfloat16)
    arrived = lax.all_to_all(
        to_slots(sent_rows), "dp", split_axis=0, concat_axis=0, tiled=True
    ).reshape(recv_rows, model_width)
    paired = lax.all_gather(arrived, "mp", axis=0, tiled=True)
    preact = jnp.dot(paired, own_up, preferred_element_type=jnp.float32) + own_up_bias
    hidden, gelu_pull = jax.vjp(exact_gelu, preact)
    hidden_low = hidden.astype(jnp.bfloat16)
    partial_out = contract_cols(hidden_low, own_down)
    expert_sum = (
        lax.psum_scatter(
            partial_out.astype(jnp.bfloat16), "mp", scatter_dimension=0, tiled=True
        ).astype(jnp.float32)
        + own_down_bias
    )
    returned = lax.all_to_all(
        expert_sum.astype(jnp.bfloat16).reshape(dp_count, capacity, model_width),
        "dp",
        split_axis=0,
        concat_axis=0,
        tiled=True,
    )
    expert_rows = from_slots(returned).astype(jnp.float32)
    block_output = (after_attn + live_rows * ffn_scale * expert_rows).astype(jnp.bfloat16)
    grad_float = output_gradient.astype(jnp.float32)
    d_expert = (live_rows * ffn_scale * grad_float).astype(jnp.bfloat16)
    ffn_scale_grad = jnp.sum(live_rows * expert_rows * grad_float, axis=0)
    down_bias_grad = jnp.dot(kind_onehot.T, d_expert.astype(jnp.float32), precision=HIGH)
    arrived_grad = lax.all_to_all(
        to_slots(d_expert), "dp", split_axis=0, concat_axis=0, tiled=True
    ).reshape(recv_rows, model_width)
    paired_grad = lax.all_gather(arrived_grad, "mp", axis=0, tiled=True)
    d_hidden = jnp.dot(paired_grad, own_down, preferred_element_type=jnp.float32)
    d_preact = gelu_pull(d_hidden)[0].astype(jnp.bfloat16)
    own_down_grad = contract_rows(paired_grad, hidden_low)
    own_up_grad = contract_rows(paired, d_preact)
    own_bias_grad = jnp.sum(d_preact.astype(jnp.float32), axis=0)
    d_normed_part = contract_cols(d_preact, own_up)
    d_normed = lax.psum_scatter(
        d_normed_part.astype(jnp.bfloat16), "mp", scatter_dimension=0, tiled=True
    )
    back_grad = lax.all_to_all(
        d_normed.reshape(dp_count, capacity, model_width),
        "dp",
        split_axis=0,
        concat_axis=0,
        tiled=True,
    )
    d_ffn_normed = from_slots(back_grad).astype(jnp.float32)
    d_after_part, gain_grad_rows, shift_grad_rows = norm2_pull(d_ffn_normed)
    ffn_gain_grad = jnp.dot(kind_onehot.T, gain_grad_rows, precision=HIGH)
    ffn_bias_grad = jnp.dot(kind_onehot.T, shift_grad_rows, precision=HIGH)
    d_after = grad_float + d_after_part
    d_branch = (live_rows * attn_scale * d_after).astype(jnp.bfloat16)
    attn_scale_grad = jnp.sum(live_rows * branch * d_after, axis=0)
    out_bias_grad = jnp.sum(d_branch.astype(jnp.float32), axis=0)
    out_weight_grad = contract_rows(attn_mixed, d_branch)
    d_mixed = contract_cols(d_branch, out_weight).astype(jnp.bfloat16)
    d_mixed_slots = d_mixed.reshape(slot_count, slot_rows, head_count, head_width)

    def attend_back(block_item):
        query_heads, key_heads, value_heads, segment, log_total, d_heads = block_item
        masked = slot_scores(query_heads, key_heads, segment)
        probs_full = jnp.exp(masked - log_total[..., None])
        d_probs = jnp.einsum(
            "qhd,khd->hqk", d_heads, value_heads, preferred_element_type=jnp.float32
        )
        row_delta = jnp.sum(probs_full * d_probs, axis=-1, keepdims=True)
        d_scores = (probs_full * (d_probs - row_delta)).astype(jnp.bfloat16)
        probs_low = probs_full.astype(jnp.bfloat16)
        grad_value = jnp.einsum(
            "hqk,qhd->khd", probs_low, d_heads, preferred_element_type=jnp.float32
        )
        grad_query = (
            jnp.einsum("hqk,khd->qhd", d_scores, key_heads, preferred_element_type=jnp.float32)
            * score_scale
        )
        grad_key = (
            jnp.einsum("hqk,qhd->khd", d_scores, query_heads, preferred_element_type=jnp.float32)
            * score_scale
        )
        joined = jnp.concatenate(
            [
                grad_query.reshape(slot_rows, model_width),
                grad_key.reshape(slot_rows, model_width),
                grad_value.reshape(slot_rows, model_width),
            ],
            axis=1,
        )
        return joined.astype(jnp.bfloat16)

    d_projected = lax.map(
        attend_back, (query_slots, key_slots, value_slots, segments, log_totals, d_mixed_slots)
    ).reshape(-1, 3 * model_width)
    qkv_weight_grad = contract_rows(activ, d_projected)
    d_proj_float = d_projected.astype(jnp.float32)
    qv_bias_grad = jnp.stack(
        [
            jnp.sum(d_proj_float[:, :model_width], axis=0),
            jnp.sum(d_proj_float[:, 2 * model_width :], axis=0),
        ]
    )
    d_attn_normed = contract_cols(d_projected, qkv_weight)
    d_input_part, attn_gain_grad, attn_bias_grad = norm_pull(d_attn_normed)
    input_grad = (d_after + d_input_part).astype(jnp.bfloat16)
    expert_pick = (jnp.arange(2) == my_expert).astype(jnp.float32)[:, None, None]
    up_weight_grad, down_weight_grad = (
        lax.psum_scatter(expert_pick * own_up_grad[None], "dp", scatter_dimension=1, tiled=True),
        lax.psum_scatter(expert_pick * own_down_grad[None], "dp", scatter_dimension=1, tiled=True),
    )
    up_bias_full = (
        jnp.zeros((2, mp_count, hidden_part), jnp.float32)
        .at[my_expert, mp_index]
        .set(own_bias_grad)
        .reshape(2, mp_count * hidden_part)
    )
    vector_sums = lax.psum(
        (
            attn_gain_grad,
            attn_bias_grad,
            qv_bias_grad,
            out_bias_grad,
            attn_scale_grad,
            ffn_scale_grad,
            ffn_gain_grad,
            ffn_bias_grad,
            up_bias_full,
            down_bias_grad,
        ),
        ("dp", "mp"),
    )
    matrix_sums = (
        lax.psum_scatter(qkv_weight_grad, ("dp", "mp"), scatter_dimension=0, tiled=True),
        lax.psum_scatter(out_weight_grad, ("dp", "mp"), scatter_dimension=0, tiled=True),
    )
    return (
        block_output,
        input_grad,
        vector_sums[0],
        vector_sums[1],
        matrix_sums[0],
        vector_sums[2],
        matrix_sums[1],
        vector_sums[3],
        vector_sums[4],
        vector_sums[5],
        vector_sums[6],
        vector_sums[7],
        up_weight_grad,
        vector_sums[8],
        down_weight_grad,
        vector_sums[9],
    )


NT = (((1,), (1,)), ((), ()))
TN = (((0,), (0,)), ((), ()))
SMALL = PATCH_SMALL + CAPTION
CAPS = 2 * CAPTION
ANY = pl.BlockSpec(memory_space=pl.ANY)
VM = pl.BlockSpec(memory_space=pltpu.VMEM)
SM = pl.BlockSpec(memory_space=pltpu.SMEM)
DMA = pltpu.SemaphoreType.DMA
CHUNK = 128
V_AG, V_AB, V_QB, V_VB, V_OB, V_AS, V_FS, V_FG, V_FB, V_DB = 0, 1, 2, 3, 4, 5, 6, 7, 9, 11
G_AG, G_AB, G_QB, G_VB, G_OB, G_AS, G_FS, G_FG, G_FB, G_DB, G_UB = 0, 1, 2, 3, 4, 5, 6, 7, 9, 11, 16


def kind_of(res, pos):
    one = lambda c: c.astype(jnp.int32)
    big_seg = 2 * one(pos >= PATCH_LARGE + CAPTION)
    big_kind = 1 - one(pos >= PATCH_LARGE) + big_seg
    small_seg = one(pos >= SMALL) + one(pos >= 2 * SMALL)
    small_pad = one(pos >= 2 * SMALL)
    within = pos - SMALL * small_seg
    small_kind = (1 - small_pad) * one(within < PATCH_SMALL) + 2 * small_pad
    return (
        res * big_kind + (1 - res) * small_kind,
        res * big_seg + (1 - res) * small_seg,
    )


def caption_place(res, slot):
    late = (slot >= CAPTION).astype(jnp.int32)
    big = (1 - late) * (PATCH_LARGE + slot) - late
    small = PATCH_SMALL + slot + late * (SMALL - CAPTION)
    none = (slot >= CAPS).astype(jnp.int32)
    place = res * big + (1 - res) * small
    return (1 - none) * place - none


def iota(shape, dim):
    return lax.broadcasted_iota(jnp.int32, shape, dim)


def fill_bias(res, bias):
    n = bias.shape[0]
    across = kind_of(res, iota((1, n), 1))[1]

    @pl.loop(0, n // CHUNK)
    def _(r):
        base = pl.multiple_of(r * CHUNK, CHUNK)
        down = kind_of(res, iota((CHUNK, 1), 0) + base)[1]
        bias[pl.ds(base, CHUNK), :] = jnp.where(down == across, 0.0, -1000000000.0)


def norm_parts(v):
    center = v - jnp.mean(v, axis=-1, keepdims=True)
    inv = lax.rsqrt(jnp.mean(center * center, axis=-1, keepdims=True) + NORM_EPS)
    return center * inv, inv


def norm_back(xhat, inv, d_hat):
    mean_d = jnp.mean(d_hat, axis=-1, keepdims=True)
    mean_dx = jnp.mean(d_hat * xhat, axis=-1, keepdims=True)
    return inv * (d_hat - mean_d - xhat * mean_dx)


def half_mask(hh, scale):
    lane = iota((1, 128), 1)
    inside = (lane < 64) if hh == 0 else (lane >= 64)
    return jnp.where(inside, scale, 0.0).astype(BF)


def colsum(v):
    return jnp.sum(v, axis=0, keepdims=True)


def dyn_unit(z, k):
    m = k // 2
    zz = z + (z // 2) * (3 - 2 * z)
    u = (1 - m) * (zz + k - 2 * k * zz) + m * k
    w = z // 2
    return u + w * (3 - 2 * u)


class Place:
    def __init__(s):
        s.dp, s.mp = lax.axis_index("dp"), lax.axis_index("mp")
        s.z = s.dp // 4
        s.y = (s.dp // 2) % 2
        s.x = s.dp % 2
        s.xn = s.dp + 1 - 2 * s.x
        s.yn = s.dp + 2 - 4 * s.y
        s.z1 = s.dp + 4 - 8 * (s.z % 2)
        s.z2 = s.dp + 8 - 16 * (s.z // 2)
        s.other = 1 - s.mp
        s.q = s.y * 2 + s.x
        s.dn = s.dp + 3 - 2 * s.x - 4 * s.y
        s.plane = [
            (s.xn, s.y * 2 + 1 - s.x), (s.yn, 2 - 2 * s.y + s.x), (s.dn, 3 - 2 * s.y - s.x)
        ]

    def barrier(s, far=False):
        bar = pltpu.get_barrier_semaphore()
        dp, z = s.dp, s.z

        def sig(d, m):
            pl.semaphore_signal(bar, inc=1, device_id=(d, m), device_id_type=MESHID)

        sig(s.xn, s.mp)
        sig(s.yn, s.mp)
        sig(dp, s.other)
        sig(s.z2 if far else s.dn, s.mp)

        @pl.when(z > 0)
        def _():
            sig(dp - 4, s.mp)

        @pl.when(z < 3)
        def _():
            sig(dp + 4, s.mp)

        pl.semaphore_wait(bar, 5 + ((z + 1) // 2) % 2)


def remote(src, dst, ss, sr, dev, core):
    return pltpu.make_async_remote_copy(
        src_ref=src, dst_ref=dst, send_sem=ss, recv_sem=sr,
        device_id=(dev, core), device_id_type=MESHID,
    )


class AG:
    def __init__(s, place, g, ss, sr, C):
        s.p, s.g, s.ss, s.sr, s.C = place, g, ss, sr, C
        s.rows, s.hid = g.shape[1] // 16, g.shape[2]
        s.ck = s.hid // C
        s.col = place.y * 2 + place.x

    def cp(s, kind, c, u, owner, dev, half=None):
        h = slice(0, 2) if half is None else slice(half, half + 1)
        at = pl.ds(pl.multiple_of(owner * s.rows, 16), s.rows)
        w = s.g.at[h, at, pl.ds(pl.multiple_of(c * s.ck, 128), s.ck)]
        rk = 0 if kind == 1 else kind
        return remote(w, w, s.ss.at[kind, c, u], s.sr.at[rk, c, u], dev, s.p.mp)

    def send(s, k, c, local):
        p = s.p
        z, dp = p.z, p.dp
        u = dyn_unit(z, k)
        owner = u * 4 + s.col
        if not local:
            s.cp(0, c, u, owner, dp).wait_recv()

        @pl.when((u <= z) & (z < 3))
        def _():
            s.cp(0, c, u, owner, dp + 4).start()

        @pl.when((u >= z) & (z > 0))
        def _():
            s.cp(1, c, u, owner, dp - 4).start()

        s.cp(2, c, u, owner, p.xn).start()
        s.cp(3, c, u, owner, p.yn).start()

    def forward(s, k, c):
        p = s.p
        u = dyn_unit(p.z, k)
        xo = u * 4 + p.y * 2 + 1 - p.x
        yo = u * 4 + 2 - 2 * p.y + p.x
        s.cp(2, c, u, xo, p.dp).wait_recv()
        s.cp(5, c, u, xo, p.yn, half=0).start()
        s.cp(3, c, u, yo, p.dp).wait_recv()
        s.cp(4, c, u, yo, p.xn, half=1).start()

    def tick(s, t):
        c, m = t // 3, t % 3
        s.send(1 + m, c, False)
        s.forward(m, c)
        if isinstance(t, int):
            if m == 0 and c > 0:
                s.forward(3, c - 1)
        else:
            @pl.when((m == 0) & (c > 0))
            def _():
                s.forward(3, c - 1)

    def arrived(s, c):
        for k in range(4):
            u = dyn_unit(s.p.z, k)
            own = u * 4 + s.col
            s.cp(4, c, u, own, s.p.dp, half=1).wait_recv()
            s.cp(5, c, u, own, s.p.dp, half=0).wait_recv()

    def finish(s, k, c):
        p = s.p
        z, dp = p.z, p.dp
        u = dyn_unit(z, k)
        own = u * 4 + s.col
        s.cp(2, c, u, own, dp).wait_send()
        s.cp(3, c, u, own, dp).wait_send()
        s.cp(4, c, u, own, dp, half=1).wait_send()
        s.cp(5, c, u, own, dp, half=0).wait_send()

        @pl.when((u <= z) & (z < 3))
        def _():
            s.cp(0, c, u, own, dp).wait_send()

        @pl.when((u >= z) & (z > 0))
        def _():
            s.cp(1, c, u, own, dp).wait_send()


class CaptionGather:
    def __init__(s, place, own, wc, lsem, ps, pr, zs, zr):
        s.p, s.own, s.wc, s.lsem, s.ps, s.pr, s.zs, s.zr = place, own, wc, lsem, ps, pr, zs, zr
        s.rows, s.quarter = own.shape[1], wc.shape[2]
        s.at = pl.ds(pl.multiple_of(place.dp * s.rows, 16), s.rows)

    def part(s, q):
        return s.own.at[:, :, pl.ds(pl.multiple_of(q * s.quarter, 128), s.quarter)]

    def keep(s):
        return pltpu.make_async_copy(s.part(s.p.q), s.wc.at[:, s.at, :], s.lsem)

    def flat(s, i):
        dev, q = s.p.plane[i]
        return remote(s.part(q), s.wc.at[:, s.at, :], s.ps.at[i], s.pr.at[i], dev, s.p.mp)

    def start(s):
        s.keep().start()
        for i in range(3):
            s.flat(i).start()

    def hop(s, kind, u, dev):
        n = 4 * s.rows
        w = s.wc.at[:, pl.ds(pl.multiple_of(u * n, 16), n), :]
        return remote(w, w, s.zs.at[kind, u], s.zr.at[u], dev, s.p.mp)

    def step(s, k):
        z, dp = s.p.z, s.p.dp
        u = dyn_unit(z, k)
        if isinstance(k, int) and k == 0:
            s.keep().wait()
            for i in range(3):
                s.flat(i).wait()
        else:
            s.hop(0, u, dp).wait_recv()

        @pl.when((u <= z) & (z < 3))
        def _():
            s.hop(0, u, dp + 4).start()

        @pl.when((u >= z) & (z > 0))
        def _():
            s.hop(1, u, dp - 4).start()

    def finish(s):
        z, dp = s.p.z, s.p.dp
        for k in range(4):
            u = dyn_unit(z, k)

            @pl.when((u <= z) & (z < 3))
            def _():
                s.hop(0, u, dp + 4).wait_send()

            @pl.when((u >= z) & (z > 0))
            def _():
                s.hop(1, u, dp - 4).wait_send()


class CaptionScatter:
    def __init__(s, place, g, bu, bd, got, ps, pr, zs, zr, out):
        s.p, s.g, s.bu, s.bd, s.got, s.out = place, g, bu, bd, got, out
        s.ps, s.pr, s.zs, s.zr = ps, pr, zs, zr
        s.rows = g.shape[1] // 16

    def win(s, u):
        n = 4 * s.rows
        return s.g.at[:, pl.ds(pl.multiple_of(u * n, 16), n), :]

    def up(s, u):
        return remote(s.win(u), s.bu.at[u], s.zs.at[0, u], s.zr.at[0, u], s.p.dp + 4, s.p.mp)

    def down(s, u):
        return remote(s.win(u), s.bd.at[u], s.zs.at[1, u], s.zr.at[1, u], s.p.dp - 4, s.p.mp)

    def owner(s, q):
        at = pl.multiple_of((s.p.z * 4 + q) * s.rows, 16)
        return s.g.at[:, pl.ds(at, s.rows), :]

    def flat(s, i):
        dev, q = s.p.plane[i]
        return remote(s.owner(q), s.got.at[i], s.ps.at[i], s.pr.at[i], dev, s.p.mp)

    def step(s, k):
        z = s.p.z
        u = dyn_unit(z, k)
        o = s.win(u)

        def go(pred, wu, wd, send):
            @pl.when(pred)
            def _():
                v = o[...].astype(F32)
                if wu:
                    s.up(u).wait_recv()
                    v = v + s.bu.at[u][...].astype(F32)
                if wd:
                    s.down(u).wait_recv()
                    v = v + s.bd.at[u][...].astype(F32)
                if wu or wd:
                    o[...] = v.astype(BF)
                if send is not None:
                    send(u).start()

        if k > 0:
            go((u > z) & (z > 0), True, False, s.up)
            go((u > z) & (z == 0), False, False, s.up)
            go((u < z) & (z < 3), False, True, s.down)
            go((u < z) & (z == 3), False, False, s.down)
        else:
            go(z == 0, False, True, None)
            go(z == 3, True, False, None)
            go((z > 0) & (z < 3), True, True, None)
            for i in range(3):
                s.flat(i).start()

    def finish(s):
        own = s.owner(s.p.q)
        s.out(s.p.q, own[0].astype(F32), own[1].astype(F32))
        for i in range(3):
            s.flat(i).wait()
            s.out(s.p.plane[i][1], s.got[i, 0].astype(F32), s.got[i, 1].astype(F32))
        for k in range(1, 4):
            u = dyn_unit(s.p.z, k)

            @pl.when(u > s.p.z)
            def _():
                s.up(u).wait_send()

            @pl.when(u < s.p.z)
            def _():
                s.down(u).wait_send()


class RS:
    def __init__(s, place, g, bufs, ss, sr, C, write):
        s.p, s.g, s.write = place, g, write
        s.bx, s.by, s.bdx, s.bdy, s.bzu, s.bzd = bufs
        s.ss, s.sr, s.C = ss, sr, C
        s.M = g.shape[0]
        s.flat = len(g.shape) == 3
        s.rows = g.shape[1] // 16 if s.flat else g.shape[2]
        s.ck = g.shape[-1] // C
        s.h0 = s.M // 2
        x, y = place.x, place.y
        s.oo = y * 2 + x
        s.ox = y * 2 + 1 - x
        s.oy = 2 - 2 * y + x
        s.od = 3 - 2 * y - x

    def cols(s, c):
        return pl.ds(pl.multiple_of(c * s.ck, 128), s.ck)

    def win(s, u, col, c, lo=0, hi=None):
        hi = s.M if hi is None else hi
        if s.flat:
            at = pl.multiple_of((u * 4 + col) * s.rows, 16)
            return s.g.at[lo:hi, pl.ds(at, s.rows), s.cols(c)]
        return s.g.at[lo:hi, u * 4 + col, :, s.cols(c)]

    def cp(s, kind, u, c, src, dst, dev):
        return remote(src, dst, s.ss.at[kind, c, u], s.sr.at[kind, c, u], dev, s.p.mp)

    def bw(s, b, u, c):
        return b.at[u, :, :, s.cols(c)]

    def c_dy(s, u, c):
        return s.cp(0, u, c, s.win(u, s.od, c, 0, s.h0), s.bw(s.bdy, u, c), s.p.yn)

    def c_dx(s, u, c):
        return s.cp(1, u, c, s.win(u, s.od, c, s.h0), s.bw(s.bdx, u, c), s.p.xn)

    def c_x(s, u, c):
        return s.cp(2, u, c, s.win(u, s.ox, c), s.bw(s.bx, u, c), s.p.xn)

    def c_y(s, u, c):
        return s.cp(3, u, c, s.win(u, s.oy, c), s.bw(s.by, u, c), s.p.yn)

    def c_zu(s, u, c):
        return s.cp(4, u, c, s.win(u, s.oo, c), s.bw(s.bzu, u, c), s.p.dp + 4)

    def c_zd(s, u, c):
        return s.cp(5, u, c, s.win(u, s.oo, c), s.bw(s.bzd, u, c), s.p.dp - 4)

    def item(s, t):
        return dyn_unit(s.p.z, 3 - t // s.C), t % s.C

    def s1(s, t):
        u, c = s.item(t)
        s.c_dy(u, c).start()
        s.c_dx(u, c).start()

    def add(s, dst, src):
        dst[...] = (dst[...].astype(F32) + src[...].astype(F32)).astype(BF)

    def s2(s, t):
        u, c = s.item(t)
        s.c_dy(u, c).wait_recv()
        s.add(s.win(u, s.ox, c, 0, s.h0), s.bw(s.bdy, u, c))
        s.c_x(u, c).start()
        s.c_dx(u, c).wait_recv()
        s.add(s.win(u, s.oy, c, s.h0), s.bw(s.bdx, u, c))
        s.c_y(u, c).start()

    def s3(s, t):
        u, c = s.item(t)
        z = s.p.z
        s.c_x(u, c).wait_recv()
        s.c_y(u, c).wait_recv()
        o = s.win(u, s.oo, c)

        def total(*bufs):
            v = o[...].astype(F32)
            for b in (s.bx, s.by) + bufs:
                v = v + s.bw(b, u, c)[...].astype(F32)
            return v

        def go(pred, wu, wd, send):
            @pl.when(pred)
            def _():
                more = ()
                if wu:
                    s.c_zu(u, c).wait_recv()
                    more += (s.bzu,)
                if wd:
                    s.c_zd(u, c).wait_recv()
                    more += (s.bzd,)
                v = total(*more)
                if send is None:
                    s.write(c, v)
                else:
                    o[...] = v.astype(BF)
                    send(u, c).start()

        up, dn, own = u > z, u < z, u == z
        go(up & (z > 0), True, False, s.c_zu)
        go(up & (z == 0), False, False, s.c_zu)
        go(dn & (z < 3), False, True, s.c_zd)
        go(dn & (z == 3), False, False, s.c_zd)
        go(own & (z == 0), False, True, None)
        go(own & (z == 3), True, False, None)
        go(own & (z > 0) & (z < 3), True, True, None)

    def tick(s, t):
        n = 4 * s.C
        if t < n:
            s.s1(t)
        if 0 <= t - 1 < n:
            s.s2(t - 1)
        if 0 <= t - 2 < n:
            s.s3(t - 2)

    def finish(s, t):
        u, c = s.item(t)
        for f in (s.c_dy, s.c_dx, s.c_x, s.c_y):
            f(u, c).wait_send()

        @pl.when(u > s.p.z)
        def _():
            s.c_zu(u, c).wait_send()

        @pl.when(u < s.p.z)
        def _():
            s.c_zd(u, c).wait_send()


def load_all(pairs, sem):
    copies = [pltpu.make_async_copy(a, b, sem.at[i]) for i, (a, b) in enumerate(pairs)]
    for c in copies:
        c.start()
    return copies


def front_kernel(
    C, res_ref, a_gain, a_bias, qv_bias, o_bias, a_scale, f_scale, f_gain, f_bias, dn_bias, up_bias,
    x, og, wqkv, wout, up_ref, down_ref,
    proj, activ, mixed, vec, ub, fsum, bsum, cgrads, grads,
    g, wc, cown, bias, qkvb, xall, gall, xt, gt, cr, crt, accf, accb, rcv, stage, hid, dpre, ubg,
    chid, cdpre, pc, prc, prq,
    lsem, ss, sr, ps, pr, cs, cg_r, zs, zr, bs, br,
):
    p = Place()
    n, width = x.shape
    res = res_ref[0]
    ag = AG(p, g, ss, sr, C)
    mine = pl.ds(pl.multiple_of(p.dp * ag.rows, 16), ag.rows)
    loads = load_all(
        [
            (up_ref.at[1], g.at[0, mine, :]), (down_ref.at[1], g.at[1, mine, :]),
            (up_ref.at[0], cown.at[0]), (down_ref.at[0], cown.at[1]),
        ],
        lsem,
    )
    p.barrier()
    for c in loads:
        c.wait()
    capg = CaptionGather(p, cown, wc, lsem.at[4], cs.at[0], cg_r.at[0], zs, zr)
    capg.start()
    for c in range(C):
        ag.send(0, c, True)

    for row, ref in (
        (V_AG, a_gain), (V_AB, a_bias), (V_OB, o_bias), (V_AS, a_scale), (V_FS, f_scale),
    ):
        vec[row:row + 1, :] = ref[...].reshape(1, width)
    for row, ref in ((V_QB, qv_bias), (V_FG, f_gain), (V_FB, f_bias), (V_DB, dn_bias)):
        vec[row:row + 2, :] = ref[...]
    vec[13:16, :] = jnp.zeros((3, width), F32)

    @pl.loop(0, n // CHUNK)
    def _(r):
        at = pl.ds(pl.multiple_of(r * CHUNK, CHUNK), CHUNK)
        hat, _ = norm_parts(x[at, :].astype(F32))
        activ[at, :] = (hat * vec[V_AG:V_AG + 1, :] + vec[V_AB:V_AB + 1, :]).astype(BF)

    qkvb[:, :width] = vec[V_QB:V_QB + 1, :]
    qkvb[:, width:2 * width] = jnp.zeros((1, width), F32)
    qkvb[:, 2 * width:] = vec[V_VB:V_VB + 1, :]
    part = 384

    @pl.loop(0, 3 * width // part)
    def _(j):
        at = pl.ds(pl.multiple_of(j * part, 128), part)
        v = jnp.dot(activ[...], wqkv[:, at], preferred_element_type=F32)
        proj[:, at] = (v + qkvb[:, at]).astype(BF)

    fill_bias(res, bias)
    capg.step(0)
    masks = [half_mask(0, 0.125), half_mask(1, 0.125)]
    first = iota((1, 128), 1) < 64

    @pl.loop(0, width // 128)
    def _(h):
        def cols(base):
            return pl.ds(pl.multiple_of(base + h * 128, 128), 128)

        @pl.when(h > 0)
        def _():
            ag.tick(h - 1)

        @pl.when((h > 0) & (h % 2 == 0))
        def _():
            capg.step(h // 2)

        q, k, v = proj[:, cols(0)], proj[:, cols(width)], proj[:, cols(2 * width)]
        outs = []
        for hh in range(2):
            s = lax.dot_general(q * masks[hh], k, NT, preferred_element_type=F32) + bias[...]
            e = jnp.exp(s - jnp.max(s, axis=-1, keepdims=True))
            pr_low = (e * (1.0 / jnp.sum(e, axis=-1, keepdims=True))).astype(BF)
            outs.append(jnp.dot(pr_low, v, preferred_element_type=F32))
        mixed[:, cols(0)] = jnp.where(first, outs[0], outs[1]).astype(BF)

    ag.tick(5)
    capg.step(3)
    half = 256

    @pl.loop(0, width // half)
    def _(j):
        at = pl.ds(pl.multiple_of(j * half, 128), half)
        accf[:n, at] = jnp.dot(mixed[...], wout[:, at], preferred_element_type=F32)

    img = p.mp * n
    caps = p.mp * 4 * CAPS + p.q * CAPS

    @pl.loop(0, n // CHUNK)
    def _(r):
        base = pl.multiple_of(r * CHUNK, CHUNK)
        at = pl.ds(base, CHUNK)
        to = pl.ds(pl.multiple_of(img + base, 128), CHUNK)
        kind = kind_of(res, iota((CHUNK, 1), 0) + base)[0]
        live = (kind < 2).astype(F32)
        row = x[at, :].astype(F32)
        row = row + live * vec[V_AS:V_AS + 1, :] * (accf[at, :] + vec[V_OB:V_OB + 1, :])
        hat, _ = norm_parts(row)
        gain = jnp.where(kind == 1, vec[V_FG + 1:V_FG + 2, :], vec[V_FG:V_FG + 1, :])
        shift = jnp.where(kind == 1, vec[V_FB + 1:V_FB + 2, :], vec[V_FB:V_FB + 1, :])
        xall[to, :] = (hat * gain + shift).astype(BF)
        gall[to, :] = (live * vec[V_FS:V_FS + 1, :] * og[at, :].astype(F32)).astype(BF)

    pick = (iota((CAPS, n), 1) == caption_place(res, iota((CAPS, 1), 0))).astype(F32).astype(BF)
    at_img = pl.ds(pl.multiple_of(img, 128), n)
    at_cap = pl.ds(pl.multiple_of(caps, 16), CAPS)
    for i, ref in enumerate((xall, gall)):
        cr[i, at_cap, :] = jnp.dot(pick, ref[at_img, :], preferred_element_type=F32).astype(BF)

    def rows_to(i):
        w = cr.at[:, at_cap, :]
        return remote(w, w, cs.at[1, i], cg_r.at[1, i], p.plane[i][0], p.mp)

    def relay(i):
        q = p.q if i == 3 else p.plane[i][1]
        w = cr.at[:, pl.ds(pl.multiple_of(p.mp * 4 * CAPS + q * CAPS, 16), CAPS), :]
        return remote(w, w, bs.at[i], br.at[i], p.dp, p.other)

    for i in range(3):
        rows_to(i).start()
    relay(3).start()

    @pl.loop(0, n // CHUNK)
    def _(r):
        base = pl.multiple_of(r * CHUNK, CHUNK)
        to = pl.ds(pl.multiple_of(img + base, 128), CHUNK)
        vis = (kind_of(res, iota((CHUNK, 1), 0) + base)[0] == 1).astype(F32)
        gall[to, :] = (gall[to, :].astype(F32) * vis).astype(BF)

    pairs = []
    for i, ref in enumerate((xall, gall)):
        w = ref.at[at_img, :]
        pairs.append(remote(w, w, ps.at[i], pr.at[i], p.dp, p.other))
        pairs[-1].start()
    ag.tick(6)
    accf[...] = jnp.zeros(accf.shape, F32)
    accb[...] = jnp.zeros(accb.shape, F32)
    ubg[...] = jnp.zeros(ubg.shape, F32)
    for c in pairs:
        c.wait()
    for src, dst in ((xall, xt), (gall, gt)):
        @pl.loop(0, 2 * n // CHUNK)
        def _(r):
            at = pl.ds(pl.multiple_of(r * CHUNK, CHUNK), CHUNK)
            dst[:, at] = src[at, :].T

    for i in range(3):
        rows_to(i).wait()
        relay(i).start()
    ag.tick(7)
    ck = ag.ck

    def saved(c):
        return pltpu.make_async_copy(stage, grads.at[:, :, c * ck:(c + 1) * ck], lsem.at[2])

    def gelu_pair(v, dh):
        cdf = 0.5 * (1.0 + lax.erf(v * (0.5 ** 0.5)))
        slope = cdf + v * (jnp.exp(v * v * -0.5) * 0.3989422804014327)
        return (v * cdf).astype(BF), (dh * slope).astype(BF)

    def rows_step(c, at):
        here = slice(c * ck, (c + 1) * ck)
        up, down = g[0, :, here], g[1, :, here]
        v = jnp.dot(xall[at, :], up, preferred_element_type=F32) + up_bias[1:2, here]
        dh = jnp.dot(gall[at, :], down, preferred_element_type=F32)
        h_low, d_low = gelu_pair(v, dh)
        hid[at, :] = h_low
        dpre[at, :] = d_low
        accf[at, :] += lax.dot_general(h_low, down, NT, preferred_element_type=F32)
        accb[at, :] += lax.dot_general(d_low, up, NT, preferred_element_type=F32)
        ubg[1:2, here] += colsum(d_low.astype(F32))

    quarter = wc.shape[2]
    my_cols = pl.ds(pl.multiple_of(p.q * quarter, 128), quarter)
    cap_all = 4 * CAPS

    def caption_pair():
        w = pc.at[:, pl.ds(pl.multiple_of(p.other * cap_all, 16), cap_all), :]
        return remote(w, prc, ps.at[4], pr.at[4], p.dp, p.other)

    def caption_flat(i):
        dev, q = p.plane[i]
        w = pc.at[:, pl.ds(pl.multiple_of(p.mp * cap_all + q * CAPS, 16), CAPS), :]
        return remote(w, prq.at[i], cs.at[2, i], cg_r.at[2, i], dev, p.mp)

    def captions():
        for i in range(4):
            relay(i).wait()

        @pl.loop(0, 5)
        def _(r):
            at = pl.ds(pl.multiple_of(r * CHUNK, CHUNK), CHUNK)
            for i in range(2):
                crt[i, :, at] = cr[i, at, :].T

        @pl.loop(0, 2)
        def _(r):
            at = pl.ds(pl.multiple_of(r * cap_all, 16), cap_all)
            v = jnp.dot(cr[0, at, :], wc[0], preferred_element_type=F32) + up_bias[0:1, my_cols]
            dh = jnp.dot(cr[1, at, :], wc[1], preferred_element_type=F32)
            h_low, d_low = gelu_pair(v, dh)
            chid[at, :] = h_low
            cdpre[at, :] = d_low
            pc[0, at, :] = lax.dot_general(h_low, wc[1], NT, preferred_element_type=F32).astype(BF)
            pc[1, at, :] = lax.dot_general(d_low, wc[0], NT, preferred_element_type=F32).astype(BF)
            ubg[0:1, my_cols] += colsum(d_low.astype(F32))

        caption_pair().start()

        @pl.loop(0, width // 256)
        def _(r):
            at = pl.ds(pl.multiple_of(r * 256, 256), 256)
            cgrads[0, at, :] = jnp.dot(
                crt[0, at, :], cdpre[...], preferred_element_type=F32
            ).astype(BF)
            cgrads[1, at, :] = jnp.dot(
                crt[1, at, :], chid[...], preferred_element_type=F32
            ).astype(BF)

        caption_pair().wait()

        @pl.loop(0, 4)
        def _(r):
            at = pl.ds(pl.multiple_of(p.mp * cap_all + r * CAPS, 16), CAPS)
            got = pl.ds(pl.multiple_of(r * CAPS, 16), CAPS)
            for i in range(2):
                pc[i, at, :] = (pc[i, at, :].astype(F32) + prc[i, got, :].astype(F32)).astype(BF)

        for i in range(3):
            caption_flat(i).start()

    back_pairs = []
    for c in range(C):
        ag.arrived(c)

        @pl.loop(0, 2 * n // 256)
        def _(r):
            rows_step(c, pl.ds(pl.multiple_of(r * 256, 256), 256))

        if c == 0:
            ag.tick(8)
        if c == C - 1:
            theirs_img = pl.ds(pl.multiple_of(p.other * n, 128), n)
            for i, (acc, low) in enumerate(((accf, xall), (accb, gall))):
                @pl.loop(0, 2 * n // CHUNK)
                def _(r):
                    at = pl.ds(pl.multiple_of(r * CHUNK, CHUNK), CHUNK)
                    low[at, :] = acc[at, :].astype(BF)

                to = rcv.at[i]
                back_pairs.append(
                    remote(low.at[theirs_img, :], to, ps.at[2 + i], pr.at[2 + i], p.dp, p.other)
                )
                back_pairs[-1].start()
        if c > 0:
            saved(c - 1).wait()

        @pl.loop(0, width // 256)
        def _(r):
            at = pl.ds(pl.multiple_of(r * 256, 256), 256)
            stage[0, at, :] = jnp.dot(xt[at, :], dpre[...], preferred_element_type=F32).astype(BF)
            stage[1, at, :] = jnp.dot(gt[at, :], hid[...], preferred_element_type=F32).astype(BF)

        saved(c).start()
        if c == 0:
            ag.forward(3, C - 1)
            captions()
    ub[...] = jnp.zeros(ub.shape, F32)
    for e in range(2):
        for j in range(2):
            ub[pl.ds(e * 4 + p.mp * 2 + j, 1), :] = ubg[e:e + 1, j * width:(j + 1) * width]
    for c in back_pairs:
        c.wait()
    for i in range(3):
        caption_flat(i).wait()
    for i, (low, out) in enumerate(((xall, fsum), (gall, bsum))):
        @pl.loop(0, n // CHUNK)
        def _(r):
            base = r * CHUNK
            at = pl.ds(pl.multiple_of(base, CHUNK), CHUNK)
            own = low[pl.ds(pl.multiple_of(img + base, CHUNK), CHUNK), :].astype(F32)
            out[at, :] = (own + rcv[i, at, :].astype(F32)).astype(BF)

        own = pc[i, at_cap, :].astype(F32)
        for j in range(3):
            own = own + prq[j, i].astype(F32)
        out[n:, :] = own.astype(BF)
    saved(C - 1).wait()
    for k in range(4):
        for c in range(C):
            ag.finish(k, c)
    capg.finish()


def front(res, small, up_bias, x, og, wqkv, wout, up, down, C=3):
    n, width = x.shape
    _, rows, hid = up.shape
    ck = hid // C
    sds = jax.ShapeDtypeStruct
    wide = 2 * n
    quarter = hid // 4
    caps = 8 * CAPS
    return pl.pallas_call(
        functools.partial(front_kernel, C),
        out_shape=(
            sds((n, 3 * width), BF),
            sds((n, width), BF),
            sds((n, width), BF),
            sds((16, width), F32),
            sds((8, width), F32),
            sds((n + CAPS, width), BF),
            sds((n + CAPS, width), BF),
            sds((2, rows * 16, quarter), BF),
            sds((2, rows * 16, hid), BF),
        ),
        in_specs=[SM] + [VM] * 14 + [ANY, ANY],
        out_specs=(VM,) * 8 + (ANY,),
        scratch_shapes=[
            pltpu.VMEM((2, rows * 16, hid), BF),
            pltpu.VMEM((2, rows * 16, quarter), BF),
            pltpu.VMEM((2, rows, hid), BF),
            pltpu.VMEM((n, n), F32),
            pltpu.VMEM((1, 3 * width), F32),
            pltpu.VMEM((wide, width), BF),
            pltpu.VMEM((wide, width), BF),
            pltpu.VMEM((width, wide), BF),
            pltpu.VMEM((width, wide), BF),
            pltpu.VMEM((2, caps, width), BF),
            pltpu.VMEM((2, width, caps), BF),
            pltpu.VMEM((wide, width), F32),
            pltpu.VMEM((wide, width), F32),
            pltpu.VMEM((2, n, width), BF),
            pltpu.VMEM((2, rows * 16, ck), BF),
            pltpu.VMEM((wide, ck), BF),
            pltpu.VMEM((wide, ck), BF),
            pltpu.VMEM((2, hid), F32),
            pltpu.VMEM((caps, quarter), BF),
            pltpu.VMEM((caps, quarter), BF),
            pltpu.VMEM((2, caps, width), BF),
            pltpu.VMEM((2, caps // 2, width), BF),
            pltpu.VMEM((3, 2, CAPS, width), BF),
            DMA((5,)), DMA((6, C, 4)), DMA((6, C, 4)), DMA((5,)), DMA((5,)),
            DMA((3, 3)), DMA((3, 3)), DMA((2, 4)), DMA((4,)), DMA((4,)), DMA((4,)),
        ],
        compiler_params=pltpu.CompilerParams(
            collective_id=0, has_side_effects=True, vmem_limit_bytes=67043328
        ),
        name="front",
    )(res, *small, up_bias, x, og, wqkv, wout, up, down)


def back_kernel(
    C, res_ref, vec, ub, x, og, fsum, bsum, proj_h, mixed_h, wout, cgrads_h, grads_h,
    out_up, out_down, block, d_proj, d_branch, d_after, vsum,
    g, bx, by, bdx, bdy, bzu, bzd, cg, cbu, cbd, cgot, proj, mixed, capf, branch, d_mixed, bias,
    lsem, ss, sr, cps, cpr, czs, czr,
):
    p = Place()
    n, width = x.shape
    res = res_ref[0]
    loads = load_all([(grads_h, g), (proj_h, proj), (mixed_h, mixed), (cgrads_h, cg)], lsem)
    p.barrier()

    def write(c, v):
        at = pl.ds(pl.multiple_of(c * (g.shape[2] // C), 128), g.shape[2] // C)
        out_up[1, :, at] = v[0]
        out_down[1, :, at] = v[1]

    def caption_out(q, up, down):
        quarter = cg.shape[2]
        at = pl.ds(pl.multiple_of(q * quarter, 128), quarter)
        out_up[0, :, at] = up
        out_down[0, :, at] = down

    rs = RS(p, g, (bx, by, bdx, bdy, bzu, bzd), ss, sr, C, write)
    cap = CaptionScatter(p, cg, cbu, cbd, cgot, cps, cpr, czs, czr, caption_out)
    loads[0].wait()
    rs.tick(0)
    loads[3].wait()
    cap.step(3)
    loads[1].wait()
    loads[2].wait()
    fill_bias(res, bias)
    half = 256

    @pl.loop(0, width // half)
    def _(j):
        at = pl.ds(pl.multiple_of(j * half, 128), half)
        branch[:, at] = jnp.dot(mixed[...], wout[:, at], preferred_element_type=F32)

    vsum[...] = jnp.zeros(vsum.shape, F32)
    vsum[G_UB:G_UB + 8, :] = ub[...]
    pad = jnp.zeros((128 - CAPS, width), BF)
    for i, ref in enumerate((fsum, bsum)):
        capf[i] = jnp.concatenate([ref[n:, :], pad], axis=0)

    def add(row, v):
        vsum[row:row + 1, :] += colsum(v)

    @pl.loop(0, n // CHUNK)
    def _(r):
        base = pl.multiple_of(r * CHUNK, CHUNK)
        at = pl.ds(base, CHUNK)
        pos = iota((CHUNK, 1), 0) + base
        kind = kind_of(res, pos)[0]
        live = (kind < 2).astype(F32)
        vis = kind == 1
        cap = kind == 0
        pick = (pos == caption_place(res, iota((1, 128), 1))).astype(F32).astype(BF)
        from_cap = jnp.dot(pick, capf[0], preferred_element_type=F32)
        d_cap = jnp.dot(pick, capf[1], preferred_element_type=F32)
        from_img = fsum[at, :].astype(F32)
        d_img = bsum[at, :].astype(F32)
        grad = og[at, :].astype(F32)
        row_branch = branch[at, :] + vec[V_OB:V_OB + 1, :]
        scale = live * vec[V_AS:V_AS + 1, :]
        after = x[at, :].astype(F32) + scale * row_branch
        expert = jnp.where(
            cap, from_cap + vec[V_DB:V_DB + 1, :], from_img + vec[V_DB + 1:V_DB + 2, :]
        ).astype(BF).astype(F32)
        ffn_scale = live * vec[V_FS:V_FS + 1, :]
        block[at, :] = (after + ffn_scale * expert).astype(BF)
        add(G_FS, live * expert * grad)
        d_expert = (ffn_scale * grad).astype(BF).astype(F32)
        add(G_DB, jnp.where(cap, d_expert, 0.0))
        add(G_DB + 1, jnp.where(vis, d_expert, 0.0))
        d_ffn = jnp.where(cap, d_cap, d_img)
        hat, inv = norm_parts(after)
        d_gain = d_ffn * hat
        add(G_FG, jnp.where(cap, d_gain, 0.0))
        add(G_FG + 1, jnp.where(vis, d_gain, 0.0))
        add(G_FB, jnp.where(cap, d_ffn, 0.0))
        add(G_FB + 1, jnp.where(vis, d_ffn, 0.0))
        gain = jnp.where(vis, vec[V_FG + 1:V_FG + 2, :], vec[V_FG:V_FG + 1, :])
        da = grad + norm_back(hat, inv, d_ffn * gain)
        d_after[at, :] = da
        add(G_AS, live * row_branch * da)
        db = (scale * da).astype(BF)
        d_branch[at, :] = db
        add(G_OB, db.astype(F32))

    rs.tick(1)
    cap.step(2)

    @pl.loop(0, width // half)
    def _(j):
        at = pl.ds(pl.multiple_of(j * half, 128), half)
        v = lax.dot_general(d_branch[...], wout[at, :], NT, preferred_element_type=F32)
        d_mixed[:, at] = v.astype(BF)

    ones = [half_mask(0, 1.0), half_mask(1, 1.0)]
    scaled = [half_mask(0, 0.125), half_mask(1, 0.125)]
    first = iota((1, 128), 1) < 64

    @pl.loop(0, width // 128)
    def _(h):
        t = h + 2
        rs.s1(t)
        rs.s2(t - 1)
        rs.s3(t - 2)

        @pl.when(h == 0)
        def _():
            cap.step(1)

        @pl.when(h == 3)
        def _():
            cap.step(0)

        def cols(base):
            return pl.ds(pl.multiple_of(base + h * 128, 128), 128)

        q, k, v = proj[:, cols(0)], proj[:, cols(width)], proj[:, cols(2 * width)]
        do = d_mixed[:, cols(0)]
        q_scaled = q * jnp.full((1, 128), 0.125, BF)
        k_turned = (k.astype(F32) * 0.125).T.astype(BF)
        dq, dk, dv = [], [], []
        for hh in range(2):
            s = lax.dot_general(k * scaled[hh], q, NT, preferred_element_type=F32) + bias[...]
            e = jnp.exp(s - jnp.max(s, axis=0, keepdims=True))
            pt = e * (1.0 / jnp.sum(e, axis=0, keepdims=True))
            dpt = lax.dot_general(v * ones[hh], do, NT, preferred_element_type=F32)
            delta = jnp.sum(pt * dpt, axis=0, keepdims=True)
            dst = (pt * (dpt - delta)).astype(BF)
            dv.append(jnp.dot(pt.astype(BF), do, preferred_element_type=F32))
            dk.append(jnp.dot(dst, q_scaled, preferred_element_type=F32))
            dq.append(jnp.dot(k_turned[64 * hh:64 * hh + 64], dst, preferred_element_type=F32))
        dq_all = jnp.concatenate(dq, axis=0).T.astype(BF)
        dv_all = jnp.where(first, dv[0], dv[1]).astype(BF)
        d_proj[:, cols(0)] = dq_all
        d_proj[:, cols(width)] = jnp.where(first, dk[0], dk[1]).astype(BF)
        d_proj[:, cols(2 * width)] = dv_all
        vsum[G_QB:G_QB + 1, cols(0)] = colsum(dq_all.astype(F32))
        vsum[G_VB:G_VB + 1, cols(0)] = colsum(dv_all.astype(F32))

    rs.tick(4 * C)
    rs.tick(4 * C + 1)
    cap.finish()
    for t in range(4 * C):
        rs.finish(t)


def back(res, vec, ub, x, og, fsum, bsum, proj, mixed, wout, cgrads, grads, C=2):
    quarter = cgrads.shape[2]
    n, width = x.shape
    M, rows, hid = grads.shape[0], grads.shape[1] // 16, grads.shape[2]
    sds = jax.ShapeDtypeStruct
    full = pltpu.VMEM((4, M, rows, hid), BF)
    part = pltpu.VMEM((4, M // 2, rows, hid), BF)
    return pl.pallas_call(
        functools.partial(back_kernel, C),
        out_shape=(
            sds((2, rows, hid), F32),
            sds((2, rows, hid), F32),
            sds((n, width), BF),
            sds((n, 3 * width), BF),
            sds((n, width), BF),
            sds((n, width), F32),
            sds((24, width), F32),
        ),
        in_specs=[SM] + [VM] * 6 + [ANY, ANY, VM, ANY, ANY],
        out_specs=(VM,) * 7,
        scratch_shapes=[
            pltpu.VMEM((M, 16 * rows, hid), BF),
            full, full, part, part, full, full,
            pltpu.VMEM((M, 16 * rows, quarter), BF),
            pltpu.VMEM((4, M, 4 * rows, quarter), BF),
            pltpu.VMEM((4, M, 4 * rows, quarter), BF),
            pltpu.VMEM((3, M, rows, quarter), BF),
            pltpu.VMEM((n, 3 * width), BF),
            pltpu.VMEM((n, width), BF),
            pltpu.VMEM((2, 128, width), BF),
            pltpu.VMEM((n, width), F32),
            pltpu.VMEM((n, width), BF),
            pltpu.VMEM((n, n), F32),
            DMA((4,)), DMA((6, C, 4)), DMA((6, C, 4)), DMA((3,)), DMA((3,)), DMA((2, 4)), DMA((2, 4)),
        ],
        compiler_params=pltpu.CompilerParams(
            collective_id=1, has_side_effects=True, vmem_limit_bytes=63 << 20
        ),
        name="back",
    )(res, vec, ub, x, og, fsum, bsum, proj, mixed, wout, cgrads, grads)


def tail_kernel(
    C, vec, x, activ, mixed, d_proj, d_branch, d_after, wqkv, vin,
    qkv_out, out_out, d_in, vout,
    full, split, got, g, bx, by, bdx, bdy, bzu, bzd, dn, vs, vr,
    ss, sr, ps, pr, vss, vsr,
):
    p = Place()
    n, width = x.shape
    rows = qkv_out.shape[0]
    p.barrier(far=True)

    def pair(j):
        return remote(split.at[p.other, j], got.at[j], ps.at[j], pr.at[j], p.dp, p.other)

    for j in (0, 2, 1, 3):
        if j < 3:
            full[...] = lax.dot_general(
                activ[...], d_proj[:, j * width:(j + 1) * width], TN, preferred_element_type=F32
            )
        else:
            full[...] = lax.dot_general(mixed[...], d_branch[...], TN, preferred_element_type=F32)

        @pl.loop(0, 16)
        def _(o):
            for core in range(2):
                at = pl.ds(pl.multiple_of((2 * o + core) * rows, 8), rows)
                split[core, j, o] = full[at, :].astype(BF)

        pair(j).start()

    def write(c, v):
        if True:
            at = pl.ds(pl.multiple_of(c * width, 128), width)
            qkv_out[:, at] = v[0]

            @pl.when(c == 0)
            def _():
                qkv_out[:, 2 * width:] = v[1]

            @pl.when(c == 1)
            def _():
                out_out[...] = v[1]

    rs = RS(p, g, (bx, by, bdx, bdy, bzu, bzd), ss, sr, C, write)
    for j in (0, 2, 1, 3):
        pair(j).wait()

        @pl.loop(0, 16)
        def _(o):
            v = split[p.mp, j, o].astype(F32) + got[j, o].astype(F32)
            g[j // 2, o, :, (j % 2) * width:(j % 2 + 1) * width] = v.astype(BF)

    rs.tick(0)
    rs.tick(1)
    half = 256
    vs[0] = vin[...]

    @pl.loop(0, width // half)
    def _(j):
        at = pl.ds(pl.multiple_of(j * half, 128), half)
        dn[:, at] = lax.dot_general(d_proj[...], wqkv[at, :], NT, preferred_element_type=F32)

    rs.tick(2)
    rs.tick(3)

    @pl.loop(0, n // CHUNK)
    def _(r):
        at = pl.ds(pl.multiple_of(r * CHUNK, CHUNK), CHUNK)
        hat, inv = norm_parts(x[at, :].astype(F32))
        d = dn[at, :]
        vs[0, G_AG:G_AG + 1, :] += colsum(d * hat)
        vs[0, G_AB:G_AB + 1, :] += colsum(d)
        d_in[at, :] = (d_after[at, :] + norm_back(hat, inv, d * vec[V_AG:V_AG + 1, :])).astype(BF)

    steps = [(p.dp, p.other), (p.xn, p.mp), (p.yn, p.mp), (p.z1, p.mp), (p.z2, p.mp)]

    def hop(i):
        return remote(vs.at[i], vr.at[i], vss.at[i], vsr.at[i], *steps[i])

    hop(0).start()
    for i in range(5):
        rs.tick(4 + i)
        hop(i).wait()
        v = vs[i] + vr[i]
        if i < 4:
            vs[i + 1] = v
            hop(i + 1).start()
        else:
            vout[...] = v
    for t in range(9, 4 * C + 2):
        rs.tick(t)
    for t in range(4 * C):
        rs.finish(t)


def tail(vec, x, activ, mixed, d_proj, d_branch, d_after, wqkv, vsum, C=2):
    n, width = x.shape
    rows = width // 32
    sds = jax.ShapeDtypeStruct
    full = pltpu.VMEM((4, 2, rows, 2 * width), BF)
    part = pltpu.VMEM((4, 1, rows, 2 * width), BF)
    return pl.pallas_call(
        functools.partial(tail_kernel, C),
        out_shape=(
            sds((rows, 3 * width), F32),
            sds((rows, width), F32),
            sds((n, width), BF),
            sds((24, width), F32),
        ),
        in_specs=[VM] * 9,
        out_specs=(VM,) * 4,
        scratch_shapes=[
            pltpu.VMEM((width, width), F32),
            pltpu.VMEM((2, 4, 16, rows, width), BF),
            pltpu.VMEM((4, 16, rows, width), BF),
            pltpu.VMEM((2, 16, rows, 2 * width), BF),
            full, full, part, part, full, full,
            pltpu.VMEM((n, width), F32),
            pltpu.VMEM((5, 24, width), F32),
            pltpu.VMEM((5, 24, width), F32),
            DMA((6, C, 4)), DMA((6, C, 4)), DMA((4,)), DMA((4,)), DMA((5,)), DMA((5,)),
        ],
        compiler_params=pltpu.CompilerParams(
            collective_id=2, has_side_effects=True, vmem_limit_bytes=60 << 20
        ),
        name="tail",
    )(vec, x, activ, mixed, d_proj, d_branch, d_after, wqkv, vsum)


def local_shards(
    layer_input_rows,
    resolution,
    attn_gain,
    attn_bias,
    qkv_weight,
    qv_bias,
    out_weight,
    out_bias,
    attn_scale,
    ffn_scale,
    ffn_gain,
    ffn_bias,
    up_weight,
    up_bias,
    down_weight,
    down_bias,
    output_gradient,
):
    x, og = layer_input_rows, output_gradient
    width = x.shape[1]
    small = (
        attn_gain, attn_bias, qv_bias, out_bias, attn_scale, ffn_scale, ffn_gain, ffn_bias, down_bias
    )
    proj, activ, mixed, vec, ub, fsum, bsum, cgrads, grads = front(
        resolution, small, up_bias, x, og, qkv_weight, out_weight, up_weight, down_weight
    )
    up_weight_grad, down_weight_grad, block_output, d_proj, d_branch, d_after, vsum = back(
        resolution, vec, ub, x, og, fsum, bsum, proj, mixed, out_weight, cgrads, grads
    )
    qkv_out, out_out, input_grad, v = tail(
        vec, x, activ, mixed, d_proj, d_branch, d_after, qkv_weight, vsum
    )
    return (
        block_output,
        input_grad,
        v[G_AG],
        v[G_AB],
        qkv_out,
        v[G_QB:G_QB + 2],
        out_out,
        v[G_OB],
        v[G_AS],
        v[G_FS],
        v[G_FG:G_FG + 2],
        v[G_FB:G_FB + 2],
        up_weight_grad,
        v[G_UB:G_UB + 8].reshape(2, 4 * width),
        down_weight_grad,
        v[G_DB:G_DB + 2],
    )


def solution(mesh):
    placed = (
        P(("dp", "mp"), None),
        P(("dp", "mp")),
        P(),
        P(),
        P(),
        P(),
        P(),
        P(),
        P(),
        P(),
        P(),
        P(),
        P(None, "dp", "mp"),
        P(None, "mp"),
        P(None, "dp", "mp"),
        P(),
        P(("dp", "mp"), None),
    )
    fast = mesh.shape["dp"] == 16 and mesh.shape["mp"] == 2
    return jax.shard_map(
        local_shards if fast else shards,
        mesh=mesh,
        in_specs=placed,
        out_specs=(
            P(("dp", "mp"), None),
            P(("dp", "mp"), None),
            P(),
            P(),
            P(("dp", "mp"), None),
            P(),
            P(("dp", "mp"), None),
            P(),
            P(),
            P(),
            P(),
            P(),
            P(None, "dp", "mp"),
            P(),
            P(None, "dp", "mp"),
            P(),
        ),
        check_vma=False,
    )
```

```python
import functools

import jax
import jax.numpy as jnp
from jax import lax
from jax.experimental import pallas as pl
from jax.experimental.pallas import tpu as pltpu
from jax.sharding import PartitionSpec as P

MESHID = pl.DeviceIdType.MESH
BF = jnp.bfloat16
F32 = jnp.float32

HEADS = 12
PATCH_SMALL = 197
PATCH_LARGE = 577
CAPTION = 40


NORM_EPS = 1e-06
HIGH = lax.Precision.HIGHEST


def layer_norm(field, gain, shift):
    center = field - jnp.mean(field, axis=-1, keepdims=True)
    spread = jnp.mean(center * center, axis=-1, keepdims=True)
    return center * lax.rsqrt(spread + NORM_EPS) * gain + shift


def exact_gelu(field):
    return jax.nn.gelu(field, approximate=False)


def ceil_div(numer, denom):
    return -(-numer // denom)


def slot_layout(res_group, row_count):
    position = jnp.arange(row_count, dtype=jnp.int32)
    small_len = PATCH_SMALL + CAPTION
    large_kind = jnp.where(
        position < PATCH_LARGE, 1, jnp.where(position < PATCH_LARGE + CAPTION, 0, 2)
    )
    large_segment = jnp.where(position < PATCH_LARGE + CAPTION, 0, 2)
    within = position % small_len
    small_kind = jnp.where(position < 2 * small_len, jnp.where(within < PATCH_SMALL, 1, 0), 2)
    small_segment = jnp.where(position < 2 * small_len, position // small_len, 2)
    row_kind = jnp.where(res_group == 1, large_kind, small_kind).astype(jnp.int32)
    segment = jnp.where(res_group == 1, large_segment, small_segment)
    return (row_kind, segment)


def contract_rows(left, right):
    return lax.dot_general(
        left, right, (((0,), (0,)), ((), ())), preferred_element_type=jnp.float32
    )


def contract_cols(left, right):
    return lax.dot_general(
        left, right, (((1,), (1,)), ((), ())), preferred_element_type=jnp.float32
    )


def shards(
    layer_input_rows,
    resolution,
    attn_gain,
    attn_bias,
    qkv_weight,
    qv_bias,
    out_weight,
    out_bias,
    attn_scale,
    ffn_scale,
    ffn_gain,
    ffn_bias,
    up_weight,
    up_bias,
    down_weight,
    down_bias,
    output_gradient,
):
    model_width = layer_input_rows.shape[1]
    slot_count = resolution.shape[0]
    slot_rows = layer_input_rows.shape[0] // slot_count
    head_count = HEADS
    head_width = model_width // head_count
    score_scale = head_width ** (-0.5)
    hidden_part = up_weight.shape[2]
    dp_count = lax.axis_size("dp")
    mp_count = lax.axis_size("mp")
    dp_index = lax.axis_index("dp")
    mp_index = lax.axis_index("mp")
    lang_count = dp_count // 4
    vis_count = dp_count - lang_count
    capacity = max(
        ceil_div(slot_count * PATCH_LARGE, vis_count),
        ceil_div(2 * slot_count * CAPTION, lang_count),
    )
    recv_rows = dp_count * capacity
    kinds, segments = jax.vmap(lambda res_group: slot_layout(res_group, slot_rows))(resolution)
    row_kind = kinds.reshape(-1)
    live_rows = (row_kind != 2).astype(jnp.float32)[:, None]
    vision = (row_kind == 1)[:, None]
    kind_onehot = jnp.stack([row_kind == 0, row_kind == 1], axis=1).astype(jnp.float32)
    rank_vis = jnp.cumsum((row_kind == 1).astype(jnp.int32)) - 1
    rank_txt = jnp.cumsum((row_kind == 0).astype(jnp.int32)) - 1
    target = jnp.where(
        row_kind == 1,
        (rank_vis + dp_index) % vis_count,
        vis_count + (rank_txt + dp_index) % lang_count,
    )
    position = jnp.where(row_kind == 1, rank_vis // vis_count, rank_txt // lang_count)
    slot_index = jnp.where(row_kind == 2, recv_rows, target * capacity + position)

    def to_slots(row_values):
        buffer = (
            jnp.zeros((recv_rows, model_width), row_values.dtype)
            .at[slot_index]
            .set(row_values, mode="drop")
        )
        return buffer.reshape(dp_count, capacity, model_width)

    def from_slots(buffer):
        return jnp.take(
            buffer.reshape(recv_rows, model_width), slot_index, axis=0, mode="fill", fill_value=0
        )

    my_expert = jnp.where(dp_index < vis_count, 1, 0)
    full_up, full_down = (
        lax.all_gather(up_weight, "dp", axis=1, tiled=True),
        lax.all_gather(down_weight, "dp", axis=1, tiled=True),
    )
    own_up = jnp.where(my_expert == 1, full_up[1], full_up[0])
    own_down = jnp.where(my_expert == 1, full_down[1], full_down[0])
    own_up_bias = jnp.where(my_expert == 1, up_bias[1], up_bias[0])
    own_down_bias = jnp.where(my_expert == 1, down_bias[1], down_bias[0])
    x_float = layer_input_rows.astype(jnp.float32)
    normed, norm_pull = jax.vjp(layer_norm, x_float, attn_gain, attn_bias)
    activ = normed.astype(jnp.bfloat16)
    projected = jnp.dot(activ, qkv_weight, preferred_element_type=jnp.float32)
    query = (projected[:, :model_width] + qv_bias[0]).astype(jnp.bfloat16)
    keys = projected[:, model_width : 2 * model_width].astype(jnp.bfloat16)
    values = (projected[:, 2 * model_width :] + qv_bias[1]).astype(jnp.bfloat16)
    query_slots = query.reshape(slot_count, slot_rows, head_count, head_width)
    key_slots = keys.reshape(slot_count, slot_rows, head_count, head_width)
    value_slots = values.reshape(slot_count, slot_rows, head_count, head_width)

    def slot_scores(query_heads, key_heads, segment):
        raw_scores = (
            jnp.einsum("qhd,khd->hqk", query_heads, key_heads, preferred_element_type=jnp.float32)
            * score_scale
        )
        same_seq = (segment[:, None] == segment[None, :])[None]
        return jnp.where(same_seq, raw_scores, -1000000000.0)

    def attend(block_item):
        query_heads, key_heads, value_heads, segment = block_item
        masked = slot_scores(query_heads, key_heads, segment)
        row_max = jnp.max(masked, axis=-1, keepdims=True)
        weights_exp = jnp.exp(masked - row_max)
        row_total = jnp.sum(weights_exp, axis=-1, keepdims=True)
        attn_probs = (weights_exp / row_total).astype(jnp.bfloat16)
        attn_mixed = jnp.einsum(
            "hqk,khd->qhd", attn_probs, value_heads, preferred_element_type=jnp.float32
        )
        log_total = (row_max + jnp.log(row_total))[..., 0]
        return (attn_mixed.reshape(slot_rows, model_width).astype(jnp.bfloat16), log_total)

    attn_mixed, log_totals = lax.map(attend, (query_slots, key_slots, value_slots, segments))
    attn_mixed = attn_mixed.reshape(-1, model_width)
    branch = jnp.dot(attn_mixed, out_weight, preferred_element_type=jnp.float32) + out_bias
    after_attn = x_float + live_rows * attn_scale * branch
    gain_rows = jnp.where(vision, ffn_gain[1], ffn_gain[0])
    shift_rows = jnp.where(vision, ffn_bias[1], ffn_bias[0])
    ffn_normed, norm2_pull = jax.vjp(layer_norm, after_attn, gain_rows, shift_rows)
    sent_rows = ffn_normed.astype(jnp.bfloat16)
    arrived = lax.all_to_all(
        to_slots(sent_rows), "dp", split_axis=0, concat_axis=0, tiled=True
    ).reshape(recv_rows, model_width)
    paired = lax.all_gather(arrived, "mp", axis=0, tiled=True)
    preact = jnp.dot(paired, own_up, preferred_element_type=jnp.float32) + own_up_bias
    hidden, gelu_pull = jax.vjp(exact_gelu, preact)
    hidden_low = hidden.astype(jnp.bfloat16)
    partial_out = contract_cols(hidden_low, own_down)
    expert_sum = (
        lax.psum_scatter(
            partial_out.astype(jnp.bfloat16), "mp", scatter_dimension=0, tiled=True
        ).astype(jnp.float32)
        + own_down_bias
    )
    returned = lax.all_to_all(
        expert_sum.astype(jnp.bfloat16).reshape(dp_count, capacity, model_width),
        "dp",
        split_axis=0,
        concat_axis=0,
        tiled=True,
    )
    expert_rows = from_slots(returned).astype(jnp.float32)
    block_output = (after_attn + live_rows * ffn_scale * expert_rows).astype(jnp.bfloat16)
    grad_float = output_gradient.astype(jnp.float32)
    d_expert = (live_rows * ffn_scale * grad_float).astype(jnp.bfloat16)
    ffn_scale_grad = jnp.sum(live_rows * expert_rows * grad_float, axis=0)
    down_bias_grad = jnp.dot(kind_onehot.T, d_expert.astype(jnp.float32), precision=HIGH)
    arrived_grad = lax.all_to_all(
        to_slots(d_expert), "dp", split_axis=0, concat_axis=0, tiled=True
    ).reshape(recv_rows, model_width)
    paired_grad = lax.all_gather(arrived_grad, "mp", axis=0, tiled=True)
    d_hidden = jnp.dot(paired_grad, own_down, preferred_element_type=jnp.float32)
    d_preact = gelu_pull(d_hidden)[0].astype(jnp.bfloat16)
    own_down_grad = contract_rows(paired_grad, hidden_low)
    own_up_grad = contract_rows(paired, d_preact)
    own_bias_grad = jnp.sum(d_preact.astype(jnp.float32), axis=0)
    d_normed_part = contract_cols(d_preact, own_up)
    d_normed = lax.psum_scatter(
        d_normed_part.astype(jnp.bfloat16), "mp", scatter_dimension=0, tiled=True
    )
    back_grad = lax.all_to_all(
        d_normed.reshape(dp_count, capacity, model_width),
        "dp",
        split_axis=0,
        concat_axis=0,
        tiled=True,
    )
    d_ffn_normed = from_slots(back_grad).astype(jnp.float32)
    d_after_part, gain_grad_rows, shift_grad_rows = norm2_pull(d_ffn_normed)
    ffn_gain_grad = jnp.dot(kind_onehot.T, gain_grad_rows, precision=HIGH)
    ffn_bias_grad = jnp.dot(kind_onehot.T, shift_grad_rows, precision=HIGH)
    d_after = grad_float + d_after_part
    d_branch = (live_rows * attn_scale * d_after).astype(jnp.bfloat16)
    attn_scale_grad = jnp.sum(live_rows * branch * d_after, axis=0)
    out_bias_grad = jnp.sum(d_branch.astype(jnp.float32), axis=0)
    out_weight_grad = contract_rows(attn_mixed, d_branch)
    d_mixed = contract_cols(d_branch, out_weight).astype(jnp.bfloat16)
    d_mixed_slots = d_mixed.reshape(slot_count, slot_rows, head_count, head_width)

    def attend_back(block_item):
        query_heads, key_heads, value_heads, segment, log_total, d_heads = block_item
        masked = slot_scores(query_heads, key_heads, segment)
        probs_full = jnp.exp(masked - log_total[..., None])
        d_probs = jnp.einsum(
            "qhd,khd->hqk", d_heads, value_heads, preferred_element_type=jnp.float32
        )
        row_delta = jnp.sum(probs_full * d_probs, axis=-1, keepdims=True)
        d_scores = (probs_full * (d_probs - row_delta)).astype(jnp.bfloat16)
        probs_low = probs_full.astype(jnp.bfloat16)
        grad_value = jnp.einsum(
            "hqk,qhd->khd", probs_low, d_heads, preferred_element_type=jnp.float32
        )
        grad_query = (
            jnp.einsum("hqk,khd->qhd", d_scores, key_heads, preferred_element_type=jnp.float32)
            * score_scale
        )
        grad_key = (
            jnp.einsum("hqk,qhd->khd", d_scores, query_heads, preferred_element_type=jnp.float32)
            * score_scale
        )
        joined = jnp.concatenate(
            [
                grad_query.reshape(slot_rows, model_width),
                grad_key.reshape(slot_rows, model_width),
                grad_value.reshape(slot_rows, model_width),
            ],
            axis=1,
        )
        return joined.astype(jnp.bfloat16)

    d_projected = lax.map(
        attend_back, (query_slots, key_slots, value_slots, segments, log_totals, d_mixed_slots)
    ).reshape(-1, 3 * model_width)
    qkv_weight_grad = contract_rows(activ, d_projected)
    d_proj_float = d_projected.astype(jnp.float32)
    qv_bias_grad = jnp.stack(
        [
            jnp.sum(d_proj_float[:, :model_width], axis=0),
            jnp.sum(d_proj_float[:, 2 * model_width :], axis=0),
        ]
    )
    d_attn_normed = contract_cols(d_projected, qkv_weight)
    d_input_part, attn_gain_grad, attn_bias_grad = norm_pull(d_attn_normed)
    input_grad = (d_after + d_input_part).astype(jnp.bfloat16)
    expert_pick = (jnp.arange(2) == my_expert).astype(jnp.float32)[:, None, None]
    up_weight_grad, down_weight_grad = (
        lax.psum_scatter(expert_pick * own_up_grad[None], "dp", scatter_dimension=1, tiled=True),
        lax.psum_scatter(expert_pick * own_down_grad[None], "dp", scatter_dimension=1, tiled=True),
    )
    up_bias_full = (
        jnp.zeros((2, mp_count, hidden_part), jnp.float32)
        .at[my_expert, mp_index]
        .set(own_bias_grad)
        .reshape(2, mp_count * hidden_part)
    )
    vector_sums = lax.psum(
        (
            attn_gain_grad,
            attn_bias_grad,
            qv_bias_grad,
            out_bias_grad,
            attn_scale_grad,
            ffn_scale_grad,
            ffn_gain_grad,
            ffn_bias_grad,
            up_bias_full,
            down_bias_grad,
        ),
        ("dp", "mp"),
    )
    matrix_sums = (
        lax.psum_scatter(qkv_weight_grad, ("dp", "mp"), scatter_dimension=0, tiled=True),
        lax.psum_scatter(out_weight_grad, ("dp", "mp"), scatter_dimension=0, tiled=True),
    )
    return (
        block_output,
        input_grad,
        vector_sums[0],
        vector_sums[1],
        matrix_sums[0],
        vector_sums[2],
        matrix_sums[1],
        vector_sums[3],
        vector_sums[4],
        vector_sums[5],
        vector_sums[6],
        vector_sums[7],
        up_weight_grad,
        vector_sums[8],
        down_weight_grad,
        vector_sums[9],
    )


NT = (((1,), (1,)), ((), ()))
TN = (((0,), (0,)), ((), ()))
SMALL = PATCH_SMALL + CAPTION
CAPS = 2 * CAPTION
ANY = pl.BlockSpec(memory_space=pl.ANY)
VM = pl.BlockSpec(memory_space=pltpu.VMEM)
SM = pl.BlockSpec(memory_space=pltpu.SMEM)
DMA = pltpu.SemaphoreType.DMA
CHUNK = 128
V_AG, V_AB, V_QB, V_VB, V_OB, V_AS, V_FS, V_FG, V_FB, V_DB = 0, 1, 2, 3, 4, 5, 6, 7, 9, 11
G_AG, G_AB, G_QB, G_VB, G_OB, G_AS, G_FS, G_FG, G_FB, G_DB, G_UB = 0, 1, 2, 3, 4, 5, 6, 7, 9, 11, 16


def kind_of(res, pos):
    one = lambda c: c.astype(jnp.int32)
    big_seg = 2 * one(pos >= PATCH_LARGE + CAPTION)
    big_kind = 1 - one(pos >= PATCH_LARGE) + big_seg
    small_seg = one(pos >= SMALL) + one(pos >= 2 * SMALL)
    small_pad = one(pos >= 2 * SMALL)
    within = pos - SMALL * small_seg
    small_kind = (1 - small_pad) * one(within < PATCH_SMALL) + 2 * small_pad
    return (
        res * big_kind + (1 - res) * small_kind,
        res * big_seg + (1 - res) * small_seg,
    )


def caption_place(res, slot):
    late = (slot >= CAPTION).astype(jnp.int32)
    big = (1 - late) * (PATCH_LARGE + slot) - late
    small = PATCH_SMALL + slot + late * (SMALL - CAPTION)
    none = (slot >= CAPS).astype(jnp.int32)
    place = res * big + (1 - res) * small
    return (1 - none) * place - none


def iota(shape, dim):
    return lax.broadcasted_iota(jnp.int32, shape, dim)


def fill_bias(res, bias):
    n = bias.shape[0]
    across = kind_of(res, iota((1, n), 1))[1]

    @pl.loop(0, n // CHUNK)
    def _(r):
        base = pl.multiple_of(r * CHUNK, CHUNK)
        down = kind_of(res, iota((CHUNK, 1), 0) + base)[1]
        bias[pl.ds(base, CHUNK), :] = jnp.where(down == across, 0.0, -1000000000.0)


def norm_parts(v):
    center = v - jnp.mean(v, axis=-1, keepdims=True)
    inv = lax.rsqrt(jnp.mean(center * center, axis=-1, keepdims=True) + NORM_EPS)
    return center * inv, inv


def norm_back(xhat, inv, d_hat):
    mean_d = jnp.mean(d_hat, axis=-1, keepdims=True)
    mean_dx = jnp.mean(d_hat * xhat, axis=-1, keepdims=True)
    return inv * (d_hat - mean_d - xhat * mean_dx)


def half_mask(hh, scale):
    lane = iota((1, 128), 1)
    inside = (lane < 64) if hh == 0 else (lane >= 64)
    return jnp.where(inside, scale, 0.0).astype(BF)


def colsum(v):
    return jnp.sum(v, axis=0, keepdims=True)


def dyn_unit(z, k):
    m = k // 2
    zz = z + (z // 2) * (3 - 2 * z)
    u = (1 - m) * (zz + k - 2 * k * zz) + m * k
    w = z // 2
    return u + w * (3 - 2 * u)


class Place:
    def __init__(s):
        s.dp, s.mp = lax.axis_index("dp"), lax.axis_index("mp")
        s.z = s.dp // 4
        s.y = (s.dp // 2) % 2
        s.x = s.dp % 2
        s.xn = s.dp + 1 - 2 * s.x
        s.yn = s.dp + 2 - 4 * s.y
        s.z1 = s.dp + 4 - 8 * (s.z % 2)
        s.z2 = s.dp + 8 - 16 * (s.z // 2)
        s.other = 1 - s.mp
        s.edge = (s.z == 0) | (s.z == 3)
        s.inner = (s.z > 0) & (s.z < 3)
        s.q = s.y * 2 + s.x
        s.dn = s.dp + 3 - 2 * s.x - 4 * s.y
        s.plane = [
            (s.xn, s.y * 2 + 1 - s.x), (s.yn, 2 - 2 * s.y + s.x), (s.dn, 3 - 2 * s.y - s.x)
        ]

    def barrier(s, far=False):
        bar = pltpu.get_barrier_semaphore()
        dp, z = s.dp, s.z

        def sig(d, m):
            pl.semaphore_signal(bar, inc=1, device_id=(d, m), device_id_type=MESHID)

        sig(s.xn, s.mp)
        sig(s.yn, s.mp)
        sig(dp, s.other)
        sig(s.z2 if far else s.dn, s.mp)

        @pl.when(z > 0)
        def _():
            sig(dp - 4, s.mp)

        @pl.when(z < 3)
        def _():
            sig(dp + 4, s.mp)

        pl.semaphore_wait(bar, 5 + ((z + 1) // 2) % 2)


def remote(src, dst, ss, sr, dev, core):
    return pltpu.make_async_remote_copy(
        src_ref=src, dst_ref=dst, send_sem=ss, recv_sem=sr,
        device_id=(dev, core), device_id_type=MESHID,
    )


class AG:
    def __init__(s, place, g, ss, sr, C):
        s.p, s.g, s.ss, s.sr, s.C = place, g, ss, sr, C
        s.rows, s.hid = g.shape[1] // 16, g.shape[2]
        s.ck = s.hid // C
        s.col = place.y * 2 + place.x

    def cp(s, kind, c, u, owner, dev, half=None):
        h = slice(0, 2) if half is None else slice(half, half + 1)
        at = pl.ds(pl.multiple_of(owner * s.rows, 16), s.rows)
        w = s.g.at[h, at, pl.ds(pl.multiple_of(c * s.ck, 128), s.ck)]
        rk = 0 if kind == 1 else kind
        return remote(w, w, s.ss.at[kind, c, u], s.sr.at[rk, c, u], dev, s.p.mp)

    def send(s, k, c, local):
        p = s.p
        z, dp = p.z, p.dp
        u = dyn_unit(z, k)
        owner = u * 4 + s.col
        if not local:
            s.cp(0, c, u, owner, dp).wait_recv()

        @pl.when((u <= z) & (z < 3))
        def _():
            s.cp(0, c, u, owner, dp + 4).start()

        @pl.when((u >= z) & (z > 0))
        def _():
            s.cp(1, c, u, owner, dp - 4).start()

        s.cp(2, c, u, owner, p.xn).start()
        s.cp(3, c, u, owner, p.yn).start()

    def forward(s, k, c):
        p = s.p
        u = dyn_unit(p.z, k)
        xo = u * 4 + p.y * 2 + 1 - p.x
        yo = u * 4 + 2 - 2 * p.y + p.x
        s.cp(2, c, u, xo, p.dp).wait_recv()
        s.cp(5, c, u, xo, p.yn, half=0).start()
        s.cp(3, c, u, yo, p.dp).wait_recv()
        s.cp(4, c, u, yo, p.xn, half=1).start()

    def by_plane(s, edge, inner, f, c):
        @pl.when(s.p.edge)
        def _():
            for k in edge:
                f(k, c)

        if inner:
            @pl.when(s.p.inner)
            def _():
                for k in inner:
                    f(k, c)

    def tick(s, t):
        m, c = t // s.C, t % s.C
        s.by_plane((1 + m,), ((1, 2), (3,), ())[m], lambda k, c: s.send(k, c, False), c)
        if m == 0:
            s.forward(0, c)
        else:
            s.by_plane((m,), ((), (1, 2), (3,))[m], s.forward, c)

    def last(s, c):
        s.by_plane((3,), (), s.forward, c)

    def arrived(s, c):
        for k in range(4):
            u = dyn_unit(s.p.z, k)
            own = u * 4 + s.col
            s.cp(4, c, u, own, s.p.dp, half=1).wait_recv()
            s.cp(5, c, u, own, s.p.dp, half=0).wait_recv()

    def finish(s, k, c):
        p = s.p
        z, dp = p.z, p.dp
        u = dyn_unit(z, k)
        own = u * 4 + s.col
        s.cp(2, c, u, own, dp).wait_send()
        s.cp(3, c, u, own, dp).wait_send()
        s.cp(4, c, u, own, dp, half=1).wait_send()
        s.cp(5, c, u, own, dp, half=0).wait_send()

        @pl.when((u <= z) & (z < 3))
        def _():
            s.cp(0, c, u, own, dp).wait_send()

        @pl.when((u >= z) & (z > 0))
        def _():
            s.cp(1, c, u, own, dp).wait_send()


class CaptionGather:
    def __init__(s, place, own, wc, lsem, ps, pr, zs, zr):
        s.p, s.own, s.wc, s.lsem, s.ps, s.pr, s.zs, s.zr = place, own, wc, lsem, ps, pr, zs, zr
        s.rows, s.quarter = own.shape[1], wc.shape[2]
        s.at = pl.ds(pl.multiple_of(place.dp * s.rows, 16), s.rows)

    def part(s, q):
        return s.own.at[:, :, pl.ds(pl.multiple_of(q * s.quarter, 128), s.quarter)]

    def keep(s):
        return pltpu.make_async_copy(s.part(s.p.q), s.wc.at[:, s.at, :], s.lsem)

    def flat(s, i):
        dev, q = s.p.plane[i]
        return remote(s.part(q), s.wc.at[:, s.at, :], s.ps.at[i], s.pr.at[i], dev, s.p.mp)

    def start(s):
        s.keep().start()
        for i in range(3):
            s.flat(i).start()

    def hop(s, kind, u, dev):
        n = 4 * s.rows
        w = s.wc.at[:, pl.ds(pl.multiple_of(u * n, 16), n), :]
        return remote(w, w, s.zs.at[kind, u], s.zr.at[u], dev, s.p.mp)

    def step(s, k):
        z, dp = s.p.z, s.p.dp
        u = dyn_unit(z, k)
        if isinstance(k, int) and k == 0:
            s.keep().wait()
            for i in range(3):
                s.flat(i).wait()
        else:
            s.hop(0, u, dp).wait_recv()

        @pl.when((u <= z) & (z < 3))
        def _():
            s.hop(0, u, dp + 4).start()

        @pl.when((u >= z) & (z > 0))
        def _():
            s.hop(1, u, dp - 4).start()

    def stage(s, m):
        @pl.when(s.p.edge)
        def _():
            s.step(m)

        if m < 3:
            @pl.when(s.p.inner)
            def _():
                for k in ((1, 2), (3,))[m - 1]:
                    s.step(k)

    def finish(s):
        z, dp = s.p.z, s.p.dp
        for k in range(4):
            u = dyn_unit(z, k)

            @pl.when((u <= z) & (z < 3))
            def _():
                s.hop(0, u, dp + 4).wait_send()

            @pl.when((u >= z) & (z > 0))
            def _():
                s.hop(1, u, dp - 4).wait_send()


class CaptionScatter:
    def __init__(s, place, g, bu, bd, got, ps, pr, zs, zr, out):
        s.p, s.g, s.bu, s.bd, s.got, s.out = place, g, bu, bd, got, out
        s.ps, s.pr, s.zs, s.zr = ps, pr, zs, zr
        s.rows = g.shape[1] // 16

    def win(s, u):
        n = 4 * s.rows
        return s.g.at[:, pl.ds(pl.multiple_of(u * n, 16), n), :]

    def up(s, u):
        return remote(s.win(u), s.bu.at[u], s.zs.at[0, u], s.zr.at[0, u], s.p.dp + 4, s.p.mp)

    def down(s, u):
        return remote(s.win(u), s.bd.at[u], s.zs.at[1, u], s.zr.at[1, u], s.p.dp - 4, s.p.mp)

    def owner(s, q):
        at = pl.multiple_of((s.p.z * 4 + q) * s.rows, 16)
        return s.g.at[:, pl.ds(at, s.rows), :]

    def flat(s, i):
        dev, q = s.p.plane[i]
        return remote(s.owner(q), s.got.at[i], s.ps.at[i], s.pr.at[i], dev, s.p.mp)

    def step(s, k):
        z = s.p.z
        u = dyn_unit(z, k)
        o = s.win(u)

        def go(pred, wu, wd, send):
            @pl.when(pred)
            def _():
                v = o[...].astype(F32)
                if wu:
                    s.up(u).wait_recv()
                    v = v + s.bu.at[u][...].astype(F32)
                if wd:
                    s.down(u).wait_recv()
                    v = v + s.bd.at[u][...].astype(F32)
                if wu or wd:
                    o[...] = v.astype(BF)
                if send is not None:
                    send(u).start()

        if k > 0:
            go((u > z) & (z > 0), True, False, s.up)
            go((u > z) & (z == 0), False, False, s.up)
            go((u < z) & (z < 3), False, True, s.down)
            go((u < z) & (z == 3), False, False, s.down)
        else:
            go(z == 0, False, True, None)
            go(z == 3, True, False, None)
            go((z > 0) & (z < 3), True, True, None)
            for i in range(3):
                s.flat(i).start()

    def stage(s, m):
        if m < 3:
            @pl.when(s.p.edge)
            def _():
                s.step(3 - m)

        if 0 < m < 4:
            @pl.when(s.p.inner)
            def _():
                s.step(4 - m)

        if m == 4:
            s.step(0)

    def finish(s):
        own = s.owner(s.p.q)
        s.out(s.p.q, own[0].astype(F32), own[1].astype(F32))
        for i in range(3):
            s.flat(i).wait()
            s.out(s.p.plane[i][1], s.got[i, 0].astype(F32), s.got[i, 1].astype(F32))
        for k in range(1, 4):
            u = dyn_unit(s.p.z, k)

            @pl.when(u > s.p.z)
            def _():
                s.up(u).wait_send()

            @pl.when(u < s.p.z)
            def _():
                s.down(u).wait_send()


class RS:
    def __init__(s, place, g, bufs, ss, sr, C, write, lags):
        s.p, s.g, s.write, s.lags = place, g, write, lags
        s.bx, s.by, s.bdx, s.bdy, s.bzu, s.bzd = bufs
        s.ss, s.sr, s.C = ss, sr, C
        s.M = g.shape[0]
        s.flat = len(g.shape) == 3
        s.rows = g.shape[1] // 16 if s.flat else g.shape[2]
        s.ck = g.shape[-1] // C
        s.h0 = s.M // 2
        x, y = place.x, place.y
        s.oo = y * 2 + x
        s.ox = y * 2 + 1 - x
        s.oy = 2 - 2 * y + x
        s.od = 3 - 2 * y - x

    def cols(s, c):
        return pl.ds(pl.multiple_of(c * s.ck, 128), s.ck)

    def win(s, u, col, c, lo=0, hi=None):
        hi = s.M if hi is None else hi
        if s.flat:
            at = pl.multiple_of((u * 4 + col) * s.rows, 16)
            return s.g.at[lo:hi, pl.ds(at, s.rows), s.cols(c)]
        return s.g.at[lo:hi, u * 4 + col, :, s.cols(c)]

    def cp(s, kind, u, c, src, dst, dev):
        return remote(src, dst, s.ss.at[kind, c, u], s.sr.at[kind, c, u], dev, s.p.mp)

    def bw(s, b, u, c):
        return b.at[u, :, :, s.cols(c)]

    def c_dy(s, u, c):
        return s.cp(0, u, c, s.win(u, s.od, c, 0, s.h0), s.bw(s.bdy, u, c), s.p.yn)

    def c_dx(s, u, c):
        return s.cp(1, u, c, s.win(u, s.od, c, s.h0), s.bw(s.bdx, u, c), s.p.xn)

    def c_x(s, u, c):
        return s.cp(2, u, c, s.win(u, s.ox, c), s.bw(s.bx, u, c), s.p.xn)

    def c_y(s, u, c):
        return s.cp(3, u, c, s.win(u, s.oy, c), s.bw(s.by, u, c), s.p.yn)

    def c_zu(s, u, c):
        return s.cp(4, u, c, s.win(u, s.oo, c), s.bw(s.bzu, u, c), s.p.dp + 4)

    def c_zd(s, u, c):
        return s.cp(5, u, c, s.win(u, s.oo, c), s.bw(s.bzd, u, c), s.p.dp - 4)

    def item(s, t):
        return dyn_unit(s.p.z, 3 - t // s.C), t % s.C

    def s1(s, t):
        u, c = s.item(t)
        s.c_dy(u, c).start()
        s.c_dx(u, c).start()

    def add(s, dst, src):
        dst[...] = (dst[...].astype(F32) + src[...].astype(F32)).astype(BF)

    def s2(s, t):
        u, c = s.item(t)
        s.c_dy(u, c).wait_recv()
        s.add(s.win(u, s.ox, c, 0, s.h0), s.bw(s.bdy, u, c))
        s.c_x(u, c).start()
        s.c_dx(u, c).wait_recv()
        s.add(s.win(u, s.oy, c, s.h0), s.bw(s.bdx, u, c))
        s.c_y(u, c).start()

    def s3(s, t):
        u, c = s.item(t)
        z = s.p.z
        s.c_x(u, c).wait_recv()
        s.c_y(u, c).wait_recv()
        o = s.win(u, s.oo, c)

        def total(*bufs):
            v = o[...].astype(F32)
            for b in (s.bx, s.by) + bufs:
                v = v + s.bw(b, u, c)[...].astype(F32)
            return v

        def go(pred, wu, wd, send):
            @pl.when(pred)
            def _():
                more = ()
                if wu:
                    s.c_zu(u, c).wait_recv()
                    more += (s.bzu,)
                if wd:
                    s.c_zd(u, c).wait_recv()
                    more += (s.bzd,)
                v = total(*more)
                if send is None:
                    s.write(c, v)
                else:
                    o[...] = v.astype(BF)
                    send(u, c).start()

        up, dn, own = u > z, u < z, u == z
        go(up & (z > 0), True, False, s.c_zu)
        go(up & (z == 0), False, False, s.c_zu)
        go(dn & (z < 3), False, True, s.c_zd)
        go(dn & (z == 3), False, False, s.c_zd)
        go(own & (z == 0), False, True, None)
        go(own & (z == 3), True, False, None)
        go(own & (z > 0) & (z < 3), True, True, None)

    def tick(s, t):
        n = 4 * s.C
        everywhere = s.p.z >= 0
        stages = [
            (lag, f, where)
            for lag, f, where in zip(
                s.lags,
                (s.s1, s.s2, s.s3, s.s3),
                (everywhere, everywhere, s.p.edge, s.p.inner),
            )
            if lag is not None
        ]
        for lag, f, where in stages:
            i = t - lag
            if isinstance(t, int):
                if 0 <= i < n:
                    if where is everywhere:
                        f(i)
                    else:
                        @pl.when(where)
                        def _():
                            f(i)
            else:
                @pl.when((i >= 0) & (i < n) & where)
                def _():
                    f(i)

    def finish(s, t):
        u, c = s.item(t)
        for f in (s.c_dy, s.c_dx, s.c_x, s.c_y):
            f(u, c).wait_send()

        @pl.when(u > s.p.z)
        def _():
            s.c_zu(u, c).wait_send()

        @pl.when(u < s.p.z)
        def _():
            s.c_zd(u, c).wait_send()


def load_all(pairs, sem):
    copies = [pltpu.make_async_copy(a, b, sem.at[i]) for i, (a, b) in enumerate(pairs)]
    for c in copies:
        c.start()
    return copies


def front_kernel(
    C, res_ref, a_gain, a_bias, qv_bias, o_bias, a_scale, f_scale, f_gain, f_bias, dn_bias, up_bias,
    x, og, wqkv, wout, up_ref, down_ref,
    proj, activ, mixed, vec, ub, fsum, bsum, cgrads, grads,
    g, wc, cown, bias, qkvb, xall, gall, xt, gt, cr, crt, accf, accb, rcv, stage, hid, dpre, ubg,
    chid, cdpre, pc, prc, prq,
    lsem, ss, sr, ps, pr, cs, cg_r, zs, zr, bs, br,
):
    p = Place()
    n, width = x.shape
    res = res_ref[0]
    ag = AG(p, g, ss, sr, C)
    mine = pl.ds(pl.multiple_of(p.dp * ag.rows, 16), ag.rows)
    loads = load_all(
        [
            (up_ref.at[1], g.at[0, mine, :]), (down_ref.at[1], g.at[1, mine, :]),
            (up_ref.at[0], cown.at[0]), (down_ref.at[0], cown.at[1]),
        ],
        lsem,
    )
    p.barrier()
    for c in loads:
        c.wait()
    capg = CaptionGather(p, cown, wc, lsem.at[4], cs.at[0], cg_r.at[0], zs, zr)
    capg.start()
    for c in range(C):
        ag.send(0, c, True)

    for row, ref in (
        (V_AG, a_gain), (V_AB, a_bias), (V_OB, o_bias), (V_AS, a_scale), (V_FS, f_scale),
    ):
        vec[row:row + 1, :] = ref[...].reshape(1, width)
    for row, ref in ((V_QB, qv_bias), (V_FG, f_gain), (V_FB, f_bias), (V_DB, dn_bias)):
        vec[row:row + 2, :] = ref[...]
    vec[13:16, :] = jnp.zeros((3, width), F32)

    @pl.loop(0, n // CHUNK)
    def _(r):
        at = pl.ds(pl.multiple_of(r * CHUNK, CHUNK), CHUNK)
        hat, _ = norm_parts(x[at, :].astype(F32))
        activ[at, :] = (hat * vec[V_AG:V_AG + 1, :] + vec[V_AB:V_AB + 1, :]).astype(BF)

    ag.tick(0)
    qkvb[:, :width] = vec[V_QB:V_QB + 1, :]
    qkvb[:, width:2 * width] = jnp.zeros((1, width), F32)
    qkvb[:, 2 * width:] = vec[V_VB:V_VB + 1, :]
    part = 384

    @pl.loop(0, 3 * width // part)
    def _(j):
        at = pl.ds(pl.multiple_of(j * part, 128), part)
        v = jnp.dot(activ[...], wqkv[:, at], preferred_element_type=F32)
        proj[:, at] = (v + qkvb[:, at]).astype(BF)

    ag.tick(1)
    fill_bias(res, bias)
    masks = [half_mask(0, 0.125), half_mask(1, 0.125)]
    first = iota((1, 128), 1) < 64

    @pl.loop(0, width // 128)
    def _(h):
        def cols(base):
            return pl.ds(pl.multiple_of(base + h * 128, 128), 128)

        for i, t in ((1, 2), (3, 3), (4, 4)):
            @pl.when(h == i)
            def _():
                ag.tick(t)

        q, k, v = proj[:, cols(0)], proj[:, cols(width)], proj[:, cols(2 * width)]
        outs = []
        for hh in range(2):
            s = lax.dot_general(q * masks[hh], k, NT, preferred_element_type=F32) + bias[...]
            e = jnp.exp(s - jnp.max(s, axis=-1, keepdims=True))
            pr_low = (e * (1.0 / jnp.sum(e, axis=-1, keepdims=True))).astype(BF)
            outs.append(jnp.dot(pr_low, v, preferred_element_type=F32))
        mixed[:, cols(0)] = jnp.where(first, outs[0], outs[1]).astype(BF)

    ag.tick(5)
    capg.step(0)
    half = 256

    @pl.loop(0, width // half)
    def _(j):
        at = pl.ds(pl.multiple_of(j * half, 128), half)
        accf[:n, at] = jnp.dot(mixed[...], wout[:, at], preferred_element_type=F32)

    ag.tick(6)
    img = p.mp * n
    caps = p.mp * 4 * CAPS + p.q * CAPS

    @pl.loop(0, n // CHUNK)
    def _(r):
        base = pl.multiple_of(r * CHUNK, CHUNK)
        at = pl.ds(base, CHUNK)
        to = pl.ds(pl.multiple_of(img + base, 128), CHUNK)
        kind = kind_of(res, iota((CHUNK, 1), 0) + base)[0]
        live = (kind < 2).astype(F32)
        row = x[at, :].astype(F32)
        row = row + live * vec[V_AS:V_AS + 1, :] * (accf[at, :] + vec[V_OB:V_OB + 1, :])
        hat, _ = norm_parts(row)
        gain = jnp.where(kind == 1, vec[V_FG + 1:V_FG + 2, :], vec[V_FG:V_FG + 1, :])
        shift = jnp.where(kind == 1, vec[V_FB + 1:V_FB + 2, :], vec[V_FB:V_FB + 1, :])
        xall[to, :] = (hat * gain + shift).astype(BF)
        gall[to, :] = (live * vec[V_FS:V_FS + 1, :] * og[at, :].astype(F32)).astype(BF)

    ag.tick(7)
    pick = (iota((CAPS, n), 1) == caption_place(res, iota((CAPS, 1), 0))).astype(F32).astype(BF)
    at_img = pl.ds(pl.multiple_of(img, 128), n)
    at_cap = pl.ds(pl.multiple_of(caps, 16), CAPS)
    for i, ref in enumerate((xall, gall)):
        cr[i, at_cap, :] = jnp.dot(pick, ref[at_img, :], preferred_element_type=F32).astype(BF)

    def rows_to(i):
        w = cr.at[:, at_cap, :]
        return remote(w, w, cs.at[1, i], cg_r.at[1, i], p.plane[i][0], p.mp)

    def relay(i):
        q = p.q if i == 3 else p.plane[i][1]
        w = cr.at[:, pl.ds(pl.multiple_of(p.mp * 4 * CAPS + q * CAPS, 16), CAPS), :]
        return remote(w, w, bs.at[i], br.at[i], p.dp, p.other)

    ag.tick(8)
    for i in range(3):
        rows_to(i).start()
    relay(3).start()

    @pl.loop(0, n // CHUNK)
    def _(r):
        base = pl.multiple_of(r * CHUNK, CHUNK)
        to = pl.ds(pl.multiple_of(img + base, 128), CHUNK)
        vis = (kind_of(res, iota((CHUNK, 1), 0) + base)[0] == 1).astype(F32)
        gall[to, :] = (gall[to, :].astype(F32) * vis).astype(BF)

    pairs = []
    for i, ref in enumerate((xall, gall)):
        w = ref.at[at_img, :]
        pairs.append(remote(w, w, ps.at[i], pr.at[i], p.dp, p.other))
        pairs[-1].start()
    capg.stage(1)
    accf[...] = jnp.zeros(accf.shape, F32)
    accb[...] = jnp.zeros(accb.shape, F32)
    ubg[...] = jnp.zeros(ubg.shape, F32)

    def turn(base):
        @pl.loop(0, n // CHUNK)
        def _(r):
            at = pl.ds(pl.multiple_of(base + r * CHUNK, CHUNK), CHUNK)
            xt[:, at] = xall[at, :].T
            gt[:, at] = gall[at, :].T

    turn(img)
    ag.last(0)
    ag.last(1)
    for c in pairs:
        c.wait()
    turn(p.other * n)
    ag.last(2)
    capg.stage(2)
    ck = ag.ck

    def saved(c):
        return pltpu.make_async_copy(stage, grads.at[:, :, c * ck:(c + 1) * ck], lsem.at[2])

    def gelu_pair(v, dh):
        cdf = 0.5 * (1.0 + lax.erf(v * (0.5 ** 0.5)))
        slope = cdf + v * (jnp.exp(v * v * -0.5) * 0.3989422804014327)
        return (v * cdf).astype(BF), (dh * slope).astype(BF)

    def rows_step(c, at):
        here = slice(c * ck, (c + 1) * ck)
        up, down = g[0, :, here], g[1, :, here]
        v = jnp.dot(xall[at, :], up, preferred_element_type=F32) + up_bias[1:2, here]
        dh = jnp.dot(gall[at, :], down, preferred_element_type=F32)
        h_low, d_low = gelu_pair(v, dh)
        hid[at, :] = h_low
        dpre[at, :] = d_low
        accf[at, :] += lax.dot_general(h_low, down, NT, preferred_element_type=F32)
        accb[at, :] += lax.dot_general(d_low, up, NT, preferred_element_type=F32)
        ubg[1:2, here] += colsum(d_low.astype(F32))

    quarter = wc.shape[2]
    my_cols = pl.ds(pl.multiple_of(p.q * quarter, 128), quarter)
    cap_all = 4 * CAPS

    def caption_pair():
        w = pc.at[:, pl.ds(pl.multiple_of(p.other * cap_all, 16), cap_all), :]
        return remote(w, prc, ps.at[4], pr.at[4], p.dp, p.other)

    def caption_flat(i):
        dev, q = p.plane[i]
        w = pc.at[:, pl.ds(pl.multiple_of(p.mp * cap_all + q * CAPS, 16), CAPS), :]
        return remote(w, prq.at[i], cs.at[2, i], cg_r.at[2, i], dev, p.mp)

    def captions():
        for i in range(4):
            relay(i).wait()

        @pl.loop(0, 5)
        def _(r):
            at = pl.ds(pl.multiple_of(r * CHUNK, CHUNK), CHUNK)
            for i in range(2):
                crt[i, :, at] = cr[i, at, :].T

        @pl.loop(0, 2)
        def _(r):
            at = pl.ds(pl.multiple_of(r * cap_all, 16), cap_all)
            v = jnp.dot(cr[0, at, :], wc[0], preferred_element_type=F32) + up_bias[0:1, my_cols]
            dh = jnp.dot(cr[1, at, :], wc[1], preferred_element_type=F32)
            h_low, d_low = gelu_pair(v, dh)
            chid[at, :] = h_low
            cdpre[at, :] = d_low
            pc[0, at, :] = lax.dot_general(h_low, wc[1], NT, preferred_element_type=F32).astype(BF)
            pc[1, at, :] = lax.dot_general(d_low, wc[0], NT, preferred_element_type=F32).astype(BF)
            ubg[0:1, my_cols] += colsum(d_low.astype(F32))

        caption_pair().start()

        @pl.loop(0, width // 256)
        def _(r):
            at = pl.ds(pl.multiple_of(r * 256, 256), 256)
            cgrads[0, at, :] = jnp.dot(
                crt[0, at, :], cdpre[...], preferred_element_type=F32
            ).astype(BF)
            cgrads[1, at, :] = jnp.dot(
                crt[1, at, :], chid[...], preferred_element_type=F32
            ).astype(BF)

        caption_pair().wait()

        @pl.loop(0, 4)
        def _(r):
            at = pl.ds(pl.multiple_of(p.mp * cap_all + r * CAPS, 16), CAPS)
            got = pl.ds(pl.multiple_of(r * CAPS, 16), CAPS)
            for i in range(2):
                pc[i, at, :] = (pc[i, at, :].astype(F32) + prc[i, got, :].astype(F32)).astype(BF)

        for i in range(3):
            caption_flat(i).start()

    back_pairs = []
    for c in range(C):
        ag.arrived(c)

        @pl.loop(0, 2 * n // 256)
        def _(r):
            rows_step(c, pl.ds(pl.multiple_of(r * 256, 256), 256))

        if c == C - 1:
            theirs_img = pl.ds(pl.multiple_of(p.other * n, 128), n)
            for i, (acc, low) in enumerate(((accf, xall), (accb, gall))):
                @pl.loop(0, 2 * n // CHUNK)
                def _(r):
                    at = pl.ds(pl.multiple_of(r * CHUNK, CHUNK), CHUNK)
                    low[at, :] = acc[at, :].astype(BF)

                to = rcv.at[i]
                back_pairs.append(
                    remote(low.at[theirs_img, :], to, ps.at[2 + i], pr.at[2 + i], p.dp, p.other)
                )
                back_pairs[-1].start()
        if c == 1:
            for i in range(3):
                rows_to(i).wait()
                relay(i).start()
            capg.stage(3)
        if c > 0:
            saved(c - 1).wait()

        @pl.loop(0, width // 256)
        def _(r):
            at = pl.ds(pl.multiple_of(r * 256, 256), 256)
            stage[0, at, :] = jnp.dot(xt[at, :], dpre[...], preferred_element_type=F32).astype(BF)
            stage[1, at, :] = jnp.dot(gt[at, :], hid[...], preferred_element_type=F32).astype(BF)

        saved(c).start()
        if c == 1:
            captions()
    ub[...] = jnp.zeros(ub.shape, F32)
    for e in range(2):
        for j in range(2):
            ub[pl.ds(e * 4 + p.mp * 2 + j, 1), :] = ubg[e:e + 1, j * width:(j + 1) * width]
    for c in back_pairs:
        c.wait()
    for i in range(3):
        caption_flat(i).wait()
    for i, (low, out) in enumerate(((xall, fsum), (gall, bsum))):
        @pl.loop(0, n // CHUNK)
        def _(r):
            base = r * CHUNK
            at = pl.ds(pl.multiple_of(base, CHUNK), CHUNK)
            own = low[pl.ds(pl.multiple_of(img + base, CHUNK), CHUNK), :].astype(F32)
            out[at, :] = (own + rcv[i, at, :].astype(F32)).astype(BF)

        own = pc[i, at_cap, :].astype(F32)
        for j in range(3):
            own = own + prq[j, i].astype(F32)
        out[n:, :] = own.astype(BF)
    saved(C - 1).wait()
    for k in range(4):
        for c in range(C):
            ag.finish(k, c)
    capg.finish()


def front(res, small, up_bias, x, og, wqkv, wout, up, down, C=3):
    n, width = x.shape
    _, rows, hid = up.shape
    ck = hid // C
    sds = jax.ShapeDtypeStruct
    wide = 2 * n
    quarter = hid // 4
    caps = 8 * CAPS
    return pl.pallas_call(
        functools.partial(front_kernel, C),
        out_shape=(
            sds((n, 3 * width), BF),
            sds((n, width), BF),
            sds((n, width), BF),
            sds((16, width), F32),
            sds((8, width), F32),
            sds((n + CAPS, width), BF),
            sds((n + CAPS, width), BF),
            sds((2, rows * 16, quarter), BF),
            sds((2, rows * 16, hid), BF),
        ),
        in_specs=[SM] + [VM] * 14 + [ANY, ANY],
        out_specs=(VM,) * 8 + (ANY,),
        scratch_shapes=[
            pltpu.VMEM((2, rows * 16, hid), BF),
            pltpu.VMEM((2, rows * 16, quarter), BF),
            pltpu.VMEM((2, rows, hid), BF),
            pltpu.VMEM((n, n), F32),
            pltpu.VMEM((1, 3 * width), F32),
            pltpu.VMEM((wide, width), BF),
            pltpu.VMEM((wide, width), BF),
            pltpu.VMEM((width, wide), BF),
            pltpu.VMEM((width, wide), BF),
            pltpu.VMEM((2, caps, width), BF),
            pltpu.VMEM((2, width, caps), BF),
            pltpu.VMEM((wide, width), F32),
            pltpu.VMEM((wide, width), F32),
            pltpu.VMEM((2, n, width), BF),
            pltpu.VMEM((2, rows * 16, ck), BF),
            pltpu.VMEM((wide, ck), BF),
            pltpu.VMEM((wide, ck), BF),
            pltpu.VMEM((2, hid), F32),
            pltpu.VMEM((caps, quarter), BF),
            pltpu.VMEM((caps, quarter), BF),
            pltpu.VMEM((2, caps, width), BF),
            pltpu.VMEM((2, caps // 2, width), BF),
            pltpu.VMEM((3, 2, CAPS, width), BF),
            DMA((5,)), DMA((6, C, 4)), DMA((6, C, 4)), DMA((5,)), DMA((5,)),
            DMA((3, 3)), DMA((3, 3)), DMA((2, 4)), DMA((4,)), DMA((4,)), DMA((4,)),
        ],
        compiler_params=pltpu.CompilerParams(
            collective_id=0, has_side_effects=True, vmem_limit_bytes=67043328
        ),
        name="front",
    )(res, *small, up_bias, x, og, wqkv, wout, up, down)


def back_kernel(
    C, res_ref, vec, ub, x, og, fsum, bsum, proj_h, mixed_h, activ_h, wout, cgrads_h, grads_h,
    out_up, out_down, block, d_proj, d_after, vsum, gq,
    g, bx, by, bdx, bdy, bzu, bzd, cg, cbu, cbd, cgot, proj, mixed, activ, turned, capf, branch, d_mixed, d_branch, bias,
    full, split, got, lsem, ss, sr, cps, cpr, czs, czr, ps, pr,
):
    p = Place()
    n, width = x.shape
    res = res_ref[0]
    loads = load_all(
        [(grads_h, g), (proj_h, proj), (mixed_h, mixed), (cgrads_h, cg), (activ_h, activ)], lsem
    )
    p.barrier()

    def write(c, v):
        at = pl.ds(pl.multiple_of(c * (g.shape[2] // C), 128), g.shape[2] // C)
        out_up[1, :, at] = v[0]
        out_down[1, :, at] = v[1]

    def caption_out(q, up, down):
        quarter = cg.shape[2]
        at = pl.ds(pl.multiple_of(q * quarter, 128), quarter)
        out_up[0, :, at] = up
        out_down[0, :, at] = down

    rs = RS(p, g, (bx, by, bdx, bdy, bzu, bzd), ss, sr, C, write, (0, 2, 4, 5))
    cap = CaptionScatter(p, cg, cbu, cbd, cgot, cps, cpr, czs, czr, caption_out)
    loads[0].wait()
    rs.tick(0)
    loads[3].wait()
    cap.stage(0)
    loads[1].wait()
    loads[2].wait()
    loads[4].wait()
    fill_bias(res, bias)
    half = 256

    @pl.loop(0, width // half)
    def _(j):
        at = pl.ds(pl.multiple_of(j * half, 128), half)
        branch[:, at] = jnp.dot(mixed[...], wout[:, at], preferred_element_type=F32)

    rs.tick(1)
    vsum[...] = jnp.zeros(vsum.shape, F32)
    vsum[G_UB:G_UB + 8, :] = ub[...]
    pad = jnp.zeros((128 - CAPS, width), BF)
    for i, ref in enumerate((fsum, bsum)):
        capf[i] = jnp.concatenate([ref[n:, :], pad], axis=0)

    def add(row, v):
        vsum[row:row + 1, :] += colsum(v)

    @pl.loop(0, n // CHUNK)
    def _(r):
        @pl.when(r == 2)
        def _():
            rs.tick(2)

        base = pl.multiple_of(r * CHUNK, CHUNK)
        at = pl.ds(base, CHUNK)
        for i, ref in enumerate((activ, mixed)):
            turned[i, :, at] = ref[at, :].T
        pos = iota((CHUNK, 1), 0) + base
        kind = kind_of(res, pos)[0]
        live = (kind < 2).astype(F32)
        vis = kind == 1
        cap = kind == 0
        pick = (pos == caption_place(res, iota((1, 128), 1))).astype(F32).astype(BF)
        from_cap = jnp.dot(pick, capf[0], preferred_element_type=F32)
        d_cap = jnp.dot(pick, capf[1], preferred_element_type=F32)
        from_img = fsum[at, :].astype(F32)
        d_img = bsum[at, :].astype(F32)
        grad = og[at, :].astype(F32)
        row_branch = branch[at, :] + vec[V_OB:V_OB + 1, :]
        scale = live * vec[V_AS:V_AS + 1, :]
        after = x[at, :].astype(F32) + scale * row_branch
        expert = jnp.where(
            cap, from_cap + vec[V_DB:V_DB + 1, :], from_img + vec[V_DB + 1:V_DB + 2, :]
        ).astype(BF).astype(F32)
        ffn_scale = live * vec[V_FS:V_FS + 1, :]
        block[at, :] = (after + ffn_scale * expert).astype(BF)
        add(G_FS, live * expert * grad)
        d_expert = (ffn_scale * grad).astype(BF).astype(F32)
        add(G_DB, jnp.where(cap, d_expert, 0.0))
        add(G_DB + 1, jnp.where(vis, d_expert, 0.0))
        d_ffn = jnp.where(cap, d_cap, d_img)
        hat, inv = norm_parts(after)
        d_gain = d_ffn * hat
        add(G_FG, jnp.where(cap, d_gain, 0.0))
        add(G_FG + 1, jnp.where(vis, d_gain, 0.0))
        add(G_FB, jnp.where(cap, d_ffn, 0.0))
        add(G_FB + 1, jnp.where(vis, d_ffn, 0.0))
        gain = jnp.where(vis, vec[V_FG + 1:V_FG + 2, :], vec[V_FG:V_FG + 1, :])
        da = grad + norm_back(hat, inv, d_ffn * gain)
        d_after[at, :] = da
        add(G_AS, live * row_branch * da)
        db = (scale * da).astype(BF)
        d_branch[at, :] = db
        add(G_OB, db.astype(F32))

    rs.tick(3)
    cap.stage(1)
    rows = width // 32

    def pair(j):
        return remote(split.at[p.other, j], got.at[j], ps.at[j], pr.at[j], p.dp, p.other)

    def weight_part(j):
        if j < 3:
            right = d_proj[:, j * width:(j + 1) * width]
        else:
            right = d_branch[...]
        full[...] = jnp.dot(turned[j // 3], right, preferred_element_type=F32)

        @pl.loop(0, 16)
        def _(o):
            for core in range(2):
                at = pl.ds(pl.multiple_of((2 * o + core) * rows, 8), rows)
                split[core, j, o] = full[at, :].astype(BF)

        pair(j).start()

    def weight_sum(j):
        pair(j).wait()

        @pl.loop(0, 16)
        def _(o):
            v = split[p.mp, j, o].astype(F32) + got[j, o].astype(F32)
            gq[j // 2, o, :, (j % 2) * width:(j % 2 + 1) * width] = v.astype(BF)

    @pl.loop(0, width // half)
    def _(j):
        at = pl.ds(pl.multiple_of(j * half, 128), half)
        v = lax.dot_general(d_branch[...], wout[at, :], NT, preferred_element_type=F32)
        d_mixed[:, at] = v.astype(BF)

    rs.tick(4)
    weight_part(3)

    ones = [half_mask(0, 1.0), half_mask(1, 1.0)]
    scaled = [half_mask(0, 0.125), half_mask(1, 0.125)]
    first = iota((1, 128), 1) < 64

    @pl.loop(0, width // 128)
    def _(h):
        rs.tick(5 + h)
        for i, m in ((1, 2), (3, 3)):
            @pl.when(h == i)
            def _():
                cap.stage(m)

        def cols(base):
            return pl.ds(pl.multiple_of(base + h * 128, 128), 128)

        q, k, v = proj[:, cols(0)], proj[:, cols(width)], proj[:, cols(2 * width)]
        do = d_mixed[:, cols(0)]
        q_scaled = q * jnp.full((1, 128), 0.125, BF)
        k_turned = (k.astype(F32) * 0.125).T.astype(BF)
        dq, dk, dv = [], [], []
        for hh in range(2):
            s = lax.dot_general(k * scaled[hh], q, NT, preferred_element_type=F32) + bias[...]
            e = jnp.exp(s - jnp.max(s, axis=0, keepdims=True))
            pt = e * (1.0 / jnp.sum(e, axis=0, keepdims=True))
            dpt = lax.dot_general(v * ones[hh], do, NT, preferred_element_type=F32)
            delta = jnp.sum(pt * dpt, axis=0, keepdims=True)
            dst = (pt * (dpt - delta)).astype(BF)
            dv.append(jnp.dot(pt.astype(BF), do, preferred_element_type=F32))
            dk.append(jnp.dot(dst, q_scaled, preferred_element_type=F32))
            dq.append(jnp.dot(k_turned[64 * hh:64 * hh + 64], dst, preferred_element_type=F32))
        dq_all = jnp.concatenate(dq, axis=0).T.astype(BF)
        dv_all = jnp.where(first, dv[0], dv[1]).astype(BF)
        d_proj[:, cols(0)] = dq_all
        d_proj[:, cols(width)] = jnp.where(first, dk[0], dk[1]).astype(BF)
        d_proj[:, cols(2 * width)] = dv_all
        vsum[G_QB:G_QB + 1, cols(0)] = colsum(dq_all.astype(F32))
        vsum[G_VB:G_VB + 1, cols(0)] = colsum(dv_all.astype(F32))

    rs.tick(11)
    cap.stage(4)
    weight_part(0)
    weight_sum(3)
    rs.tick(12)
    weight_part(1)
    weight_sum(0)
    rs.tick(13)
    weight_part(2)
    weight_sum(1)
    rs.tick(14)
    rs.tick(15)
    rs.tick(16)
    cap.finish()
    weight_sum(2)
    for t in range(4 * C):
        rs.finish(t)


def back(res, vec, ub, x, og, fsum, bsum, proj, mixed, activ, wout, cgrads, grads, C=3):
    quarter = cgrads.shape[2]
    n, width = x.shape
    M, rows, hid = grads.shape[0], grads.shape[1] // 16, grads.shape[2]
    own = width // 32
    sds = jax.ShapeDtypeStruct
    full = pltpu.VMEM((4, M, rows, hid), BF)
    part = pltpu.VMEM((4, M // 2, rows, hid), BF)
    return pl.pallas_call(
        functools.partial(back_kernel, C),
        out_shape=(
            sds((2, rows, hid), F32),
            sds((2, rows, hid), F32),
            sds((n, width), BF),
            sds((n, 3 * width), BF),
            sds((n, width), F32),
            sds((24, width), F32),
            sds((2, 16, own, 2 * width), BF),
        ),
        in_specs=[SM] + [VM] * 6 + [ANY, ANY, ANY, VM, ANY, ANY],
        out_specs=(VM,) * 7,
        scratch_shapes=[
            pltpu.VMEM((M, 16 * rows, hid), BF),
            full, full, part, part, full, full,
            pltpu.VMEM((M, 16 * rows, quarter), BF),
            pltpu.VMEM((4, M, 4 * rows, quarter), BF),
            pltpu.VMEM((4, M, 4 * rows, quarter), BF),
            pltpu.VMEM((3, M, rows, quarter), BF),
            pltpu.VMEM((n, 3 * width), BF),
            pltpu.VMEM((n, width), BF),
            pltpu.VMEM((n, width), BF),
            pltpu.VMEM((2, width, n), BF),
            pltpu.VMEM((2, 128, width), BF),
            pltpu.VMEM((n, width), F32),
            pltpu.VMEM((n, width), BF),
            pltpu.VMEM((n, width), BF),
            pltpu.VMEM((n, n), F32),
            pltpu.VMEM((width, width), F32),
            pltpu.VMEM((2, 4, 16, own, width), BF),
            pltpu.VMEM((4, 16, own, width), BF),
            DMA((5,)), DMA((6, C, 4)), DMA((6, C, 4)), DMA((3,)), DMA((3,)), DMA((2, 4)), DMA((2, 4)),
            DMA((4,)), DMA((4,)),
        ],
        compiler_params=pltpu.CompilerParams(
            collective_id=1, has_side_effects=True, vmem_limit_bytes=63 << 20
        ),
        name="back",
    )(res, vec, ub, x, og, fsum, bsum, proj, mixed, activ, wout, cgrads, grads)


def tail_kernel(
    C, vec, x, d_proj, d_after, wqkv, vin, gq,
    qkv_out, out_out, d_in, vout,
    g, bx, by, bdx, bdy, bzu, bzd, dn, vs, vr, ws, wr, wo,
    lsem, ss, sr, vss, vsr,
):
    p = Place()
    n, width = x.shape
    load = pltpu.make_async_copy(gq, g, lsem)
    load.start()
    p.barrier(far=True)

    def write(c, v):
        at = pl.ds(pl.multiple_of(c * width, 128), width)
        qkv_out[:, at] = v[0]
        if isinstance(c, int):
            if c == 0:
                qkv_out[:, 2 * width:] = v[1]
            else:
                out_out[...] = v[1]
            return

        @pl.when(c == 0)
        def _():
            qkv_out[:, 2 * width:] = v[1]

        @pl.when(c == 1)
        def _():
            out_out[...] = v[1]

    rs = RS(p, g, (bx, by, bdx, bdy, bzu, bzd), ss, sr, C, write, (None, 1, 3, 4))
    steps = [(p.dp, p.other), (p.xn, p.mp), (p.yn, p.mp), (p.z1, p.mp), (p.z2, p.mp)]

    def early(i):
        return remote(vs.at[i], vr.at[i], vss.at[0, i], vsr.at[0, i], *steps[i])

    def late(i):
        return remote(ws.at[i], wr.at[i], vss.at[1, i], vsr.at[1, i], *steps[i])

    def advance(i, hop, sent, got, out):
        hop(i).wait()
        v = sent[i] + got[i]
        if i < 4:
            sent[i + 1] = v
            hop(i + 1).start()
        else:
            out[...] = v

    vs[0] = vin[...]
    ws[0] = jnp.zeros((8, width), F32)
    early(0).start()
    load.wait()
    for t in range(4 * C):
        rs.s1(t)
    third = width // 3
    for j in range(3):
        at = slice(j * third, (j + 1) * third)
        dn[:, at] = lax.dot_general(d_proj[...], wqkv[at, :], NT, preferred_element_type=F32)
        rs.tick(1 + j)
        advance(j, early, vs, vr, vout)

    @pl.loop(0, n // CHUNK)
    def _(r):
        at = pl.ds(pl.multiple_of(r * CHUNK, CHUNK), CHUNK)
        hat, inv = norm_parts(x[at, :].astype(F32))
        d = dn[at, :]
        ws[0, G_AG:G_AG + 1, :] += colsum(d * hat)
        ws[0, G_AB:G_AB + 1, :] += colsum(d)
        d_in[at, :] = (d_after[at, :] + norm_back(hat, inv, d * vec[V_AG:V_AG + 1, :])).astype(BF)

    late(0).start()
    advance(3, early, vs, vr, vout)
    rs.tick(4)
    for i in range(5):
        rs.tick(5 + i)
        if i == 1:
            advance(4, early, vs, vr, vout)
        advance(i, late, ws, wr, wo)
    vout[:2, :] = wo[:2, :]
    for t in range(10, 4 * C + 4):
        rs.tick(t)
    for t in range(4 * C):
        rs.finish(t)


def tail(vec, x, d_proj, d_after, wqkv, vsum, gq, C=2):
    n, width = x.shape
    rows = width // 32
    sds = jax.ShapeDtypeStruct
    full = pltpu.VMEM((4, 2, rows, 2 * width), BF)
    part = pltpu.VMEM((4, 1, rows, 2 * width), BF)
    return pl.pallas_call(
        functools.partial(tail_kernel, C),
        out_shape=(
            sds((rows, 3 * width), F32),
            sds((rows, width), F32),
            sds((n, width), BF),
            sds((24, width), F32),
        ),
        in_specs=[VM] * 6 + [ANY],
        out_specs=(VM,) * 4,
        scratch_shapes=[
            pltpu.VMEM((2, 16, rows, 2 * width), BF),
            full, full, part, part, full, full,
            pltpu.VMEM((n, width), F32),
            pltpu.VMEM((5, 24, width), F32),
            pltpu.VMEM((5, 24, width), F32),
            pltpu.VMEM((5, 8, width), F32),
            pltpu.VMEM((5, 8, width), F32),
            pltpu.VMEM((8, width), F32),
            DMA, DMA((6, C, 4)), DMA((6, C, 4)), DMA((2, 5)), DMA((2, 5)),
        ],
        compiler_params=pltpu.CompilerParams(
            collective_id=2, has_side_effects=True, vmem_limit_bytes=60 << 20
        ),
        name="tail",
    )(vec, x, d_proj, d_after, wqkv, vsum, gq)


def local_shards(
    layer_input_rows,
    resolution,
    attn_gain,
    attn_bias,
    qkv_weight,
    qv_bias,
    out_weight,
    out_bias,
    attn_scale,
    ffn_scale,
    ffn_gain,
    ffn_bias,
    up_weight,
    up_bias,
    down_weight,
    down_bias,
    output_gradient,
):
    x, og = layer_input_rows, output_gradient
    width = x.shape[1]
    small = (
        attn_gain, attn_bias, qv_bias, out_bias, attn_scale, ffn_scale, ffn_gain, ffn_bias, down_bias
    )
    proj, activ, mixed, vec, ub, fsum, bsum, cgrads, grads = front(
        resolution, small, up_bias, x, og, qkv_weight, out_weight, up_weight, down_weight
    )
    up_weight_grad, down_weight_grad, block_output, d_proj, d_after, vsum, gq = back(
        resolution, vec, ub, x, og, fsum, bsum, proj, mixed, activ, out_weight, cgrads, grads
    )
    qkv_out, out_out, input_grad, v = tail(
        vec, x, d_proj, d_after, qkv_weight, vsum, gq
    )
    return (
        block_output,
        input_grad,
        v[G_AG],
        v[G_AB],
        qkv_out,
        v[G_QB:G_QB + 2],
        out_out,
        v[G_OB],
        v[G_AS],
        v[G_FS],
        v[G_FG:G_FG + 2],
        v[G_FB:G_FB + 2],
        up_weight_grad,
        v[G_UB:G_UB + 8].reshape(2, 4 * width),
        down_weight_grad,
        v[G_DB:G_DB + 2],
    )


def solution(mesh):
    placed = (
        P(("dp", "mp"), None),
        P(("dp", "mp")),
        P(),
        P(),
        P(),
        P(),
        P(),
        P(),
        P(),
        P(),
        P(),
        P(),
        P(None, "dp", "mp"),
        P(None, "mp"),
        P(None, "dp", "mp"),
        P(),
        P(("dp", "mp"), None),
    )
    fast = mesh.shape["dp"] == 16 and mesh.shape["mp"] == 2
    return jax.shard_map(
        local_shards if fast else shards,
        mesh=mesh,
        in_specs=placed,
        out_specs=(
            P(("dp", "mp"), None),
            P(("dp", "mp"), None),
            P(),
            P(),
            P(("dp", "mp"), None),
            P(),
            P(("dp", "mp"), None),
            P(),
            P(),
            P(),
            P(),
            P(),
            P(None, "dp", "mp"),
            P(),
            P(None, "dp", "mp"),
            P(),
        ),
        check_vma=False,
    )
```

```python
import functools

import jax
import jax.numpy as jnp
from jax import lax
from jax.experimental import pallas as pl
from jax.experimental.pallas import tpu as pltpu
from jax.sharding import PartitionSpec as P

MESHID = pl.DeviceIdType.MESH
BF = jnp.bfloat16
F32 = jnp.float32

HEADS = 12
PATCH_SMALL = 197
PATCH_LARGE = 577
CAPTION = 40


NORM_EPS = 1e-06
HIGH = lax.Precision.HIGHEST


def layer_norm(field, gain, shift):
    center = field - jnp.mean(field, axis=-1, keepdims=True)
    spread = jnp.mean(center * center, axis=-1, keepdims=True)
    return center * lax.rsqrt(spread + NORM_EPS) * gain + shift


def exact_gelu(field):
    return jax.nn.gelu(field, approximate=False)


def ceil_div(numer, denom):
    return -(-numer // denom)


def slot_layout(res_group, row_count):
    position = jnp.arange(row_count, dtype=jnp.int32)
    small_len = PATCH_SMALL + CAPTION
    large_kind = jnp.where(
        position < PATCH_LARGE, 1, jnp.where(position < PATCH_LARGE + CAPTION, 0, 2)
    )
    large_segment = jnp.where(position < PATCH_LARGE + CAPTION, 0, 2)
    within = position % small_len
    small_kind = jnp.where(position < 2 * small_len, jnp.where(within < PATCH_SMALL, 1, 0), 2)
    small_segment = jnp.where(position < 2 * small_len, position // small_len, 2)
    row_kind = jnp.where(res_group == 1, large_kind, small_kind).astype(jnp.int32)
    segment = jnp.where(res_group == 1, large_segment, small_segment)
    return (row_kind, segment)


def contract_rows(left, right):
    return lax.dot_general(
        left, right, (((0,), (0,)), ((), ())), preferred_element_type=jnp.float32
    )


def contract_cols(left, right):
    return lax.dot_general(
        left, right, (((1,), (1,)), ((), ())), preferred_element_type=jnp.float32
    )


def shards(
    layer_input_rows,
    resolution,
    attn_gain,
    attn_bias,
    qkv_weight,
    qv_bias,
    out_weight,
    out_bias,
    attn_scale,
    ffn_scale,
    ffn_gain,
    ffn_bias,
    up_weight,
    up_bias,
    down_weight,
    down_bias,
    output_gradient,
):
    model_width = layer_input_rows.shape[1]
    slot_count = resolution.shape[0]
    slot_rows = layer_input_rows.shape[0] // slot_count
    head_count = HEADS
    head_width = model_width // head_count
    score_scale = head_width ** (-0.5)
    hidden_part = up_weight.shape[2]
    dp_count = lax.axis_size("dp")
    mp_count = lax.axis_size("mp")
    dp_index = lax.axis_index("dp")
    mp_index = lax.axis_index("mp")
    lang_count = dp_count // 4
    vis_count = dp_count - lang_count
    capacity = max(
        ceil_div(slot_count * PATCH_LARGE, vis_count),
        ceil_div(2 * slot_count * CAPTION, lang_count),
    )
    recv_rows = dp_count * capacity
    kinds, segments = jax.vmap(lambda res_group: slot_layout(res_group, slot_rows))(resolution)
    row_kind = kinds.reshape(-1)
    live_rows = (row_kind != 2).astype(jnp.float32)[:, None]
    vision = (row_kind == 1)[:, None]
    kind_onehot = jnp.stack([row_kind == 0, row_kind == 1], axis=1).astype(jnp.float32)
    rank_vis = jnp.cumsum((row_kind == 1).astype(jnp.int32)) - 1
    rank_txt = jnp.cumsum((row_kind == 0).astype(jnp.int32)) - 1
    target = jnp.where(
        row_kind == 1,
        (rank_vis + dp_index) % vis_count,
        vis_count + (rank_txt + dp_index) % lang_count,
    )
    position = jnp.where(row_kind == 1, rank_vis // vis_count, rank_txt // lang_count)
    slot_index = jnp.where(row_kind == 2, recv_rows, target * capacity + position)

    def to_slots(row_values):
        buffer = (
            jnp.zeros((recv_rows, model_width), row_values.dtype)
            .at[slot_index]
            .set(row_values, mode="drop")
        )
        return buffer.reshape(dp_count, capacity, model_width)

    def from_slots(buffer):
        return jnp.take(
            buffer.reshape(recv_rows, model_width), slot_index, axis=0, mode="fill", fill_value=0
        )

    my_expert = jnp.where(dp_index < vis_count, 1, 0)
    full_up, full_down = (
        lax.all_gather(up_weight, "dp", axis=1, tiled=True),
        lax.all_gather(down_weight, "dp", axis=1, tiled=True),
    )
    own_up = jnp.where(my_expert == 1, full_up[1], full_up[0])
    own_down = jnp.where(my_expert == 1, full_down[1], full_down[0])
    own_up_bias = jnp.where(my_expert == 1, up_bias[1], up_bias[0])
    own_down_bias = jnp.where(my_expert == 1, down_bias[1], down_bias[0])
    x_float = layer_input_rows.astype(jnp.float32)
    normed, norm_pull = jax.vjp(layer_norm, x_float, attn_gain, attn_bias)
    activ = normed.astype(jnp.bfloat16)
    projected = jnp.dot(activ, qkv_weight, preferred_element_type=jnp.float32)
    query = (projected[:, :model_width] + qv_bias[0]).astype(jnp.bfloat16)
    keys = projected[:, model_width : 2 * model_width].astype(jnp.bfloat16)
    values = (projected[:, 2 * model_width :] + qv_bias[1]).astype(jnp.bfloat16)
    query_slots = query.reshape(slot_count, slot_rows, head_count, head_width)
    key_slots = keys.reshape(slot_count, slot_rows, head_count, head_width)
    value_slots = values.reshape(slot_count, slot_rows, head_count, head_width)

    def slot_scores(query_heads, key_heads, segment):
        raw_scores = (
            jnp.einsum("qhd,khd->hqk", query_heads, key_heads, preferred_element_type=jnp.float32)
            * score_scale
        )
        same_seq = (segment[:, None] == segment[None, :])[None]
        return jnp.where(same_seq, raw_scores, -1000000000.0)

    def attend(block_item):
        query_heads, key_heads, value_heads, segment = block_item
        masked = slot_scores(query_heads, key_heads, segment)
        row_max = jnp.max(masked, axis=-1, keepdims=True)
        weights_exp = jnp.exp(masked - row_max)
        row_total = jnp.sum(weights_exp, axis=-1, keepdims=True)
        attn_probs = (weights_exp / row_total).astype(jnp.bfloat16)
        attn_mixed = jnp.einsum(
            "hqk,khd->qhd", attn_probs, value_heads, preferred_element_type=jnp.float32
        )
        log_total = (row_max + jnp.log(row_total))[..., 0]
        return (attn_mixed.reshape(slot_rows, model_width).astype(jnp.bfloat16), log_total)

    attn_mixed, log_totals = lax.map(attend, (query_slots, key_slots, value_slots, segments))
    attn_mixed = attn_mixed.reshape(-1, model_width)
    branch = jnp.dot(attn_mixed, out_weight, preferred_element_type=jnp.float32) + out_bias
    after_attn = x_float + live_rows * attn_scale * branch
    gain_rows = jnp.where(vision, ffn_gain[1], ffn_gain[0])
    shift_rows = jnp.where(vision, ffn_bias[1], ffn_bias[0])
    ffn_normed, norm2_pull = jax.vjp(layer_norm, after_attn, gain_rows, shift_rows)
    sent_rows = ffn_normed.astype(jnp.bfloat16)
    arrived = lax.all_to_all(
        to_slots(sent_rows), "dp", split_axis=0, concat_axis=0, tiled=True
    ).reshape(recv_rows, model_width)
    paired = lax.all_gather(arrived, "mp", axis=0, tiled=True)
    preact = jnp.dot(paired, own_up, preferred_element_type=jnp.float32) + own_up_bias
    hidden, gelu_pull = jax.vjp(exact_gelu, preact)
    hidden_low = hidden.astype(jnp.bfloat16)
    partial_out = contract_cols(hidden_low, own_down)
    expert_sum = (
        lax.psum_scatter(
            partial_out.astype(jnp.bfloat16), "mp", scatter_dimension=0, tiled=True
        ).astype(jnp.float32)
        + own_down_bias
    )
    returned = lax.all_to_all(
        expert_sum.astype(jnp.bfloat16).reshape(dp_count, capacity, model_width),
        "dp",
        split_axis=0,
        concat_axis=0,
        tiled=True,
    )
    expert_rows = from_slots(returned).astype(jnp.float32)
    block_output = (after_attn + live_rows * ffn_scale * expert_rows).astype(jnp.bfloat16)
    grad_float = output_gradient.astype(jnp.float32)
    d_expert = (live_rows * ffn_scale * grad_float).astype(jnp.bfloat16)
    ffn_scale_grad = jnp.sum(live_rows * expert_rows * grad_float, axis=0)
    down_bias_grad = jnp.dot(kind_onehot.T, d_expert.astype(jnp.float32), precision=HIGH)
    arrived_grad = lax.all_to_all(
        to_slots(d_expert), "dp", split_axis=0, concat_axis=0, tiled=True
    ).reshape(recv_rows, model_width)
    paired_grad = lax.all_gather(arrived_grad, "mp", axis=0, tiled=True)
    d_hidden = jnp.dot(paired_grad, own_down, preferred_element_type=jnp.float32)
    d_preact = gelu_pull(d_hidden)[0].astype(jnp.bfloat16)
    own_down_grad = contract_rows(paired_grad, hidden_low)
    own_up_grad = contract_rows(paired, d_preact)
    own_bias_grad = jnp.sum(d_preact.astype(jnp.float32), axis=0)
    d_normed_part = contract_cols(d_preact, own_up)
    d_normed = lax.psum_scatter(
        d_normed_part.astype(jnp.bfloat16), "mp", scatter_dimension=0, tiled=True
    )
    back_grad = lax.all_to_all(
        d_normed.reshape(dp_count, capacity, model_width),
        "dp",
        split_axis=0,
        concat_axis=0,
        tiled=True,
    )
    d_ffn_normed = from_slots(back_grad).astype(jnp.float32)
    d_after_part, gain_grad_rows, shift_grad_rows = norm2_pull(d_ffn_normed)
    ffn_gain_grad = jnp.dot(kind_onehot.T, gain_grad_rows, precision=HIGH)
    ffn_bias_grad = jnp.dot(kind_onehot.T, shift_grad_rows, precision=HIGH)
    d_after = grad_float + d_after_part
    d_branch = (live_rows * attn_scale * d_after).astype(jnp.bfloat16)
    attn_scale_grad = jnp.sum(live_rows * branch * d_after, axis=0)
    out_bias_grad = jnp.sum(d_branch.astype(jnp.float32), axis=0)
    out_weight_grad = contract_rows(attn_mixed, d_branch)
    d_mixed = contract_cols(d_branch, out_weight).astype(jnp.bfloat16)
    d_mixed_slots = d_mixed.reshape(slot_count, slot_rows, head_count, head_width)

    def attend_back(block_item):
        query_heads, key_heads, value_heads, segment, log_total, d_heads = block_item
        masked = slot_scores(query_heads, key_heads, segment)
        probs_full = jnp.exp(masked - log_total[..., None])
        d_probs = jnp.einsum(
            "qhd,khd->hqk", d_heads, value_heads, preferred_element_type=jnp.float32
        )
        row_delta = jnp.sum(probs_full * d_probs, axis=-1, keepdims=True)
        d_scores = (probs_full * (d_probs - row_delta)).astype(jnp.bfloat16)
        probs_low = probs_full.astype(jnp.bfloat16)
        grad_value = jnp.einsum(
            "hqk,qhd->khd", probs_low, d_heads, preferred_element_type=jnp.float32
        )
        grad_query = (
            jnp.einsum("hqk,khd->qhd", d_scores, key_heads, preferred_element_type=jnp.float32)
            * score_scale
        )
        grad_key = (
            jnp.einsum("hqk,qhd->khd", d_scores, query_heads, preferred_element_type=jnp.float32)
            * score_scale
        )
        joined = jnp.concatenate(
            [
                grad_query.reshape(slot_rows, model_width),
                grad_key.reshape(slot_rows, model_width),
                grad_value.reshape(slot_rows, model_width),
            ],
            axis=1,
        )
        return joined.astype(jnp.bfloat16)

    d_projected = lax.map(
        attend_back, (query_slots, key_slots, value_slots, segments, log_totals, d_mixed_slots)
    ).reshape(-1, 3 * model_width)
    qkv_weight_grad = contract_rows(activ, d_projected)
    d_proj_float = d_projected.astype(jnp.float32)
    qv_bias_grad = jnp.stack(
        [
            jnp.sum(d_proj_float[:, :model_width], axis=0),
            jnp.sum(d_proj_float[:, 2 * model_width :], axis=0),
        ]
    )
    d_attn_normed = contract_cols(d_projected, qkv_weight)
    d_input_part, attn_gain_grad, attn_bias_grad = norm_pull(d_attn_normed)
    input_grad = (d_after + d_input_part).astype(jnp.bfloat16)
    expert_pick = (jnp.arange(2) == my_expert).astype(jnp.float32)[:, None, None]
    up_weight_grad, down_weight_grad = (
        lax.psum_scatter(expert_pick * own_up_grad[None], "dp", scatter_dimension=1, tiled=True),
        lax.psum_scatter(expert_pick * own_down_grad[None], "dp", scatter_dimension=1, tiled=True),
    )
    up_bias_full = (
        jnp.zeros((2, mp_count, hidden_part), jnp.float32)
        .at[my_expert, mp_index]
        .set(own_bias_grad)
        .reshape(2, mp_count * hidden_part)
    )
    vector_sums = lax.psum(
        (
            attn_gain_grad,
            attn_bias_grad,
            qv_bias_grad,
            out_bias_grad,
            attn_scale_grad,
            ffn_scale_grad,
            ffn_gain_grad,
            ffn_bias_grad,
            up_bias_full,
            down_bias_grad,
        ),
        ("dp", "mp"),
    )
    matrix_sums = (
        lax.psum_scatter(qkv_weight_grad, ("dp", "mp"), scatter_dimension=0, tiled=True),
        lax.psum_scatter(out_weight_grad, ("dp", "mp"), scatter_dimension=0, tiled=True),
    )
    return (
        block_output,
        input_grad,
        vector_sums[0],
        vector_sums[1],
        matrix_sums[0],
        vector_sums[2],
        matrix_sums[1],
        vector_sums[3],
        vector_sums[4],
        vector_sums[5],
        vector_sums[6],
        vector_sums[7],
        up_weight_grad,
        vector_sums[8],
        down_weight_grad,
        vector_sums[9],
    )


NT = (((1,), (1,)), ((), ()))
TN = (((0,), (0,)), ((), ()))
SMALL = PATCH_SMALL + CAPTION
CAPS = 2 * CAPTION
ANY = pl.BlockSpec(memory_space=pl.ANY)
VM = pl.BlockSpec(memory_space=pltpu.VMEM)
SM = pl.BlockSpec(memory_space=pltpu.SMEM)
DMA = pltpu.SemaphoreType.DMA
CHUNK = 128
V_AG, V_AB, V_QB, V_VB, V_OB, V_AS, V_FS, V_FG, V_FB, V_DB = 0, 1, 2, 3, 4, 5, 6, 7, 9, 11
G_AG, G_AB, G_QB, G_VB, G_OB, G_AS, G_FS, G_FG, G_FB, G_DB, G_UB = 0, 1, 2, 3, 4, 5, 6, 7, 9, 11, 16


def kind_of(res, pos):
    one = lambda c: c.astype(jnp.int32)
    big_seg = 2 * one(pos >= PATCH_LARGE + CAPTION)
    big_kind = 1 - one(pos >= PATCH_LARGE) + big_seg
    small_seg = one(pos >= SMALL) + one(pos >= 2 * SMALL)
    small_pad = one(pos >= 2 * SMALL)
    within = pos - SMALL * small_seg
    small_kind = (1 - small_pad) * one(within < PATCH_SMALL) + 2 * small_pad
    return (
        res * big_kind + (1 - res) * small_kind,
        res * big_seg + (1 - res) * small_seg,
    )


def caption_place(res, slot):
    late = (slot >= CAPTION).astype(jnp.int32)
    big = (1 - late) * (PATCH_LARGE + slot) - late
    small = PATCH_SMALL + slot + late * (SMALL - CAPTION)
    none = (slot >= CAPS).astype(jnp.int32)
    place = res * big + (1 - res) * small
    return (1 - none) * place - none


def iota(shape, dim):
    return lax.broadcasted_iota(jnp.int32, shape, dim)


def fill_bias(res, bias):
    n = bias.shape[0]
    across = kind_of(res, iota((1, n), 1))[1]

    @pl.loop(0, n // CHUNK)
    def _(r):
        base = pl.multiple_of(r * CHUNK, CHUNK)
        down = kind_of(res, iota((CHUNK, 1), 0) + base)[1]
        bias[pl.ds(base, CHUNK), :] = jnp.where(down == across, 0.0, -1000000000.0)


def norm_parts(v):
    center = v - jnp.mean(v, axis=-1, keepdims=True)
    inv = lax.rsqrt(jnp.mean(center * center, axis=-1, keepdims=True) + NORM_EPS)
    return center * inv, inv


def norm_back(xhat, inv, d_hat):
    mean_d = jnp.mean(d_hat, axis=-1, keepdims=True)
    mean_dx = jnp.mean(d_hat * xhat, axis=-1, keepdims=True)
    return inv * (d_hat - mean_d - xhat * mean_dx)


def half_mask(hh, scale):
    lane = iota((1, 128), 1)
    inside = (lane < 64) if hh == 0 else (lane >= 64)
    return jnp.where(inside, scale, 0.0).astype(BF)


def colsum(v):
    return jnp.sum(v, axis=0, keepdims=True)


def dyn_unit(z, k):
    m = k // 2
    zz = z + (z // 2) * (3 - 2 * z)
    u = (1 - m) * (zz + k - 2 * k * zz) + m * k
    w = z // 2
    return u + w * (3 - 2 * u)


class Place:
    def __init__(s):
        s.dp, s.mp = lax.axis_index("dp"), lax.axis_index("mp")
        s.z = s.dp // 4
        s.y = (s.dp // 2) % 2
        s.x = s.dp % 2
        s.xn = s.dp + 1 - 2 * s.x
        s.yn = s.dp + 2 - 4 * s.y
        s.z1 = s.dp + 4 - 8 * (s.z % 2)
        s.z2 = s.dp + 8 - 16 * (s.z // 2)
        s.other = 1 - s.mp
        s.edge = (s.z == 0) | (s.z == 3)
        s.inner = (s.z > 0) & (s.z < 3)
        s.q = s.y * 2 + s.x
        s.dn = s.dp + 3 - 2 * s.x - 4 * s.y
        s.plane = [
            (s.xn, s.y * 2 + 1 - s.x), (s.yn, 2 - 2 * s.y + s.x), (s.dn, 3 - 2 * s.y - s.x)
        ]

    def barrier(s, far=False):
        bar = pltpu.get_barrier_semaphore()
        dp, z = s.dp, s.z

        def sig(d, m):
            pl.semaphore_signal(bar, inc=1, device_id=(d, m), device_id_type=MESHID)

        sig(s.xn, s.mp)
        sig(s.yn, s.mp)
        sig(dp, s.other)
        sig(s.z2 if far else s.dn, s.mp)

        @pl.when(z > 0)
        def _():
            sig(dp - 4, s.mp)

        @pl.when(z < 3)
        def _():
            sig(dp + 4, s.mp)

        pl.semaphore_wait(bar, 5 + ((z + 1) // 2) % 2)


def remote(src, dst, ss, sr, dev, core):
    return pltpu.make_async_remote_copy(
        src_ref=src, dst_ref=dst, send_sem=ss, recv_sem=sr,
        device_id=(dev, core), device_id_type=MESHID,
    )


class AG:
    def __init__(s, place, g, ss, sr, C):
        s.p, s.g, s.ss, s.sr, s.C = place, g, ss, sr, C
        s.rows, s.hid = g.shape[1] // 16, g.shape[2]
        s.ck = s.hid // C
        s.col = place.y * 2 + place.x

    def cp(s, kind, c, u, owner, dev, half=None):
        h = slice(0, 2) if half is None else slice(half, half + 1)
        at = pl.ds(pl.multiple_of(owner * s.rows, 16), s.rows)
        w = s.g.at[h, at, pl.ds(pl.multiple_of(c * s.ck, 128), s.ck)]
        rk = 0 if kind == 1 else kind
        return remote(w, w, s.ss.at[kind, c, u], s.sr.at[rk, c, u], dev, s.p.mp)

    def send(s, k, c, local):
        p = s.p
        z, dp = p.z, p.dp
        u = dyn_unit(z, k)
        owner = u * 4 + s.col
        if not local:
            s.cp(0, c, u, owner, dp).wait_recv()

        @pl.when((u <= z) & (z < 3))
        def _():
            s.cp(0, c, u, owner, dp + 4).start()

        @pl.when((u >= z) & (z > 0))
        def _():
            s.cp(1, c, u, owner, dp - 4).start()

        s.cp(2, c, u, owner, p.xn).start()
        s.cp(3, c, u, owner, p.yn).start()

    def forward(s, k, c):
        p = s.p
        u = dyn_unit(p.z, k)
        xo = u * 4 + p.y * 2 + 1 - p.x
        yo = u * 4 + 2 - 2 * p.y + p.x
        s.cp(2, c, u, xo, p.dp).wait_recv()
        s.cp(5, c, u, xo, p.yn, half=0).start()
        s.cp(3, c, u, yo, p.dp).wait_recv()
        s.cp(4, c, u, yo, p.xn, half=1).start()

    def by_plane(s, edge, inner, f, c):
        @pl.when(s.p.edge)
        def _():
            for k in edge:
                f(k, c)

        if inner:
            @pl.when(s.p.inner)
            def _():
                for k in inner:
                    f(k, c)

    def tick(s, t):
        m, c = t // s.C, t % s.C
        s.by_plane((1 + m,), ((1, 2), (3,), ())[m], lambda k, c: s.send(k, c, False), c)
        if m == 0:
            s.forward(0, c)
        else:
            s.by_plane((m,), ((), (1, 2), (3,))[m], s.forward, c)

    def last(s, c):
        s.by_plane((3,), (), s.forward, c)

    def arrived(s, c):
        for k in range(4):
            u = dyn_unit(s.p.z, k)
            own = u * 4 + s.col
            s.cp(4, c, u, own, s.p.dp, half=1).wait_recv()
            s.cp(5, c, u, own, s.p.dp, half=0).wait_recv()

    def finish(s, k, c):
        p = s.p
        z, dp = p.z, p.dp
        u = dyn_unit(z, k)
        own = u * 4 + s.col
        s.cp(2, c, u, own, dp).wait_send()
        s.cp(3, c, u, own, dp).wait_send()
        s.cp(4, c, u, own, dp, half=1).wait_send()
        s.cp(5, c, u, own, dp, half=0).wait_send()

        @pl.when((u <= z) & (z < 3))
        def _():
            s.cp(0, c, u, own, dp).wait_send()

        @pl.when((u >= z) & (z > 0))
        def _():
            s.cp(1, c, u, own, dp).wait_send()


class CaptionGather:
    def __init__(s, place, own, wc, lsem, ps, pr, zs, zr):
        s.p, s.own, s.wc, s.lsem, s.ps, s.pr, s.zs, s.zr = place, own, wc, lsem, ps, pr, zs, zr
        s.rows, s.quarter = own.shape[1], wc.shape[2]
        s.at = pl.ds(pl.multiple_of(place.dp * s.rows, 16), s.rows)

    def part(s, q):
        return s.own.at[:, :, pl.ds(pl.multiple_of(q * s.quarter, 128), s.quarter)]

    def keep(s):
        return pltpu.make_async_copy(s.part(s.p.q), s.wc.at[:, s.at, :], s.lsem)

    def flat(s, i):
        dev, q = s.p.plane[i]
        return remote(s.part(q), s.wc.at[:, s.at, :], s.ps.at[i], s.pr.at[i], dev, s.p.mp)

    def start(s):
        s.keep().start()
        for i in range(3):
            s.flat(i).start()

    def hop(s, kind, u, dev):
        n = 4 * s.rows
        w = s.wc.at[:, pl.ds(pl.multiple_of(u * n, 16), n), :]
        return remote(w, w, s.zs.at[kind, u], s.zr.at[u], dev, s.p.mp)

    def step(s, k):
        z, dp = s.p.z, s.p.dp
        u = dyn_unit(z, k)
        if isinstance(k, int) and k == 0:
            s.keep().wait()
            for i in range(3):
                s.flat(i).wait()
        else:
            s.hop(0, u, dp).wait_recv()

        @pl.when((u <= z) & (z < 3))
        def _():
            s.hop(0, u, dp + 4).start()

        @pl.when((u >= z) & (z > 0))
        def _():
            s.hop(1, u, dp - 4).start()

    def stage(s, m):
        @pl.when(s.p.edge)
        def _():
            s.step(m)

        if m < 3:
            @pl.when(s.p.inner)
            def _():
                for k in ((1, 2), (3,))[m - 1]:
                    s.step(k)

    def finish(s):
        z, dp = s.p.z, s.p.dp
        for k in range(4):
            u = dyn_unit(z, k)

            @pl.when((u <= z) & (z < 3))
            def _():
                s.hop(0, u, dp + 4).wait_send()

            @pl.when((u >= z) & (z > 0))
            def _():
                s.hop(1, u, dp - 4).wait_send()


class CaptionScatter:
    def __init__(s, place, g, bu, bd, got, ps, pr, zs, zr, out):
        s.p, s.g, s.bu, s.bd, s.got, s.out = place, g, bu, bd, got, out
        s.ps, s.pr, s.zs, s.zr = ps, pr, zs, zr
        s.rows = g.shape[1] // 16

    def win(s, u):
        n = 4 * s.rows
        return s.g.at[:, pl.ds(pl.multiple_of(u * n, 16), n), :]

    def up(s, u):
        return remote(s.win(u), s.bu.at[u], s.zs.at[0, u], s.zr.at[0, u], s.p.dp + 4, s.p.mp)

    def down(s, u):
        return remote(s.win(u), s.bd.at[u], s.zs.at[1, u], s.zr.at[1, u], s.p.dp - 4, s.p.mp)

    def owner(s, q):
        at = pl.multiple_of((s.p.z * 4 + q) * s.rows, 16)
        return s.g.at[:, pl.ds(at, s.rows), :]

    def flat(s, i):
        dev, q = s.p.plane[i]
        return remote(s.owner(q), s.got.at[i], s.ps.at[i], s.pr.at[i], dev, s.p.mp)

    def step(s, k, edge=None):
        z = s.p.z
        u = dyn_unit(z, k)
        o = s.win(u)

        def go(pred, wu, wd, send):
            @pl.when(pred)
            def _():
                v = o[...].astype(F32)
                if wu:
                    s.up(u).wait_recv()
                    v = v + s.bu.at[u][...].astype(F32)
                if wd:
                    s.down(u).wait_recv()
                    v = v + s.bd.at[u][...].astype(F32)
                if wu or wd:
                    o[...] = v.astype(BF)
                if send is not None:
                    send(u).start()

        if k > 0:
            if edge:
                go(u > z, False, False, s.up)
                go(u < z, False, False, s.down)
            else:
                go(u > z, True, False, s.up)
                go(u < z, False, True, s.down)
        else:
            go(z == 0, False, True, None)
            go(z == 3, True, False, None)
            go((z > 0) & (z < 3), True, True, None)
            for i in range(3):
                s.flat(i).start()

    def stage(s, m):
        if m < 3:
            @pl.when(s.p.edge)
            def _():
                s.step(3 - m, True)

        if 0 < m < 4:
            @pl.when(s.p.inner)
            def _():
                s.step(4 - m, False)

        if m == 4:
            s.step(0)

    def finish(s):
        own = s.owner(s.p.q)
        s.out(s.p.q, own[0].astype(F32), own[1].astype(F32))
        for i in range(3):
            s.flat(i).wait()
            s.out(s.p.plane[i][1], s.got[i, 0].astype(F32), s.got[i, 1].astype(F32))
        for k in range(1, 4):
            u = dyn_unit(s.p.z, k)

            @pl.when(u > s.p.z)
            def _():
                s.up(u).wait_send()

            @pl.when(u < s.p.z)
            def _():
                s.down(u).wait_send()


class RS:
    def __init__(s, place, g, bufs, ss, sr, C, write, lags):
        s.p, s.g, s.write, s.lags = place, g, write, lags
        s.bx, s.by, s.bdx, s.bdy, s.bzu, s.bzd = bufs
        s.ss, s.sr, s.C = ss, sr, C
        s.M = g.shape[0]
        s.flat = len(g.shape) == 3
        s.rows = g.shape[1] // 16 if s.flat else g.shape[2]
        s.ck = g.shape[-1] // C
        s.h0 = s.M // 2
        x, y = place.x, place.y
        s.oo = y * 2 + x
        s.ox = y * 2 + 1 - x
        s.oy = 2 - 2 * y + x
        s.od = 3 - 2 * y - x

    def cols(s, c):
        return pl.ds(pl.multiple_of(c * s.ck, 128), s.ck)

    def win(s, u, col, c, lo=0, hi=None):
        hi = s.M if hi is None else hi
        if s.flat:
            at = pl.multiple_of((u * 4 + col) * s.rows, 16)
            return s.g.at[lo:hi, pl.ds(at, s.rows), s.cols(c)]
        return s.g.at[lo:hi, u * 4 + col, :, s.cols(c)]

    def cp(s, kind, u, c, src, dst, dev):
        return remote(src, dst, s.ss.at[kind, c, u], s.sr.at[kind, c, u], dev, s.p.mp)

    def bw(s, b, u, c):
        return b.at[u, :, :, s.cols(c)]

    def c_dy(s, u, c):
        return s.cp(0, u, c, s.win(u, s.od, c, 0, s.h0), s.bw(s.bdy, u, c), s.p.yn)

    def c_dx(s, u, c):
        return s.cp(1, u, c, s.win(u, s.od, c, s.h0), s.bw(s.bdx, u, c), s.p.xn)

    def c_x(s, u, c):
        return s.cp(2, u, c, s.win(u, s.ox, c), s.bw(s.bx, u, c), s.p.xn)

    def c_y(s, u, c):
        return s.cp(3, u, c, s.win(u, s.oy, c), s.bw(s.by, u, c), s.p.yn)

    def c_zu(s, u, c):
        return s.cp(4, u, c, s.win(u, s.oo, c), s.bw(s.bzu, u, c), s.p.dp + 4)

    def c_zd(s, u, c):
        return s.cp(5, u, c, s.win(u, s.oo, c), s.bw(s.bzd, u, c), s.p.dp - 4)

    def item(s, t):
        return dyn_unit(s.p.z, 3 - t // s.C), t % s.C

    def s1(s, t):
        u, c = s.item(t)
        s.c_dy(u, c).start()
        s.c_dx(u, c).start()

    def add(s, dst, src):
        dst[...] = (dst[...].astype(F32) + src[...].astype(F32)).astype(BF)

    def s2(s, t):
        u, c = s.item(t)
        s.c_dy(u, c).wait_recv()
        s.add(s.win(u, s.ox, c, 0, s.h0), s.bw(s.bdy, u, c))
        s.c_x(u, c).start()
        s.c_dx(u, c).wait_recv()
        s.add(s.win(u, s.oy, c, s.h0), s.bw(s.bdx, u, c))
        s.c_y(u, c).start()

    def s3(s, edge, t):
        u, c = s.item(t)
        z = s.p.z
        s.c_x(u, c).wait_recv()
        s.c_y(u, c).wait_recv()
        o = s.win(u, s.oo, c)

        def total(*bufs):
            v = o[...].astype(F32)
            for b in (s.bx, s.by) + bufs:
                v = v + s.bw(b, u, c)[...].astype(F32)
            return v

        def go(pred, wu, wd, send):
            @pl.when(pred)
            def _():
                more = ()
                if wu:
                    s.c_zu(u, c).wait_recv()
                    more += (s.bzu,)
                if wd:
                    s.c_zd(u, c).wait_recv()
                    more += (s.bzd,)
                v = total(*more)
                if send is None:
                    s.write(c, v)
                else:
                    o[...] = v.astype(BF)
                    send(u, c).start()

        up, dn, own = u > z, u < z, u == z
        if edge:
            go(up, False, False, s.c_zu)
            go(dn, False, False, s.c_zd)
            go(own & (z == 0), False, True, None)
            go(own & (z == 3), True, False, None)
        else:
            go(up, True, False, s.c_zu)
            go(dn, False, True, s.c_zd)
            go(own, True, True, None)

    def tick(s, t):
        n = 4 * s.C
        everywhere = s.p.z >= 0
        stages = [
            (lag, f, where)
            for lag, f, where in zip(
                s.lags,
                (s.s1, s.s2, functools.partial(s.s3, True), functools.partial(s.s3, False)),
                (everywhere, everywhere, s.p.edge, s.p.inner),
            )
            if lag is not None
        ]
        for lag, f, where in stages:
            i = t - lag
            if isinstance(t, int):
                if 0 <= i < n:
                    if where is everywhere:
                        f(i)
                    else:
                        @pl.when(where)
                        def _():
                            f(i)
            else:
                @pl.when((i >= 0) & (i < n) & where)
                def _():
                    f(i)

    def finish(s, t):
        u, c = s.item(t)
        for f in (s.c_dy, s.c_dx, s.c_x, s.c_y):
            f(u, c).wait_send()

        @pl.when(u > s.p.z)
        def _():
            s.c_zu(u, c).wait_send()

        @pl.when(u < s.p.z)
        def _():
            s.c_zd(u, c).wait_send()


def load_all(pairs, sem):
    copies = [pltpu.make_async_copy(a, b, sem.at[i]) for i, (a, b) in enumerate(pairs)]
    for c in copies:
        c.start()
    return copies


def front_kernel(
    C, res_ref, a_gain, a_bias, qv_bias, o_bias, a_scale, f_scale, f_gain, f_bias, dn_bias, up_bias,
    x, og, wqkv, wout, up_ref, down_ref,
    proj, activ, mixed, vec, ub, fsum, bsum, cgrads, grads,
    g, wc, cown, bias, qkvb, xall, gall, xt, gt, cr, crt, accf, accb, rcv, stage, hid, dpre, ubg,
    chid, cdpre, pc, prc, prq,
    lsem, ss, sr, ps, pr, cs, cg_r, zs, zr, bs, br,
):
    p = Place()
    n, width = x.shape
    res = res_ref[0]
    ag = AG(p, g, ss, sr, C)
    mine = pl.ds(pl.multiple_of(p.dp * ag.rows, 16), ag.rows)
    loads = load_all(
        [
            (up_ref.at[1], g.at[0, mine, :]), (down_ref.at[1], g.at[1, mine, :]),
            (up_ref.at[0], cown.at[0]), (down_ref.at[0], cown.at[1]),
        ],
        lsem,
    )
    p.barrier()
    for c in loads:
        c.wait()
    capg = CaptionGather(p, cown, wc, lsem.at[4], cs.at[0], cg_r.at[0], zs, zr)
    capg.start()
    for c in range(C):
        ag.send(0, c, True)

    for row, ref in (
        (V_AG, a_gain), (V_AB, a_bias), (V_OB, o_bias), (V_AS, a_scale), (V_FS, f_scale),
    ):
        vec[row:row + 1, :] = ref[...].reshape(1, width)
    for row, ref in ((V_QB, qv_bias), (V_FG, f_gain), (V_FB, f_bias), (V_DB, dn_bias)):
        vec[row:row + 2, :] = ref[...]
    vec[13:16, :] = jnp.zeros((3, width), F32)

    @pl.loop(0, n // CHUNK)
    def _(r):
        at = pl.ds(pl.multiple_of(r * CHUNK, CHUNK), CHUNK)
        hat, _ = norm_parts(x[at, :].astype(F32))
        activ[at, :] = (hat * vec[V_AG:V_AG + 1, :] + vec[V_AB:V_AB + 1, :]).astype(BF)

    ag.tick(0)
    qkvb[:, :width] = vec[V_QB:V_QB + 1, :]
    qkvb[:, width:2 * width] = jnp.zeros((1, width), F32)
    qkvb[:, 2 * width:] = vec[V_VB:V_VB + 1, :]
    part = 384

    @pl.loop(0, 3 * width // part)
    def _(j):
        at = pl.ds(pl.multiple_of(j * part, 128), part)
        v = jnp.dot(activ[...], wqkv[:, at], preferred_element_type=F32)
        proj[:, at] = (v + qkvb[:, at]).astype(BF)

    ag.tick(1)
    fill_bias(res, bias)
    masks = [half_mask(0, 0.125), half_mask(1, 0.125)]
    first = iota((1, 128), 1) < 64

    @pl.loop(0, width // 128)
    def _(h):
        def cols(base):
            return pl.ds(pl.multiple_of(base + h * 128, 128), 128)

        for i, t in ((1, 2), (3, 3), (4, 4)):
            @pl.when(h == i)
            def _():
                ag.tick(t)

        q, k, v = proj[:, cols(0)], proj[:, cols(width)], proj[:, cols(2 * width)]
        outs = []
        for hh in range(2):
            s = lax.dot_general(q * masks[hh], k, NT, preferred_element_type=F32) + bias[...]
            e = jnp.exp(s - jnp.max(s, axis=-1, keepdims=True))
            pr_low = (e * (1.0 / jnp.sum(e, axis=-1, keepdims=True))).astype(BF)
            outs.append(jnp.dot(pr_low, v, preferred_element_type=F32))
        mixed[:, cols(0)] = jnp.where(first, outs[0], outs[1]).astype(BF)

    ag.tick(5)
    capg.step(0)
    half = 256

    @pl.loop(0, width // half)
    def _(j):
        at = pl.ds(pl.multiple_of(j * half, 128), half)
        accf[:n, at] = jnp.dot(mixed[...], wout[:, at], preferred_element_type=F32)

    ag.tick(6)
    img = p.mp * n
    caps = p.mp * 4 * CAPS + p.q * CAPS

    @pl.loop(0, n // CHUNK)
    def _(r):
        base = pl.multiple_of(r * CHUNK, CHUNK)
        at = pl.ds(base, CHUNK)
        to = pl.ds(pl.multiple_of(img + base, 128), CHUNK)
        kind = kind_of(res, iota((CHUNK, 1), 0) + base)[0]
        live = (kind < 2).astype(F32)
        row = x[at, :].astype(F32)
        row = row + live * vec[V_AS:V_AS + 1, :] * (accf[at, :] + vec[V_OB:V_OB + 1, :])
        hat, _ = norm_parts(row)
        gain = jnp.where(kind == 1, vec[V_FG + 1:V_FG + 2, :], vec[V_FG:V_FG + 1, :])
        shift = jnp.where(kind == 1, vec[V_FB + 1:V_FB + 2, :], vec[V_FB:V_FB + 1, :])
        xall[to, :] = (hat * gain + shift).astype(BF)
        gall[to, :] = (live * vec[V_FS:V_FS + 1, :] * og[at, :].astype(F32)).astype(BF)

    ag.tick(7)
    pick = (iota((CAPS, n), 1) == caption_place(res, iota((CAPS, 1), 0))).astype(F32).astype(BF)
    at_img = pl.ds(pl.multiple_of(img, 128), n)
    at_cap = pl.ds(pl.multiple_of(caps, 16), CAPS)
    for i, ref in enumerate((xall, gall)):
        cr[i, at_cap, :] = jnp.dot(pick, ref[at_img, :], preferred_element_type=F32).astype(BF)

    def rows_to(i):
        w = cr.at[:, at_cap, :]
        return remote(w, w, cs.at[1, i], cg_r.at[1, i], p.plane[i][0], p.mp)

    def relay(i):
        q = p.q if i == 3 else p.plane[i][1]
        w = cr.at[:, pl.ds(pl.multiple_of(p.mp * 4 * CAPS + q * CAPS, 16), CAPS), :]
        return remote(w, w, bs.at[i], br.at[i], p.dp, p.other)

    ag.tick(8)
    relay(3).start()

    @pl.loop(0, n // CHUNK)
    def _(r):
        base = pl.multiple_of(r * CHUNK, CHUNK)
        to = pl.ds(pl.multiple_of(img + base, 128), CHUNK)
        vis = (kind_of(res, iota((CHUNK, 1), 0) + base)[0] == 1).astype(F32)
        gall[to, :] = (gall[to, :].astype(F32) * vis).astype(BF)

    pairs = []
    for i, ref in enumerate((xall, gall)):
        w = ref.at[at_img, :]
        pairs.append(remote(w, w, ps.at[i], pr.at[i], p.dp, p.other))
        pairs[-1].start()
    capg.stage(1)
    accf[...] = jnp.zeros(accf.shape, F32)
    accb[...] = jnp.zeros(accb.shape, F32)
    ubg[...] = jnp.zeros(ubg.shape, F32)

    def turn(base):
        @pl.loop(0, n // CHUNK)
        def _(r):
            at = pl.ds(pl.multiple_of(base + r * CHUNK, CHUNK), CHUNK)
            xt[:, at] = xall[at, :].T
            gt[:, at] = gall[at, :].T

    turn(img)
    ag.last(0)
    ag.last(1)
    for c in pairs:
        c.wait()
    turn(p.other * n)
    ag.last(2)
    for i in range(3):
        rows_to(i).start()
    capg.stage(2)
    ck = ag.ck

    def saved(c):
        return pltpu.make_async_copy(stage, grads.at[:, :, c * ck:(c + 1) * ck], lsem.at[2])

    def gelu_pair(v, dh):
        cdf = 0.5 * (1.0 + lax.erf(v * (0.5 ** 0.5)))
        slope = cdf + v * (jnp.exp(v * v * -0.5) * 0.3989422804014327)
        return (v * cdf).astype(BF), (dh * slope).astype(BF)

    def rows_step(c, at):
        here = slice(c * ck, (c + 1) * ck)
        up, down = g[0, :, here], g[1, :, here]
        v = jnp.dot(xall[at, :], up, preferred_element_type=F32) + up_bias[1:2, here]
        dh = jnp.dot(gall[at, :], down, preferred_element_type=F32)
        h_low, d_low = gelu_pair(v, dh)
        hid[at, :] = h_low
        dpre[at, :] = d_low
        accf[at, :] += lax.dot_general(h_low, down, NT, preferred_element_type=F32)
        accb[at, :] += lax.dot_general(d_low, up, NT, preferred_element_type=F32)
        ubg[1:2, here] += colsum(d_low.astype(F32))

    quarter = wc.shape[2]
    my_cols = pl.ds(pl.multiple_of(p.q * quarter, 128), quarter)
    cap_all = 4 * CAPS

    def caption_pair():
        w = pc.at[:, pl.ds(pl.multiple_of(p.other * cap_all, 16), cap_all), :]
        return remote(w, prc, ps.at[4], pr.at[4], p.dp, p.other)

    def caption_flat(i):
        dev, q = p.plane[i]
        w = pc.at[:, pl.ds(pl.multiple_of(p.mp * cap_all + q * CAPS, 16), CAPS), :]
        return remote(w, prq.at[i], cs.at[2, i], cg_r.at[2, i], dev, p.mp)

    def captions():
        for i in range(4):
            relay(i).wait()

        @pl.loop(0, 5)
        def _(r):
            at = pl.ds(pl.multiple_of(r * CHUNK, CHUNK), CHUNK)
            for i in range(2):
                crt[i, :, at] = cr[i, at, :].T

        @pl.loop(0, 2)
        def _(r):
            at = pl.ds(pl.multiple_of(r * cap_all, 16), cap_all)
            v = jnp.dot(cr[0, at, :], wc[0], preferred_element_type=F32) + up_bias[0:1, my_cols]
            dh = jnp.dot(cr[1, at, :], wc[1], preferred_element_type=F32)
            h_low, d_low = gelu_pair(v, dh)
            chid[at, :] = h_low
            cdpre[at, :] = d_low
            pc[0, at, :] = lax.dot_general(h_low, wc[1], NT, preferred_element_type=F32).astype(BF)
            pc[1, at, :] = lax.dot_general(d_low, wc[0], NT, preferred_element_type=F32).astype(BF)
            ubg[0:1, my_cols] += colsum(d_low.astype(F32))

        caption_pair().start()

        @pl.loop(0, width // 256)
        def _(r):
            at = pl.ds(pl.multiple_of(r * 256, 256), 256)
            cgrads[0, at, :] = jnp.dot(
                crt[0, at, :], cdpre[...], preferred_element_type=F32
            ).astype(BF)
            cgrads[1, at, :] = jnp.dot(
                crt[1, at, :], chid[...], preferred_element_type=F32
            ).astype(BF)

        caption_pair().wait()

        @pl.loop(0, 4)
        def _(r):
            at = pl.ds(pl.multiple_of(p.mp * cap_all + r * CAPS, 16), CAPS)
            got = pl.ds(pl.multiple_of(r * CAPS, 16), CAPS)
            for i in range(2):
                pc[i, at, :] = (pc[i, at, :].astype(F32) + prc[i, got, :].astype(F32)).astype(BF)

        for i in range(3):
            caption_flat(i).start()

    back_pairs = []
    for c in range(C):
        ag.arrived(c)

        @pl.loop(0, 2 * n // 256)
        def _(r):
            rows_step(c, pl.ds(pl.multiple_of(r * 256, 256), 256))

        if c == C - 1:
            theirs_img = pl.ds(pl.multiple_of(p.other * n, 128), n)
            for i, (acc, low) in enumerate(((accf, xall), (accb, gall))):
                @pl.loop(0, 2 * n // CHUNK)
                def _(r):
                    at = pl.ds(pl.multiple_of(r * CHUNK, CHUNK), CHUNK)
                    low[at, :] = acc[at, :].astype(BF)

                to = rcv.at[i]
                back_pairs.append(
                    remote(low.at[theirs_img, :], to, ps.at[2 + i], pr.at[2 + i], p.dp, p.other)
                )
                back_pairs[-1].start()
        if c == 1:
            for i in range(3):
                rows_to(i).wait()
                relay(i).start()
            capg.stage(3)
        if c > 0:
            saved(c - 1).wait()

        @pl.loop(0, width // 256)
        def _(r):
            at = pl.ds(pl.multiple_of(r * 256, 256), 256)
            stage[0, at, :] = jnp.dot(xt[at, :], dpre[...], preferred_element_type=F32).astype(BF)
            stage[1, at, :] = jnp.dot(gt[at, :], hid[...], preferred_element_type=F32).astype(BF)

        saved(c).start()
        if c == 1:
            captions()
    ub[...] = jnp.zeros(ub.shape, F32)
    for e in range(2):
        for j in range(2):
            ub[pl.ds(e * 4 + p.mp * 2 + j, 1), :] = ubg[e:e + 1, j * width:(j + 1) * width]
    for c in back_pairs:
        c.wait()
    for i in range(3):
        caption_flat(i).wait()
    for i, (low, out) in enumerate(((xall, fsum), (gall, bsum))):
        @pl.loop(0, n // CHUNK)
        def _(r):
            base = r * CHUNK
            at = pl.ds(pl.multiple_of(base, CHUNK), CHUNK)
            own = low[pl.ds(pl.multiple_of(img + base, CHUNK), CHUNK), :].astype(F32)
            out[at, :] = (own + rcv[i, at, :].astype(F32)).astype(BF)

        own = pc[i, at_cap, :].astype(F32)
        for j in range(3):
            own = own + prq[j, i].astype(F32)
        out[n:, :] = own.astype(BF)
    saved(C - 1).wait()
    pl.loop(0, 4 * C)(lambda t: ag.finish(t // C, t % C))
    capg.finish()


def front(res, small, up_bias, x, og, wqkv, wout, up, down, C=3):
    n, width = x.shape
    _, rows, hid = up.shape
    ck = hid // C
    sds = jax.ShapeDtypeStruct
    wide = 2 * n
    quarter = hid // 4
    caps = 8 * CAPS
    return pl.pallas_call(
        functools.partial(front_kernel, C),
        out_shape=(
            sds((n, 3 * width), BF),
            sds((n, width), BF),
            sds((n, width), BF),
            sds((16, width), F32),
            sds((8, width), F32),
            sds((n + CAPS, width), BF),
            sds((n + CAPS, width), BF),
            sds((2, rows * 16, quarter), BF),
            sds((2, rows * 16, hid), BF),
        ),
        in_specs=[SM] + [VM] * 14 + [ANY, ANY],
        out_specs=(VM,) * 8 + (ANY,),
        scratch_shapes=[
            pltpu.VMEM((2, rows * 16, hid), BF),
            pltpu.VMEM((2, rows * 16, quarter), BF),
            pltpu.VMEM((2, rows, hid), BF),
            pltpu.VMEM((n, n), F32),
            pltpu.VMEM((1, 3 * width), F32),
            pltpu.VMEM((wide, width), BF),
            pltpu.VMEM((wide, width), BF),
            pltpu.VMEM((width, wide), BF),
            pltpu.VMEM((width, wide), BF),
            pltpu.VMEM((2, caps, width), BF),
            pltpu.VMEM((2, width, caps), BF),
            pltpu.VMEM((wide, width), F32),
            pltpu.VMEM((wide, width), F32),
            pltpu.VMEM((2, n, width), BF),
            pltpu.VMEM((2, rows * 16, ck), BF),
            pltpu.VMEM((wide, ck), BF),
            pltpu.VMEM((wide, ck), BF),
            pltpu.VMEM((2, hid), F32),
            pltpu.VMEM((caps, quarter), BF),
            pltpu.VMEM((caps, quarter), BF),
            pltpu.VMEM((2, caps, width), BF),
            pltpu.VMEM((2, caps // 2, width), BF),
            pltpu.VMEM((3, 2, CAPS, width), BF),
            DMA((5,)), DMA((6, C, 4)), DMA((6, C, 4)), DMA((5,)), DMA((5,)),
            DMA((3, 3)), DMA((3, 3)), DMA((2, 4)), DMA((4,)), DMA((4,)), DMA((4,)),
        ],
        compiler_params=pltpu.CompilerParams(
            collective_id=0, has_side_effects=True, vmem_limit_bytes=67043328
        ),
        name="front",
    )(res, *small, up_bias, x, og, wqkv, wout, up, down)


def back_kernel(
    C, res_ref, vec, ub, x, og, fsum, bsum, proj_h, mixed_h, activ_h, wout, cgrads_h, grads_h,
    out_up, out_down, block, d_proj, d_after, vsum, gq,
    g, bx, by, bdx, bdy, bzu, bzd, cg, cbu, cbd, cgot, proj, mixed, activ, turned, capf, branch, d_mixed, d_branch, bias,
    full, split, got, lsem, ss, sr, cps, cpr, czs, czr, ps, pr,
):
    p = Place()
    n, width = x.shape
    res = res_ref[0]
    loads = load_all(
        [(grads_h, g), (proj_h, proj), (mixed_h, mixed), (cgrads_h, cg), (activ_h, activ)], lsem
    )
    p.barrier()

    def write(c, v):
        at = pl.ds(pl.multiple_of(c * (g.shape[2] // C), 128), g.shape[2] // C)
        out_up[1, :, at] = v[0]
        out_down[1, :, at] = v[1]

    def caption_out(q, up, down):
        quarter = cg.shape[2]
        at = pl.ds(pl.multiple_of(q * quarter, 128), quarter)
        out_up[0, :, at] = up
        out_down[0, :, at] = down

    rs = RS(p, g, (bx, by, bdx, bdy, bzu, bzd), ss, sr, C, write, (0, 2, 4, 5))
    cap = CaptionScatter(p, cg, cbu, cbd, cgot, cps, cpr, czs, czr, caption_out)
    loads[0].wait()
    rs.tick(0)
    loads[3].wait()
    cap.stage(0)
    loads[1].wait()
    loads[2].wait()
    loads[4].wait()
    fill_bias(res, bias)
    half = 256

    @pl.loop(0, width // half)
    def _(j):
        at = pl.ds(pl.multiple_of(j * half, 128), half)
        branch[:, at] = jnp.dot(mixed[...], wout[:, at], preferred_element_type=F32)

    rs.tick(1)
    vsum[...] = jnp.zeros(vsum.shape, F32)
    vsum[G_UB:G_UB + 8, :] = ub[...]
    pad = jnp.zeros((128 - CAPS, width), BF)
    for i, ref in enumerate((fsum, bsum)):
        capf[i] = jnp.concatenate([ref[n:, :], pad], axis=0)

    def add(row, v):
        vsum[row:row + 1, :] += colsum(v)

    @pl.loop(0, n // CHUNK)
    def _(r):
        @pl.when(r == 2)
        def _():
            rs.tick(2)

        base = pl.multiple_of(r * CHUNK, CHUNK)
        at = pl.ds(base, CHUNK)
        for i, ref in enumerate((activ, mixed)):
            turned[i, :, at] = ref[at, :].T
        pos = iota((CHUNK, 1), 0) + base
        kind = kind_of(res, pos)[0]
        live = (kind < 2).astype(F32)
        vis = kind == 1
        cap = kind == 0
        pick = (pos == caption_place(res, iota((1, 128), 1))).astype(F32).astype(BF)
        from_cap = jnp.dot(pick, capf[0], preferred_element_type=F32)
        d_cap = jnp.dot(pick, capf[1], preferred_element_type=F32)
        from_img = fsum[at, :].astype(F32)
        d_img = bsum[at, :].astype(F32)
        grad = og[at, :].astype(F32)
        row_branch = branch[at, :] + vec[V_OB:V_OB + 1, :]
        scale = live * vec[V_AS:V_AS + 1, :]
        after = x[at, :].astype(F32) + scale * row_branch
        expert = jnp.where(
            cap, from_cap + vec[V_DB:V_DB + 1, :], from_img + vec[V_DB + 1:V_DB + 2, :]
        ).astype(BF).astype(F32)
        ffn_scale = live * vec[V_FS:V_FS + 1, :]
        block[at, :] = (after + ffn_scale * expert).astype(BF)
        add(G_FS, live * expert * grad)
        d_expert = (ffn_scale * grad).astype(BF).astype(F32)
        add(G_DB, jnp.where(cap, d_expert, 0.0))
        add(G_DB + 1, jnp.where(vis, d_expert, 0.0))
        d_ffn = jnp.where(cap, d_cap, d_img)
        hat, inv = norm_parts(after)
        d_gain = d_ffn * hat
        add(G_FG, jnp.where(cap, d_gain, 0.0))
        add(G_FG + 1, jnp.where(vis, d_gain, 0.0))
        add(G_FB, jnp.where(cap, d_ffn, 0.0))
        add(G_FB + 1, jnp.where(vis, d_ffn, 0.0))
        gain = jnp.where(vis, vec[V_FG + 1:V_FG + 2, :], vec[V_FG:V_FG + 1, :])
        da = grad + norm_back(hat, inv, d_ffn * gain)
        d_after[at, :] = da
        add(G_AS, live * row_branch * da)
        db = (scale * da).astype(BF)
        d_branch[at, :] = db
        add(G_OB, db.astype(F32))

    rs.tick(3)
    cap.stage(1)
    rows = width // 32

    def pair(j):
        return remote(split.at[p.other, j], got.at[j], ps.at[j], pr.at[j], p.dp, p.other)

    def weight_part(j):
        if j < 3:
            right = d_proj[:, j * width:(j + 1) * width]
        else:
            right = d_branch[...]
        full[...] = jnp.dot(turned[j // 3], right, preferred_element_type=F32)

        @pl.loop(0, 16)
        def _(o):
            for core in range(2):
                at = pl.ds(pl.multiple_of((2 * o + core) * rows, 8), rows)
                split[core, j, o] = full[at, :].astype(BF)

        pair(j).start()

    def weight_sum(j):
        pair(j).wait()

        @pl.loop(0, 16)
        def _(o):
            v = split[p.mp, j, o].astype(F32) + got[j, o].astype(F32)
            gq[j // 2, o, :, (j % 2) * width:(j % 2 + 1) * width] = v.astype(BF)

    @pl.loop(0, width // half)
    def _(j):
        at = pl.ds(pl.multiple_of(j * half, 128), half)
        v = lax.dot_general(d_branch[...], wout[at, :], NT, preferred_element_type=F32)
        d_mixed[:, at] = v.astype(BF)

    rs.tick(4)
    weight_part(3)

    ones = [half_mask(0, 1.0), half_mask(1, 1.0)]
    scaled = [half_mask(0, 0.125), half_mask(1, 0.125)]
    first = iota((1, 128), 1) < 64

    @pl.loop(0, width // 128)
    def _(h):
        rs.tick(5 + h)
        for i, m in ((1, 2), (3, 3)):
            @pl.when(h == i)
            def _():
                cap.stage(m)

        def cols(base):
            return pl.ds(pl.multiple_of(base + h * 128, 128), 128)

        q, k, v = proj[:, cols(0)], proj[:, cols(width)], proj[:, cols(2 * width)]
        do = d_mixed[:, cols(0)]
        q_scaled = q * jnp.full((1, 128), 0.125, BF)
        k_turned = (k.astype(F32) * 0.125).T.astype(BF)
        dq, dk, dv = [], [], []
        for hh in range(2):
            s = lax.dot_general(k * scaled[hh], q, NT, preferred_element_type=F32) + bias[...]
            e = jnp.exp(s - jnp.max(s, axis=0, keepdims=True))
            pt = e * (1.0 / jnp.sum(e, axis=0, keepdims=True))
            dpt = lax.dot_general(v * ones[hh], do, NT, preferred_element_type=F32)
            delta = jnp.sum(pt * dpt, axis=0, keepdims=True)
            dst = (pt * (dpt - delta)).astype(BF)
            dv.append(jnp.dot(pt.astype(BF), do, preferred_element_type=F32))
            dk.append(jnp.dot(dst, q_scaled, preferred_element_type=F32))
            dq.append(jnp.dot(k_turned[64 * hh:64 * hh + 64], dst, preferred_element_type=F32))
        dq_all = jnp.concatenate(dq, axis=0).T.astype(BF)
        dv_all = jnp.where(first, dv[0], dv[1]).astype(BF)
        d_proj[:, cols(0)] = dq_all
        d_proj[:, cols(width)] = jnp.where(first, dk[0], dk[1]).astype(BF)
        d_proj[:, cols(2 * width)] = dv_all
        vsum[G_QB:G_QB + 1, cols(0)] = colsum(dq_all.astype(F32))
        vsum[G_VB:G_VB + 1, cols(0)] = colsum(dv_all.astype(F32))

    rs.tick(11)
    cap.stage(4)
    weight_part(0)
    weight_sum(3)
    rs.tick(12)
    weight_part(1)
    weight_sum(0)
    rs.tick(13)
    weight_part(2)
    weight_sum(1)
    rs.tick(14)
    rs.tick(15)
    rs.tick(16)
    cap.finish()
    weight_sum(2)
    pl.loop(0, 4 * C)(rs.finish)


def back(res, vec, ub, x, og, fsum, bsum, proj, mixed, activ, wout, cgrads, grads, C=3):
    quarter = cgrads.shape[2]
    n, width = x.shape
    M, rows, hid = grads.shape[0], grads.shape[1] // 16, grads.shape[2]
    own = width // 32
    sds = jax.ShapeDtypeStruct
    full = pltpu.VMEM((4, M, rows, hid), BF)
    part = pltpu.VMEM((4, M // 2, rows, hid), BF)
    return pl.pallas_call(
        functools.partial(back_kernel, C),
        out_shape=(
            sds((2, rows, hid), F32),
            sds((2, rows, hid), F32),
            sds((n, width), BF),
            sds((n, 3 * width), BF),
            sds((n, width), F32),
            sds((24, width), F32),
            sds((2, 16, own, 2 * width), BF),
        ),
        in_specs=[SM] + [VM] * 6 + [ANY, ANY, ANY, VM, ANY, ANY],
        out_specs=(VM,) * 7,
        scratch_shapes=[
            pltpu.VMEM((M, 16 * rows, hid), BF),
            full, full, part, part, full, full,
            pltpu.VMEM((M, 16 * rows, quarter), BF),
            pltpu.VMEM((4, M, 4 * rows, quarter), BF),
            pltpu.VMEM((4, M, 4 * rows, quarter), BF),
            pltpu.VMEM((3, M, rows, quarter), BF),
            pltpu.VMEM((n, 3 * width), BF),
            pltpu.VMEM((n, width), BF),
            pltpu.VMEM((n, width), BF),
            pltpu.VMEM((2, width, n), BF),
            pltpu.VMEM((2, 128, width), BF),
            pltpu.VMEM((n, width), F32),
            pltpu.VMEM((n, width), BF),
            pltpu.VMEM((n, width), BF),
            pltpu.VMEM((n, n), F32),
            pltpu.VMEM((width, width), F32),
            pltpu.VMEM((2, 4, 16, own, width), BF),
            pltpu.VMEM((4, 16, own, width), BF),
            DMA((5,)), DMA((6, C, 4)), DMA((6, C, 4)), DMA((3,)), DMA((3,)), DMA((2, 4)), DMA((2, 4)),
            DMA((4,)), DMA((4,)),
        ],
        compiler_params=pltpu.CompilerParams(
            collective_id=1, has_side_effects=True, vmem_limit_bytes=63 << 20
        ),
        name="back",
    )(res, vec, ub, x, og, fsum, bsum, proj, mixed, activ, wout, cgrads, grads)


def tail_kernel(
    C, vec, x, d_proj, d_after, wqkv, vin, gq,
    qkv_out, out_out, d_in, vout,
    g, bx, by, bdx, bdy, bzu, bzd, dn, vs, vr, ws, wr, wo,
    lsem, ss, sr, vss, vsr,
):
    p = Place()
    n, width = x.shape
    load = pltpu.make_async_copy(gq, g, lsem)
    load.start()
    p.barrier(far=True)

    def write(c, v):
        at = pl.ds(pl.multiple_of(c * width, 128), width)
        qkv_out[:, at] = v[0]
        if isinstance(c, int):
            if c == 0:
                qkv_out[:, 2 * width:] = v[1]
            else:
                out_out[...] = v[1]
            return

        @pl.when(c == 0)
        def _():
            qkv_out[:, 2 * width:] = v[1]

        @pl.when(c == 1)
        def _():
            out_out[...] = v[1]

    rs = RS(p, g, (bx, by, bdx, bdy, bzu, bzd), ss, sr, C, write, (None, 1, 3, 4))
    steps = [(p.dp, p.other), (p.xn, p.mp), (p.yn, p.mp), (p.z1, p.mp), (p.z2, p.mp)]

    def early(i):
        return remote(vs.at[i], vr.at[i], vss.at[0, i], vsr.at[0, i], *steps[i])

    def late(i):
        return remote(ws.at[i], wr.at[i], vss.at[1, i], vsr.at[1, i], *steps[i])

    def advance(i, hop, sent, got, out):
        hop(i).wait()
        v = sent[i] + got[i]
        if i < 4:
            sent[i + 1] = v
            hop(i + 1).start()
        else:
            out[...] = v

    vs[0] = vin[...]
    ws[0] = jnp.zeros((8, width), F32)
    early(0).start()
    load.wait()
    for t in range(4 * C):
        rs.s1(t)
    third = width // 3
    for j in range(3):
        at = slice(j * third, (j + 1) * third)
        dn[:, at] = lax.dot_general(d_proj[...], wqkv[at, :], NT, preferred_element_type=F32)
        rs.tick(1 + j)
        advance(j, early, vs, vr, vout)

    @pl.loop(0, n // CHUNK)
    def _(r):
        at = pl.ds(pl.multiple_of(r * CHUNK, CHUNK), CHUNK)
        hat, inv = norm_parts(x[at, :].astype(F32))
        d = dn[at, :]
        ws[0, G_AG:G_AG + 1, :] += colsum(d * hat)
        ws[0, G_AB:G_AB + 1, :] += colsum(d)
        d_in[at, :] = (d_after[at, :] + norm_back(hat, inv, d * vec[V_AG:V_AG + 1, :])).astype(BF)

    late(0).start()
    advance(3, early, vs, vr, vout)
    rs.tick(4)
    for i in range(5):
        rs.tick(5 + i)
        if i == 1:
            advance(4, early, vs, vr, vout)
        advance(i, late, ws, wr, wo)
    vout[:2, :] = wo[:2, :]
    for t in range(10, 4 * C + 4):
        rs.tick(t)
    pl.loop(0, 4 * C)(rs.finish)


def tail(vec, x, d_proj, d_after, wqkv, vsum, gq, C=2):
    n, width = x.shape
    rows = width // 32
    sds = jax.ShapeDtypeStruct
    full = pltpu.VMEM((4, 2, rows, 2 * width), BF)
    part = pltpu.VMEM((4, 1, rows, 2 * width), BF)
    return pl.pallas_call(
        functools.partial(tail_kernel, C),
        out_shape=(
            sds((rows, 3 * width), F32),
            sds((rows, width), F32),
            sds((n, width), BF),
            sds((24, width), F32),
        ),
        in_specs=[VM] * 6 + [ANY],
        out_specs=(VM,) * 4,
        scratch_shapes=[
            pltpu.VMEM((2, 16, rows, 2 * width), BF),
            full, full, part, part, full, full,
            pltpu.VMEM((n, width), F32),
            pltpu.VMEM((5, 24, width), F32),
            pltpu.VMEM((5, 24, width), F32),
            pltpu.VMEM((5, 8, width), F32),
            pltpu.VMEM((5, 8, width), F32),
            pltpu.VMEM((8, width), F32),
            DMA, DMA((6, C, 4)), DMA((6, C, 4)), DMA((2, 5)), DMA((2, 5)),
        ],
        compiler_params=pltpu.CompilerParams(
            collective_id=2, has_side_effects=True, vmem_limit_bytes=60 << 20
        ),
        name="tail",
    )(vec, x, d_proj, d_after, wqkv, vsum, gq)


def deliver_kernel(
    v, block, d_in, qkv, out, up, down,
    block_o, d_in_o, ag_o, ab_o, qkv_o, qv_o, out_o, ob_o, as_o, fs_o, fg_o, fb_o,
    up_o, ub_o, down_o, db_o,
):
    width = v.shape[1]
    for src, dst in (
        (block, block_o), (d_in, d_in_o), (qkv, qkv_o), (out, out_o), (up, up_o), (down, down_o),
    ):
        dst[...] = src[...]
    for row, dst in ((G_AG, ag_o), (G_AB, ab_o), (G_OB, ob_o), (G_AS, as_o), (G_FS, fs_o)):
        dst[...] = v[row:row + 1, :].reshape(width)
    for row, dst in ((G_QB, qv_o), (G_FG, fg_o), (G_FB, fb_o), (G_DB, db_o)):
        dst[...] = v[row:row + 2, :]
    for e in range(2):
        for j in range(4):
            row = G_UB + 4 * e + j
            ub_o[e:e + 1, j * width:(j + 1) * width] = v[row:row + 1, :]


def deliver(v, block, d_in, qkv, out, up, down):
    width = v.shape[1]
    like = lambda a: jax.ShapeDtypeStruct(a.shape, a.dtype)
    one = jax.ShapeDtypeStruct((width,), F32)
    two = jax.ShapeDtypeStruct((2, width), F32)
    wide = jax.ShapeDtypeStruct((2, 4 * width), F32)
    return pl.pallas_call(
        deliver_kernel,
        out_shape=(
            like(block), like(d_in), one, one, like(qkv), two, like(out), one, one, one,
            two, two, like(up), wide, like(down), two,
        ),
        in_specs=[VM] * 7,
        out_specs=(VM,) * 16,
        compiler_params=pltpu.CompilerParams(vmem_limit_bytes=40 << 20),
        name="deliver",
    )(v, block, d_in, qkv, out, up, down)


def local_shards(
    layer_input_rows,
    resolution,
    attn_gain,
    attn_bias,
    qkv_weight,
    qv_bias,
    out_weight,
    out_bias,
    attn_scale,
    ffn_scale,
    ffn_gain,
    ffn_bias,
    up_weight,
    up_bias,
    down_weight,
    down_bias,
    output_gradient,
):
    x, og = layer_input_rows, output_gradient
    width = x.shape[1]
    small = (
        attn_gain, attn_bias, qv_bias, out_bias, attn_scale, ffn_scale, ffn_gain, ffn_bias, down_bias
    )
    proj, activ, mixed, vec, ub, fsum, bsum, cgrads, grads = front(
        resolution, small, up_bias, x, og, qkv_weight, out_weight, up_weight, down_weight
    )
    up_weight_grad, down_weight_grad, block_output, d_proj, d_after, vsum, gq = back(
        resolution, vec, ub, x, og, fsum, bsum, proj, mixed, activ, out_weight, cgrads, grads
    )
    qkv_out, out_out, input_grad, v = tail(
        vec, x, d_proj, d_after, qkv_weight, vsum, gq
    )
    return deliver(
        v, block_output, input_grad, qkv_out, out_out, up_weight_grad, down_weight_grad
    )


def solution(mesh):
    placed = (
        P(("dp", "mp"), None),
        P(("dp", "mp")),
        P(),
        P(),
        P(),
        P(),
        P(),
        P(),
        P(),
        P(),
        P(),
        P(),
        P(None, "dp", "mp"),
        P(None, "mp"),
        P(None, "dp", "mp"),
        P(),
        P(("dp", "mp"), None),
    )
    fast = mesh.shape["dp"] == 16 and mesh.shape["mp"] == 2
    return jax.shard_map(
        local_shards if fast else shards,
        mesh=mesh,
        in_specs=placed,
        out_specs=(
            P(("dp", "mp"), None),
            P(("dp", "mp"), None),
            P(),
            P(),
            P(("dp", "mp"), None),
            P(),
            P(("dp", "mp"), None),
            P(),
            P(),
            P(),
            P(),
            P(),
            P(None, "dp", "mp"),
            P(),
            P(None, "dp", "mp"),
            P(),
        ),
        check_vma=False,
    )
```

```python
import functools

import jax
import jax.numpy as jnp
from jax import lax
from jax.experimental import pallas as pl
from jax.experimental.pallas import tpu as pltpu
from jax.sharding import PartitionSpec as P

MESHID = pl.DeviceIdType.MESH
BF = jnp.bfloat16
F32 = jnp.float32

HEADS = 12
PATCH_SMALL = 197
PATCH_LARGE = 577
CAPTION = 40


NORM_EPS = 1e-06
HIGH = lax.Precision.HIGHEST


def layer_norm(field, gain, shift):
    center = field - jnp.mean(field, axis=-1, keepdims=True)
    spread = jnp.mean(center * center, axis=-1, keepdims=True)
    return center * lax.rsqrt(spread + NORM_EPS) * gain + shift


def exact_gelu(field):
    return jax.nn.gelu(field, approximate=False)


def ceil_div(numer, denom):
    return -(-numer // denom)


def slot_layout(res_group, row_count):
    position = jnp.arange(row_count, dtype=jnp.int32)
    small_len = PATCH_SMALL + CAPTION
    large_kind = jnp.where(
        position < PATCH_LARGE, 1, jnp.where(position < PATCH_LARGE + CAPTION, 0, 2)
    )
    large_segment = jnp.where(position < PATCH_LARGE + CAPTION, 0, 2)
    within = position % small_len
    small_kind = jnp.where(position < 2 * small_len, jnp.where(within < PATCH_SMALL, 1, 0), 2)
    small_segment = jnp.where(position < 2 * small_len, position // small_len, 2)
    row_kind = jnp.where(res_group == 1, large_kind, small_kind).astype(jnp.int32)
    segment = jnp.where(res_group == 1, large_segment, small_segment)
    return (row_kind, segment)


def contract_rows(left, right):
    return lax.dot_general(
        left, right, (((0,), (0,)), ((), ())), preferred_element_type=jnp.float32
    )


def contract_cols(left, right):
    return lax.dot_general(
        left, right, (((1,), (1,)), ((), ())), preferred_element_type=jnp.float32
    )


def shards(
    layer_input_rows,
    resolution,
    attn_gain,
    attn_bias,
    qkv_weight,
    qv_bias,
    out_weight,
    out_bias,
    attn_scale,
    ffn_scale,
    ffn_gain,
    ffn_bias,
    up_weight,
    up_bias,
    down_weight,
    down_bias,
    output_gradient,
):
    model_width = layer_input_rows.shape[1]
    slot_count = resolution.shape[0]
    slot_rows = layer_input_rows.shape[0] // slot_count
    head_count = HEADS
    head_width = model_width // head_count
    score_scale = head_width ** (-0.5)
    hidden_part = up_weight.shape[2]
    dp_count = lax.axis_size("dp")
    mp_count = lax.axis_size("mp")
    dp_index = lax.axis_index("dp")
    mp_index = lax.axis_index("mp")
    lang_count = dp_count // 4
    vis_count = dp_count - lang_count
    capacity = max(
        ceil_div(slot_count * PATCH_LARGE, vis_count),
        ceil_div(2 * slot_count * CAPTION, lang_count),
    )
    recv_rows = dp_count * capacity
    kinds, segments = jax.vmap(lambda res_group: slot_layout(res_group, slot_rows))(resolution)
    row_kind = kinds.reshape(-1)
    live_rows = (row_kind != 2).astype(jnp.float32)[:, None]
    vision = (row_kind == 1)[:, None]
    kind_onehot = jnp.stack([row_kind == 0, row_kind == 1], axis=1).astype(jnp.float32)
    rank_vis = jnp.cumsum((row_kind == 1).astype(jnp.int32)) - 1
    rank_txt = jnp.cumsum((row_kind == 0).astype(jnp.int32)) - 1
    target = jnp.where(
        row_kind == 1,
        (rank_vis + dp_index) % vis_count,
        vis_count + (rank_txt + dp_index) % lang_count,
    )
    position = jnp.where(row_kind == 1, rank_vis // vis_count, rank_txt // lang_count)
    slot_index = jnp.where(row_kind == 2, recv_rows, target * capacity + position)

    def to_slots(row_values):
        buffer = (
            jnp.zeros((recv_rows, model_width), row_values.dtype)
            .at[slot_index]
            .set(row_values, mode="drop")
        )
        return buffer.reshape(dp_count, capacity, model_width)

    def from_slots(buffer):
        return jnp.take(
            buffer.reshape(recv_rows, model_width), slot_index, axis=0, mode="fill", fill_value=0
        )

    my_expert = jnp.where(dp_index < vis_count, 1, 0)
    full_up, full_down = (
        lax.all_gather(up_weight, "dp", axis=1, tiled=True),
        lax.all_gather(down_weight, "dp", axis=1, tiled=True),
    )
    own_up = jnp.where(my_expert == 1, full_up[1], full_up[0])
    own_down = jnp.where(my_expert == 1, full_down[1], full_down[0])
    own_up_bias = jnp.where(my_expert == 1, up_bias[1], up_bias[0])
    own_down_bias = jnp.where(my_expert == 1, down_bias[1], down_bias[0])
    x_float = layer_input_rows.astype(jnp.float32)
    normed, norm_pull = jax.vjp(layer_norm, x_float, attn_gain, attn_bias)
    activ = normed.astype(jnp.bfloat16)
    projected = jnp.dot(activ, qkv_weight, preferred_element_type=jnp.float32)
    query = (projected[:, :model_width] + qv_bias[0]).astype(jnp.bfloat16)
    keys = projected[:, model_width : 2 * model_width].astype(jnp.bfloat16)
    values = (projected[:, 2 * model_width :] + qv_bias[1]).astype(jnp.bfloat16)
    query_slots = query.reshape(slot_count, slot_rows, head_count, head_width)
    key_slots = keys.reshape(slot_count, slot_rows, head_count, head_width)
    value_slots = values.reshape(slot_count, slot_rows, head_count, head_width)

    def slot_scores(query_heads, key_heads, segment):
        raw_scores = (
            jnp.einsum("qhd,khd->hqk", query_heads, key_heads, preferred_element_type=jnp.float32)
            * score_scale
        )
        same_seq = (segment[:, None] == segment[None, :])[None]
        return jnp.where(same_seq, raw_scores, -1000000000.0)

    def attend(block_item):
        query_heads, key_heads, value_heads, segment = block_item
        masked = slot_scores(query_heads, key_heads, segment)
        row_max = jnp.max(masked, axis=-1, keepdims=True)
        weights_exp = jnp.exp(masked - row_max)
        row_total = jnp.sum(weights_exp, axis=-1, keepdims=True)
        attn_probs = (weights_exp / row_total).astype(jnp.bfloat16)
        attn_mixed = jnp.einsum(
            "hqk,khd->qhd", attn_probs, value_heads, preferred_element_type=jnp.float32
        )
        log_total = (row_max + jnp.log(row_total))[..., 0]
        return (attn_mixed.reshape(slot_rows, model_width).astype(jnp.bfloat16), log_total)

    attn_mixed, log_totals = lax.map(attend, (query_slots, key_slots, value_slots, segments))
    attn_mixed = attn_mixed.reshape(-1, model_width)
    branch = jnp.dot(attn_mixed, out_weight, preferred_element_type=jnp.float32) + out_bias
    after_attn = x_float + live_rows * attn_scale * branch
    gain_rows = jnp.where(vision, ffn_gain[1], ffn_gain[0])
    shift_rows = jnp.where(vision, ffn_bias[1], ffn_bias[0])
    ffn_normed, norm2_pull = jax.vjp(layer_norm, after_attn, gain_rows, shift_rows)
    sent_rows = ffn_normed.astype(jnp.bfloat16)
    arrived = lax.all_to_all(
        to_slots(sent_rows), "dp", split_axis=0, concat_axis=0, tiled=True
    ).reshape(recv_rows, model_width)
    paired = lax.all_gather(arrived, "mp", axis=0, tiled=True)
    preact = jnp.dot(paired, own_up, preferred_element_type=jnp.float32) + own_up_bias
    hidden, gelu_pull = jax.vjp(exact_gelu, preact)
    hidden_low = hidden.astype(jnp.bfloat16)
    partial_out = contract_cols(hidden_low, own_down)
    expert_sum = (
        lax.psum_scatter(
            partial_out.astype(jnp.bfloat16), "mp", scatter_dimension=0, tiled=True
        ).astype(jnp.float32)
        + own_down_bias
    )
    returned = lax.all_to_all(
        expert_sum.astype(jnp.bfloat16).reshape(dp_count, capacity, model_width),
        "dp",
        split_axis=0,
        concat_axis=0,
        tiled=True,
    )
    expert_rows = from_slots(returned).astype(jnp.float32)
    block_output = (after_attn + live_rows * ffn_scale * expert_rows).astype(jnp.bfloat16)
    grad_float = output_gradient.astype(jnp.float32)
    d_expert = (live_rows * ffn_scale * grad_float).astype(jnp.bfloat16)
    ffn_scale_grad = jnp.sum(live_rows * expert_rows * grad_float, axis=0)
    down_bias_grad = jnp.dot(kind_onehot.T, d_expert.astype(jnp.float32), precision=HIGH)
    arrived_grad = lax.all_to_all(
        to_slots(d_expert), "dp", split_axis=0, concat_axis=0, tiled=True
    ).reshape(recv_rows, model_width)
    paired_grad = lax.all_gather(arrived_grad, "mp", axis=0, tiled=True)
    d_hidden = jnp.dot(paired_grad, own_down, preferred_element_type=jnp.float32)
    d_preact = gelu_pull(d_hidden)[0].astype(jnp.bfloat16)
    own_down_grad = contract_rows(paired_grad, hidden_low)
    own_up_grad = contract_rows(paired, d_preact)
    own_bias_grad = jnp.sum(d_preact.astype(jnp.float32), axis=0)
    d_normed_part = contract_cols(d_preact, own_up)
    d_normed = lax.psum_scatter(
        d_normed_part.astype(jnp.bfloat16), "mp", scatter_dimension=0, tiled=True
    )
    back_grad = lax.all_to_all(
        d_normed.reshape(dp_count, capacity, model_width),
        "dp",
        split_axis=0,
        concat_axis=0,
        tiled=True,
    )
    d_ffn_normed = from_slots(back_grad).astype(jnp.float32)
    d_after_part, gain_grad_rows, shift_grad_rows = norm2_pull(d_ffn_normed)
    ffn_gain_grad = jnp.dot(kind_onehot.T, gain_grad_rows, precision=HIGH)
    ffn_bias_grad = jnp.dot(kind_onehot.T, shift_grad_rows, precision=HIGH)
    d_after = grad_float + d_after_part
    d_branch = (live_rows * attn_scale * d_after).astype(jnp.bfloat16)
    attn_scale_grad = jnp.sum(live_rows * branch * d_after, axis=0)
    out_bias_grad = jnp.sum(d_branch.astype(jnp.float32), axis=0)
    out_weight_grad = contract_rows(attn_mixed, d_branch)
    d_mixed = contract_cols(d_branch, out_weight).astype(jnp.bfloat16)
    d_mixed_slots = d_mixed.reshape(slot_count, slot_rows, head_count, head_width)

    def attend_back(block_item):
        query_heads, key_heads, value_heads, segment, log_total, d_heads = block_item
        masked = slot_scores(query_heads, key_heads, segment)
        probs_full = jnp.exp(masked - log_total[..., None])
        d_probs = jnp.einsum(
            "qhd,khd->hqk", d_heads, value_heads, preferred_element_type=jnp.float32
        )
        row_delta = jnp.sum(probs_full * d_probs, axis=-1, keepdims=True)
        d_scores = (probs_full * (d_probs - row_delta)).astype(jnp.bfloat16)
        probs_low = probs_full.astype(jnp.bfloat16)
        grad_value = jnp.einsum(
            "hqk,qhd->khd", probs_low, d_heads, preferred_element_type=jnp.float32
        )
        grad_query = (
            jnp.einsum("hqk,khd->qhd", d_scores, key_heads, preferred_element_type=jnp.float32)
            * score_scale
        )
        grad_key = (
            jnp.einsum("hqk,qhd->khd", d_scores, query_heads, preferred_element_type=jnp.float32)
            * score_scale
        )
        joined = jnp.concatenate(
            [
                grad_query.reshape(slot_rows, model_width),
                grad_key.reshape(slot_rows, model_width),
                grad_value.reshape(slot_rows, model_width),
            ],
            axis=1,
        )
        return joined.astype(jnp.bfloat16)

    d_projected = lax.map(
        attend_back, (query_slots, key_slots, value_slots, segments, log_totals, d_mixed_slots)
    ).reshape(-1, 3 * model_width)
    qkv_weight_grad = contract_rows(activ, d_projected)
    d_proj_float = d_projected.astype(jnp.float32)
    qv_bias_grad = jnp.stack(
        [
            jnp.sum(d_proj_float[:, :model_width], axis=0),
            jnp.sum(d_proj_float[:, 2 * model_width :], axis=0),
        ]
    )
    d_attn_normed = contract_cols(d_projected, qkv_weight)
    d_input_part, attn_gain_grad, attn_bias_grad = norm_pull(d_attn_normed)
    input_grad = (d_after + d_input_part).astype(jnp.bfloat16)
    expert_pick = (jnp.arange(2) == my_expert).astype(jnp.float32)[:, None, None]
    up_weight_grad, down_weight_grad = (
        lax.psum_scatter(expert_pick * own_up_grad[None], "dp", scatter_dimension=1, tiled=True),
        lax.psum_scatter(expert_pick * own_down_grad[None], "dp", scatter_dimension=1, tiled=True),
    )
    up_bias_full = (
        jnp.zeros((2, mp_count, hidden_part), jnp.float32)
        .at[my_expert, mp_index]
        .set(own_bias_grad)
        .reshape(2, mp_count * hidden_part)
    )
    vector_sums = lax.psum(
        (
            attn_gain_grad,
            attn_bias_grad,
            qv_bias_grad,
            out_bias_grad,
            attn_scale_grad,
            ffn_scale_grad,
            ffn_gain_grad,
            ffn_bias_grad,
            up_bias_full,
            down_bias_grad,
        ),
        ("dp", "mp"),
    )
    matrix_sums = (
        lax.psum_scatter(qkv_weight_grad, ("dp", "mp"), scatter_dimension=0, tiled=True),
        lax.psum_scatter(out_weight_grad, ("dp", "mp"), scatter_dimension=0, tiled=True),
    )
    return (
        block_output,
        input_grad,
        vector_sums[0],
        vector_sums[1],
        matrix_sums[0],
        vector_sums[2],
        matrix_sums[1],
        vector_sums[3],
        vector_sums[4],
        vector_sums[5],
        vector_sums[6],
        vector_sums[7],
        up_weight_grad,
        vector_sums[8],
        down_weight_grad,
        vector_sums[9],
    )


NT = (((1,), (1,)), ((), ()))
TN = (((0,), (0,)), ((), ()))
SMALL = PATCH_SMALL + CAPTION
CAPS = 2 * CAPTION
ANY = pl.BlockSpec(memory_space=pl.ANY)
VM = pl.BlockSpec(memory_space=pltpu.VMEM)
SM = pl.BlockSpec(memory_space=pltpu.SMEM)
DMA = pltpu.SemaphoreType.DMA
CHUNK = 128
V_AG, V_AB, V_QB, V_VB, V_OB, V_AS, V_FS, V_FG, V_FB, V_DB = 0, 1, 2, 3, 4, 5, 6, 7, 9, 11
G_AG, G_AB, G_QB, G_VB, G_OB, G_AS, G_FS, G_FG, G_FB, G_DB, G_UB = 0, 1, 2, 3, 4, 5, 6, 7, 9, 11, 16


def kind_of(res, pos):
    one = lambda c: c.astype(jnp.int32)
    big_seg = 2 * one(pos >= PATCH_LARGE + CAPTION)
    big_kind = 1 - one(pos >= PATCH_LARGE) + big_seg
    small_seg = one(pos >= SMALL) + one(pos >= 2 * SMALL)
    small_pad = one(pos >= 2 * SMALL)
    within = pos - SMALL * small_seg
    small_kind = (1 - small_pad) * one(within < PATCH_SMALL) + 2 * small_pad
    return (
        res * big_kind + (1 - res) * small_kind,
        res * big_seg + (1 - res) * small_seg,
    )


def caption_place(res, slot):
    late = (slot >= CAPTION).astype(jnp.int32)
    big = (1 - late) * (PATCH_LARGE + slot) - late
    small = PATCH_SMALL + slot + late * (SMALL - CAPTION)
    none = (slot >= CAPS).astype(jnp.int32)
    place = res * big + (1 - res) * small
    return (1 - none) * place - none


def iota(shape, dim):
    return lax.broadcasted_iota(jnp.int32, shape, dim)


def fill_bias(res, bias):
    n = bias.shape[0]
    across = kind_of(res, iota((1, n), 1))[1]

    @pl.loop(0, n // CHUNK)
    def _(r):
        base = pl.multiple_of(r * CHUNK, CHUNK)
        down = kind_of(res, iota((CHUNK, 1), 0) + base)[1]
        bias[pl.ds(base, CHUNK), :] = jnp.where(down == across, 0.0, -1000000000.0)


def norm_parts(v):
    center = v - jnp.mean(v, axis=-1, keepdims=True)
    inv = lax.rsqrt(jnp.mean(center * center, axis=-1, keepdims=True) + NORM_EPS)
    return center * inv, inv


def norm_back(xhat, inv, d_hat):
    mean_d = jnp.mean(d_hat, axis=-1, keepdims=True)
    mean_dx = jnp.mean(d_hat * xhat, axis=-1, keepdims=True)
    return inv * (d_hat - mean_d - xhat * mean_dx)


def half_mask(hh, scale):
    lane = iota((1, 128), 1)
    inside = (lane < 64) if hh == 0 else (lane >= 64)
    return jnp.where(inside, scale, 0.0).astype(BF)


def colsum(v):
    return jnp.sum(v, axis=0, keepdims=True)


def dyn_unit(z, k):
    m = k // 2
    zz = z + (z // 2) * (3 - 2 * z)
    u = (1 - m) * (zz + k - 2 * k * zz) + m * k
    w = z // 2
    return u + w * (3 - 2 * u)


class Place:
    def __init__(s):
        s.dp, s.mp = lax.axis_index("dp"), lax.axis_index("mp")
        s.z = s.dp // 4
        s.y = (s.dp // 2) % 2
        s.x = s.dp % 2
        s.xn = s.dp + 1 - 2 * s.x
        s.yn = s.dp + 2 - 4 * s.y
        s.z1 = s.dp + 4 - 8 * (s.z % 2)
        s.z2 = s.dp + 8 - 16 * (s.z // 2)
        s.other = 1 - s.mp
        s.edge = (s.z == 0) | (s.z == 3)
        s.inner = (s.z > 0) & (s.z < 3)
        s.q = s.y * 2 + s.x
        s.dn = s.dp + 3 - 2 * s.x - 4 * s.y
        s.plane = [
            (s.xn, s.y * 2 + 1 - s.x), (s.yn, 2 - 2 * s.y + s.x), (s.dn, 3 - 2 * s.y - s.x)
        ]

    def barrier(s, far=False):
        bar = pltpu.get_barrier_semaphore()
        dp, z = s.dp, s.z

        def sig(d, m):
            pl.semaphore_signal(bar, inc=1, device_id=(d, m), device_id_type=MESHID)

        sig(s.xn, s.mp)
        sig(s.yn, s.mp)
        sig(dp, s.other)
        sig(s.z2 if far else s.dn, s.mp)

        @pl.when(z > 0)
        def _():
            sig(dp - 4, s.mp)

        @pl.when(z < 3)
        def _():
            sig(dp + 4, s.mp)

        pl.semaphore_wait(bar, 5 + ((z + 1) // 2) % 2)


def remote(src, dst, ss, sr, dev, core):
    return pltpu.make_async_remote_copy(
        src_ref=src, dst_ref=dst, send_sem=ss, recv_sem=sr,
        device_id=(dev, core), device_id_type=MESHID,
    )


class AG:
    def __init__(s, place, g, ss, sr, C):
        s.p, s.g, s.ss, s.sr, s.C = place, g, ss, sr, C
        s.rows, s.hid = g.shape[1] // 16, g.shape[2]
        s.ck = s.hid // C
        s.col = place.y * 2 + place.x

    def cp(s, kind, c, u, owner, dev, half=None):
        h = slice(0, 2) if half is None else slice(half, half + 1)
        at = pl.ds(pl.multiple_of(owner * s.rows, 16), s.rows)
        w = s.g.at[h, at, pl.ds(pl.multiple_of(c * s.ck, 128), s.ck)]
        rk = 0 if kind == 1 else kind
        return remote(w, w, s.ss.at[kind, c, u], s.sr.at[rk, c, u], dev, s.p.mp)

    def send(s, k, c, local):
        p = s.p
        z, dp = p.z, p.dp
        u = dyn_unit(z, k)
        owner = u * 4 + s.col
        if not local:
            s.cp(0, c, u, owner, dp).wait_recv()

        @pl.when((u <= z) & (z < 3))
        def _():
            s.cp(0, c, u, owner, dp + 4).start()

        @pl.when((u >= z) & (z > 0))
        def _():
            s.cp(1, c, u, owner, dp - 4).start()

        s.cp(2, c, u, owner, p.xn).start()
        s.cp(3, c, u, owner, p.yn).start()

    def forward(s, k, c):
        p = s.p
        u = dyn_unit(p.z, k)
        xo = u * 4 + p.y * 2 + 1 - p.x
        yo = u * 4 + 2 - 2 * p.y + p.x
        s.cp(2, c, u, xo, p.dp).wait_recv()
        s.cp(5, c, u, xo, p.yn, half=0).start()
        s.cp(3, c, u, yo, p.dp).wait_recv()
        s.cp(4, c, u, yo, p.xn, half=1).start()

    def by_plane(s, edge, inner, f, c):
        @pl.when(s.p.edge)
        def _():
            for k in edge:
                f(k, c)

        if inner:
            @pl.when(s.p.inner)
            def _():
                for k in inner:
                    f(k, c)

    def tick(s, t):
        m, c = t // s.C, t % s.C
        s.by_plane((1 + m,), ((1, 2), (3,), ())[m], lambda k, c: s.send(k, c, False), c)
        if m == 0:
            s.forward(0, c)
        else:
            s.by_plane((m,), ((), (1, 2), (3,))[m], s.forward, c)

    def last(s, c):
        s.by_plane((3,), (), s.forward, c)

    def arrived(s, c):
        for k in range(4):
            u = dyn_unit(s.p.z, k)
            own = u * 4 + s.col
            s.cp(4, c, u, own, s.p.dp, half=1).wait_recv()
            s.cp(5, c, u, own, s.p.dp, half=0).wait_recv()

    def finish(s, k, c):
        p = s.p
        z, dp = p.z, p.dp
        u = dyn_unit(z, k)
        own = u * 4 + s.col
        s.cp(2, c, u, own, dp).wait_send()
        s.cp(3, c, u, own, dp).wait_send()
        s.cp(4, c, u, own, dp, half=1).wait_send()
        s.cp(5, c, u, own, dp, half=0).wait_send()

        @pl.when((u <= z) & (z < 3))
        def _():
            s.cp(0, c, u, own, dp).wait_send()

        @pl.when((u >= z) & (z > 0))
        def _():
            s.cp(1, c, u, own, dp).wait_send()


class CaptionGather:
    def __init__(s, place, own, wc, lsem, ps, pr, zs, zr):
        s.p, s.own, s.wc, s.lsem, s.ps, s.pr, s.zs, s.zr = place, own, wc, lsem, ps, pr, zs, zr
        s.rows, s.quarter = own.shape[1], wc.shape[2]
        s.at = pl.ds(pl.multiple_of(place.dp * s.rows, 16), s.rows)

    def part(s, q):
        return s.own.at[:, :, pl.ds(pl.multiple_of(q * s.quarter, 128), s.quarter)]

    def keep(s):
        return pltpu.make_async_copy(s.part(s.p.q), s.wc.at[:, s.at, :], s.lsem)

    def flat(s, i):
        dev, q = s.p.plane[i]
        return remote(s.part(q), s.wc.at[:, s.at, :], s.ps.at[i], s.pr.at[i], dev, s.p.mp)

    def start(s):
        s.keep().start()
        for i in range(3):
            s.flat(i).start()

    def hop(s, kind, u, dev):
        n = 4 * s.rows
        w = s.wc.at[:, pl.ds(pl.multiple_of(u * n, 16), n), :]
        return remote(w, w, s.zs.at[kind, u], s.zr.at[u], dev, s.p.mp)

    def step(s, k):
        z, dp = s.p.z, s.p.dp
        u = dyn_unit(z, k)
        if isinstance(k, int) and k == 0:
            s.keep().wait()
            for i in range(3):
                s.flat(i).wait()
        else:
            s.hop(0, u, dp).wait_recv()

        @pl.when((u <= z) & (z < 3))
        def _():
            s.hop(0, u, dp + 4).start()

        @pl.when((u >= z) & (z > 0))
        def _():
            s.hop(1, u, dp - 4).start()

    def stage(s, m):
        @pl.when(s.p.edge)
        def _():
            s.step(m)

        if m < 3:
            @pl.when(s.p.inner)
            def _():
                for k in ((1, 2), (3,))[m - 1]:
                    s.step(k)

    def finish(s):
        z, dp = s.p.z, s.p.dp
        for k in range(4):
            u = dyn_unit(z, k)

            @pl.when((u <= z) & (z < 3))
            def _():
                s.hop(0, u, dp + 4).wait_send()

            @pl.when((u >= z) & (z > 0))
            def _():
                s.hop(1, u, dp - 4).wait_send()


class CaptionScatter:
    def __init__(s, place, g, bu, bd, got, ps, pr, zs, zr, out):
        s.p, s.g, s.bu, s.bd, s.got, s.out = place, g, bu, bd, got, out
        s.ps, s.pr, s.zs, s.zr = ps, pr, zs, zr
        s.rows = g.shape[1] // 16

    def win(s, u):
        n = 4 * s.rows
        return s.g.at[:, pl.ds(pl.multiple_of(u * n, 16), n), :]

    def up(s, u):
        return remote(s.win(u), s.bu.at[u], s.zs.at[0, u], s.zr.at[0, u], s.p.dp + 4, s.p.mp)

    def down(s, u):
        return remote(s.win(u), s.bd.at[u], s.zs.at[1, u], s.zr.at[1, u], s.p.dp - 4, s.p.mp)

    def owner(s, q):
        at = pl.multiple_of((s.p.z * 4 + q) * s.rows, 16)
        return s.g.at[:, pl.ds(at, s.rows), :]

    def flat(s, i):
        dev, q = s.p.plane[i]
        return remote(s.owner(q), s.got.at[i], s.ps.at[i], s.pr.at[i], dev, s.p.mp)

    def step(s, k, edge=None):
        z = s.p.z
        u = dyn_unit(z, k)
        o = s.win(u)

        def go(pred, wu, wd, send):
            @pl.when(pred)
            def _():
                v = o[...].astype(F32)
                if wu:
                    s.up(u).wait_recv()
                    v = v + s.bu.at[u][...].astype(F32)
                if wd:
                    s.down(u).wait_recv()
                    v = v + s.bd.at[u][...].astype(F32)
                if wu or wd:
                    o[...] = v.astype(BF)
                if send is not None:
                    send(u).start()

        if k > 0:
            if edge:
                go(u > z, False, False, s.up)
                go(u < z, False, False, s.down)
            else:
                go(u > z, True, False, s.up)
                go(u < z, False, True, s.down)
        else:
            go(z == 0, False, True, None)
            go(z == 3, True, False, None)
            go((z > 0) & (z < 3), True, True, None)
            for i in range(3):
                s.flat(i).start()

    def stage(s, m):
        if m < 3:
            @pl.when(s.p.edge)
            def _():
                s.step(3 - m, True)

        if 0 < m < 4:
            @pl.when(s.p.inner)
            def _():
                s.step(4 - m, False)

        if m == 4:
            s.step(0)

    def finish(s):
        own = s.owner(s.p.q)
        s.out(s.p.q, own[0].astype(F32), own[1].astype(F32))
        for i in range(3):
            s.flat(i).wait()
            s.out(s.p.plane[i][1], s.got[i, 0].astype(F32), s.got[i, 1].astype(F32))
        for k in range(1, 4):
            u = dyn_unit(s.p.z, k)

            @pl.when(u > s.p.z)
            def _():
                s.up(u).wait_send()

            @pl.when(u < s.p.z)
            def _():
                s.down(u).wait_send()


class RS:
    def __init__(s, place, g, bufs, ss, sr, C, write, lags):
        s.p, s.g, s.write, s.lags = place, g, write, lags
        s.bx, s.by, s.bdx, s.bdy, s.bzu, s.bzd = bufs
        s.ss, s.sr, s.C = ss, sr, C
        s.M = g.shape[0]
        s.flat = len(g.shape) == 3
        s.rows = g.shape[1] // 16 if s.flat else g.shape[2]
        s.ck = g.shape[-1] // C
        s.h0 = s.M // 2
        x, y = place.x, place.y
        s.oo = y * 2 + x
        s.ox = y * 2 + 1 - x
        s.oy = 2 - 2 * y + x
        s.od = 3 - 2 * y - x

    def cols(s, c):
        return pl.ds(pl.multiple_of(c * s.ck, 128), s.ck)

    def win(s, u, col, c, lo=0, hi=None):
        hi = s.M if hi is None else hi
        if s.flat:
            at = pl.multiple_of((u * 4 + col) * s.rows, 16)
            return s.g.at[lo:hi, pl.ds(at, s.rows), s.cols(c)]
        return s.g.at[lo:hi, u * 4 + col, :, s.cols(c)]

    def cp(s, kind, u, c, src, dst, dev):
        return remote(src, dst, s.ss.at[kind, c, u], s.sr.at[kind, c, u], dev, s.p.mp)

    def bw(s, b, u, c):
        return b.at[u, :, :, s.cols(c)]

    def c_dy(s, u, c):
        return s.cp(0, u, c, s.win(u, s.od, c, 0, s.h0), s.bw(s.bdy, u, c), s.p.yn)

    def c_dx(s, u, c):
        return s.cp(1, u, c, s.win(u, s.od, c, s.h0), s.bw(s.bdx, u, c), s.p.xn)

    def c_x(s, u, c):
        return s.cp(2, u, c, s.win(u, s.ox, c), s.bw(s.bx, u, c), s.p.xn)

    def c_y(s, u, c):
        return s.cp(3, u, c, s.win(u, s.oy, c), s.bw(s.by, u, c), s.p.yn)

    def c_zu(s, u, c):
        return s.cp(4, u, c, s.win(u, s.oo, c), s.bw(s.bzu, u, c), s.p.dp + 4)

    def c_zd(s, u, c):
        return s.cp(5, u, c, s.win(u, s.oo, c), s.bw(s.bzd, u, c), s.p.dp - 4)

    def item(s, t):
        return dyn_unit(s.p.z, 3 - t // s.C), t % s.C

    def s1(s, t):
        u, c = s.item(t)
        s.c_dy(u, c).start()
        s.c_dx(u, c).start()

    def add(s, dst, src):
        dst[...] = (dst[...].astype(F32) + src[...].astype(F32)).astype(BF)

    def s2(s, t):
        u, c = s.item(t)
        s.c_dy(u, c).wait_recv()
        s.add(s.win(u, s.ox, c, 0, s.h0), s.bw(s.bdy, u, c))
        s.c_x(u, c).start()
        s.c_dx(u, c).wait_recv()
        s.add(s.win(u, s.oy, c, s.h0), s.bw(s.bdx, u, c))
        s.c_y(u, c).start()

    def s3(s, edge, t):
        u, c = s.item(t)
        z = s.p.z
        s.c_x(u, c).wait_recv()
        s.c_y(u, c).wait_recv()
        o = s.win(u, s.oo, c)

        def total(*bufs):
            v = o[...].astype(F32)
            for b in (s.bx, s.by) + bufs:
                v = v + s.bw(b, u, c)[...].astype(F32)
            return v

        def go(pred, wu, wd, send):
            @pl.when(pred)
            def _():
                more = ()
                if wu:
                    s.c_zu(u, c).wait_recv()
                    more += (s.bzu,)
                if wd:
                    s.c_zd(u, c).wait_recv()
                    more += (s.bzd,)
                v = total(*more)
                if send is None:
                    s.write(c, v)
                else:
                    o[...] = v.astype(BF)
                    send(u, c).start()

        up, dn, own = u > z, u < z, u == z
        if edge:
            go(up, False, False, s.c_zu)
            go(dn, False, False, s.c_zd)
            go(own & (z == 0), False, True, None)
            go(own & (z == 3), True, False, None)
        else:
            go(up, True, False, s.c_zu)
            go(dn, False, True, s.c_zd)
            go(own, True, True, None)

    def tick(s, t):
        n = 4 * s.C
        everywhere = s.p.z >= 0
        stages = [
            (lag, f, where)
            for lag, f, where in zip(
                s.lags,
                (s.s1, s.s2, functools.partial(s.s3, True), functools.partial(s.s3, False)),
                (everywhere, everywhere, s.p.edge, s.p.inner),
            )
            if lag is not None
        ]
        for lag, f, where in stages:
            i = t - lag
            if isinstance(t, int):
                if 0 <= i < n:
                    if where is everywhere:
                        f(i)
                    else:
                        @pl.when(where)
                        def _():
                            f(i)
            else:
                @pl.when((i >= 0) & (i < n) & where)
                def _():
                    f(i)

    def finish(s, t):
        u, c = s.item(t)
        for f in (s.c_dy, s.c_dx, s.c_x, s.c_y):
            f(u, c).wait_send()

        @pl.when(u > s.p.z)
        def _():
            s.c_zu(u, c).wait_send()

        @pl.when(u < s.p.z)
        def _():
            s.c_zd(u, c).wait_send()


def load_all(pairs, sem):
    copies = [pltpu.make_async_copy(a, b, sem.at[i]) for i, (a, b) in enumerate(pairs)]
    for c in copies:
        c.start()
    return copies


def front_kernel(
    C, res_ref, a_gain, a_bias, qv_bias, o_bias, a_scale, f_scale, f_gain, f_bias, dn_bias, up_bias,
    x, og, wqkv, wout, up_ref, down_ref,
    proj, activ, mixed, vec, ub, fsum, bsum, cgrads, grads,
    g, wc, cown, bias, qkvb, xall, gall, xt, gt, cr, crt, accf, accb, rcv, stage, hid, dpre, ubg,
    chid, cdpre, pc, prc, prq,
    lsem, ss, sr, ps, pr, cs, cg_r, zs, zr, bs, br,
):
    p = Place()
    n, width = x.shape
    res = res_ref[0]
    ag = AG(p, g, ss, sr, C)
    mine = pl.ds(pl.multiple_of(p.dp * ag.rows, 16), ag.rows)
    loads = load_all(
        [
            (up_ref.at[1], g.at[0, mine, :]), (down_ref.at[1], g.at[1, mine, :]),
            (up_ref.at[0], cown.at[0]), (down_ref.at[0], cown.at[1]),
        ],
        lsem,
    )
    p.barrier()
    for c in loads:
        c.wait()
    capg = CaptionGather(p, cown, wc, lsem.at[4], cs.at[0], cg_r.at[0], zs, zr)
    capg.start()
    for c in range(C):
        ag.send(0, c, True)

    for row, ref in (
        (V_AG, a_gain), (V_AB, a_bias), (V_OB, o_bias), (V_AS, a_scale), (V_FS, f_scale),
    ):
        vec[row:row + 1, :] = ref[...].reshape(1, width)
    for row, ref in ((V_QB, qv_bias), (V_FG, f_gain), (V_FB, f_bias), (V_DB, dn_bias)):
        vec[row:row + 2, :] = ref[...]
    vec[13:16, :] = jnp.zeros((3, width), F32)

    @pl.loop(0, n // CHUNK)
    def _(r):
        at = pl.ds(pl.multiple_of(r * CHUNK, CHUNK), CHUNK)
        hat, _ = norm_parts(x[at, :].astype(F32))
        activ[at, :] = (hat * vec[V_AG:V_AG + 1, :] + vec[V_AB:V_AB + 1, :]).astype(BF)

    ag.tick(0)
    qkvb[:, :width] = vec[V_QB:V_QB + 1, :]
    qkvb[:, width:2 * width] = jnp.zeros((1, width), F32)
    qkvb[:, 2 * width:] = vec[V_VB:V_VB + 1, :]
    part = 384

    @pl.loop(0, 3 * width // part)
    def _(j):
        at = pl.ds(pl.multiple_of(j * part, 128), part)
        v = jnp.dot(activ[...], wqkv[:, at], preferred_element_type=F32)
        proj[:, at] = (v + qkvb[:, at]).astype(BF)

    ag.tick(1)
    fill_bias(res, bias)
    masks = [half_mask(0, 0.125), half_mask(1, 0.125)]
    first = iota((1, 128), 1) < 64

    @pl.loop(0, width // 128)
    def _(h):
        def cols(base):
            return pl.ds(pl.multiple_of(base + h * 128, 128), 128)

        for i, t in ((1, 2), (3, 3), (4, 4)):
            @pl.when(h == i)
            def _():
                ag.tick(t)

        q, k, v = proj[:, cols(0)], proj[:, cols(width)], proj[:, cols(2 * width)]
        outs = []
        for hh in range(2):
            s = lax.dot_general(q * masks[hh], k, NT, preferred_element_type=F32) + bias[...]
            e = jnp.exp(s - jnp.max(s, axis=-1, keepdims=True))
            pr_low = (e * (1.0 / jnp.sum(e, axis=-1, keepdims=True))).astype(BF)
            outs.append(jnp.dot(pr_low, v, preferred_element_type=F32))
        mixed[:, cols(0)] = jnp.where(first, outs[0], outs[1]).astype(BF)

    ag.tick(5)
    capg.step(0)
    half = 256

    @pl.loop(0, width // half)
    def _(j):
        at = pl.ds(pl.multiple_of(j * half, 128), half)
        accf[:n, at] = jnp.dot(mixed[...], wout[:, at], preferred_element_type=F32)

    ag.tick(6)
    img = p.mp * n
    caps = p.mp * 4 * CAPS + p.q * CAPS

    @pl.loop(0, n // CHUNK)
    def _(r):
        base = pl.multiple_of(r * CHUNK, CHUNK)
        at = pl.ds(base, CHUNK)
        to = pl.ds(pl.multiple_of(img + base, 128), CHUNK)
        kind = kind_of(res, iota((CHUNK, 1), 0) + base)[0]
        live = (kind < 2).astype(F32)
        row = x[at, :].astype(F32)
        row = row + live * vec[V_AS:V_AS + 1, :] * (accf[at, :] + vec[V_OB:V_OB + 1, :])
        hat, _ = norm_parts(row)
        gain = jnp.where(kind == 1, vec[V_FG + 1:V_FG + 2, :], vec[V_FG:V_FG + 1, :])
        shift = jnp.where(kind == 1, vec[V_FB + 1:V_FB + 2, :], vec[V_FB:V_FB + 1, :])
        xall[to, :] = (hat * gain + shift).astype(BF)
        gall[to, :] = (live * vec[V_FS:V_FS + 1, :] * og[at, :].astype(F32)).astype(BF)

    ag.tick(7)
    pick = (iota((CAPS, n), 1) == caption_place(res, iota((CAPS, 1), 0))).astype(F32).astype(BF)
    at_img = pl.ds(pl.multiple_of(img, 128), n)
    at_cap = pl.ds(pl.multiple_of(caps, 16), CAPS)
    for i, ref in enumerate((xall, gall)):
        cr[i, at_cap, :] = jnp.dot(pick, ref[at_img, :], preferred_element_type=F32).astype(BF)

    def rows_to(i):
        w = cr.at[:, at_cap, :]
        return remote(w, w, cs.at[1, i], cg_r.at[1, i], p.plane[i][0], p.mp)

    def relay(i):
        q = p.q if i == 3 else p.plane[i][1]
        w = cr.at[:, pl.ds(pl.multiple_of(p.mp * 4 * CAPS + q * CAPS, 16), CAPS), :]
        return remote(w, w, bs.at[i], br.at[i], p.dp, p.other)

    ag.tick(8)
    relay(3).start()

    @pl.loop(0, n // CHUNK)
    def _(r):
        base = pl.multiple_of(r * CHUNK, CHUNK)
        to = pl.ds(pl.multiple_of(img + base, 128), CHUNK)
        vis = (kind_of(res, iota((CHUNK, 1), 0) + base)[0] == 1).astype(F32)
        gall[to, :] = (gall[to, :].astype(F32) * vis).astype(BF)

    pairs = []
    for i, ref in enumerate((xall, gall)):
        w = ref.at[at_img, :]
        pairs.append(remote(w, w, ps.at[i], pr.at[i], p.dp, p.other))
        pairs[-1].start()
    capg.stage(1)
    accf[...] = jnp.zeros(accf.shape, F32)
    accb[...] = jnp.zeros(accb.shape, F32)
    ubg[...] = jnp.zeros(ubg.shape, F32)

    def turn(base):
        @pl.loop(0, n // CHUNK)
        def _(r):
            at = pl.ds(pl.multiple_of(base + r * CHUNK, CHUNK), CHUNK)
            xt[:, at] = xall[at, :].T
            gt[:, at] = gall[at, :].T

    turn(img)
    ag.last(0)
    ag.last(1)
    for c in pairs:
        c.wait()
    turn(p.other * n)
    ag.last(2)
    for i in range(3):
        rows_to(i).start()
    capg.stage(2)
    ck = ag.ck

    def saved(c):
        return pltpu.make_async_copy(stage, grads.at[:, :, c * ck:(c + 1) * ck], lsem.at[2])

    def gelu_pair(v, dh):
        cdf = 0.5 * (1.0 + lax.erf(v * (0.5 ** 0.5)))
        slope = cdf + v * (jnp.exp(v * v * -0.5) * 0.3989422804014327)
        return (v * cdf).astype(BF), (dh * slope).astype(BF)

    def rows_step(c, at):
        here = slice(c * ck, (c + 1) * ck)
        up, down = g[0, :, here], g[1, :, here]
        v = jnp.dot(xall[at, :], up, preferred_element_type=F32) + up_bias[1:2, here]
        dh = jnp.dot(gall[at, :], down, preferred_element_type=F32)
        h_low, d_low = gelu_pair(v, dh)
        hid[at, :] = h_low
        dpre[at, :] = d_low
        accf[at, :] += lax.dot_general(h_low, down, NT, preferred_element_type=F32)
        accb[at, :] += lax.dot_general(d_low, up, NT, preferred_element_type=F32)
        ubg[1:2, here] += colsum(d_low.astype(F32))

    quarter = wc.shape[2]
    my_cols = pl.ds(pl.multiple_of(p.q * quarter, 128), quarter)
    cap_all = 4 * CAPS

    def caption_pair():
        w = pc.at[:, pl.ds(pl.multiple_of(p.other * cap_all, 16), cap_all), :]
        return remote(w, prc, ps.at[4], pr.at[4], p.dp, p.other)

    def caption_flat(i):
        dev, q = p.plane[i]
        w = pc.at[:, pl.ds(pl.multiple_of(p.mp * cap_all + q * CAPS, 16), CAPS), :]
        return remote(w, prq.at[i], cs.at[2, i], cg_r.at[2, i], dev, p.mp)

    def captions():
        for i in range(4):
            relay(i).wait()

        @pl.loop(0, 5)
        def _(r):
            at = pl.ds(pl.multiple_of(r * CHUNK, CHUNK), CHUNK)
            for i in range(2):
                crt[i, :, at] = cr[i, at, :].T

        @pl.loop(0, 2)
        def _(r):
            at = pl.ds(pl.multiple_of(r * cap_all, 16), cap_all)
            v = jnp.dot(cr[0, at, :], wc[0], preferred_element_type=F32) + up_bias[0:1, my_cols]
            dh = jnp.dot(cr[1, at, :], wc[1], preferred_element_type=F32)
            h_low, d_low = gelu_pair(v, dh)
            chid[at, :] = h_low
            cdpre[at, :] = d_low
            pc[0, at, :] = lax.dot_general(h_low, wc[1], NT, preferred_element_type=F32).astype(BF)
            pc[1, at, :] = lax.dot_general(d_low, wc[0], NT, preferred_element_type=F32).astype(BF)
            ubg[0:1, my_cols] += colsum(d_low.astype(F32))

        caption_pair().start()

        @pl.loop(0, width // 256)
        def _(r):
            at = pl.ds(pl.multiple_of(r * 256, 256), 256)
            cgrads[0, at, :] = jnp.dot(
                crt[0, at, :], cdpre[...], preferred_element_type=F32
            ).astype(BF)
            cgrads[1, at, :] = jnp.dot(
                crt[1, at, :], chid[...], preferred_element_type=F32
            ).astype(BF)

        caption_pair().wait()

        @pl.loop(0, 4)
        def _(r):
            at = pl.ds(pl.multiple_of(p.mp * cap_all + r * CAPS, 16), CAPS)
            got = pl.ds(pl.multiple_of(r * CAPS, 16), CAPS)
            for i in range(2):
                pc[i, at, :] = (pc[i, at, :].astype(F32) + prc[i, got, :].astype(F32)).astype(BF)

        for i in range(3):
            caption_flat(i).start()

    back_pairs = []
    for c in range(C):
        ag.arrived(c)

        @pl.loop(0, 2 * n // 256)
        def _(r):
            rows_step(c, pl.ds(pl.multiple_of(r * 256, 256), 256))

        if c == C - 1:
            theirs_img = pl.ds(pl.multiple_of(p.other * n, 128), n)
            for i, (acc, low) in enumerate(((accf, xall), (accb, gall))):
                @pl.loop(0, 2 * n // CHUNK)
                def _(r):
                    at = pl.ds(pl.multiple_of(r * CHUNK, CHUNK), CHUNK)
                    low[at, :] = acc[at, :].astype(BF)

                to = rcv.at[i]
                back_pairs.append(
                    remote(low.at[theirs_img, :], to, ps.at[2 + i], pr.at[2 + i], p.dp, p.other)
                )
                back_pairs[-1].start()
        if c == 1:
            for i in range(3):
                rows_to(i).wait()
                relay(i).start()
            capg.stage(3)
        if c > 0:
            saved(c - 1).wait()

        @pl.loop(0, width // 256)
        def _(r):
            at = pl.ds(pl.multiple_of(r * 256, 256), 256)
            stage[0, at, :] = jnp.dot(xt[at, :], dpre[...], preferred_element_type=F32).astype(BF)
            stage[1, at, :] = jnp.dot(gt[at, :], hid[...], preferred_element_type=F32).astype(BF)

        saved(c).start()
        if c == 1:
            captions()
    ub[...] = jnp.zeros(ub.shape, F32)
    for e in range(2):
        for j in range(2):
            ub[pl.ds(e * 4 + p.mp * 2 + j, 1), :] = ubg[e:e + 1, j * width:(j + 1) * width]
    for c in back_pairs:
        c.wait()
    for i in range(3):
        caption_flat(i).wait()
    for i, (low, out) in enumerate(((xall, fsum), (gall, bsum))):
        @pl.loop(0, n // CHUNK)
        def _(r):
            base = r * CHUNK
            at = pl.ds(pl.multiple_of(base, CHUNK), CHUNK)
            own = low[pl.ds(pl.multiple_of(img + base, CHUNK), CHUNK), :].astype(F32)
            out[at, :] = (own + rcv[i, at, :].astype(F32)).astype(BF)

        own = pc[i, at_cap, :].astype(F32)
        for j in range(3):
            own = own + prq[j, i].astype(F32)
        out[n:, :] = own.astype(BF)
    saved(C - 1).wait()
    pl.loop(0, 4 * C)(lambda t: ag.finish(t // C, t % C))
    capg.finish()


def front(res, small, up_bias, x, og, wqkv, wout, up, down, C=3):
    n, width = x.shape
    _, rows, hid = up.shape
    ck = hid // C
    sds = jax.ShapeDtypeStruct
    wide = 2 * n
    quarter = hid // 4
    caps = 8 * CAPS
    return pl.pallas_call(
        functools.partial(front_kernel, C),
        out_shape=(
            sds((n, 3 * width), BF),
            sds((n, width), BF),
            sds((n, width), BF),
            sds((16, width), F32),
            sds((8, width), F32),
            sds((n + CAPS, width), BF),
            sds((n + CAPS, width), BF),
            sds((2, rows * 16, quarter), BF),
            sds((2, rows * 16, hid), BF),
        ),
        in_specs=[SM] + [VM] * 14 + [ANY, ANY],
        out_specs=(VM,) * 8 + (ANY,),
        scratch_shapes=[
            pltpu.VMEM((2, rows * 16, hid), BF),
            pltpu.VMEM((2, rows * 16, quarter), BF),
            pltpu.VMEM((2, rows, hid), BF),
            pltpu.VMEM((n, n), F32),
            pltpu.VMEM((1, 3 * width), F32),
            pltpu.VMEM((wide, width), BF),
            pltpu.VMEM((wide, width), BF),
            pltpu.VMEM((width, wide), BF),
            pltpu.VMEM((width, wide), BF),
            pltpu.VMEM((2, caps, width), BF),
            pltpu.VMEM((2, width, caps), BF),
            pltpu.VMEM((wide, width), F32),
            pltpu.VMEM((wide, width), F32),
            pltpu.VMEM((2, n, width), BF),
            pltpu.VMEM((2, rows * 16, ck), BF),
            pltpu.VMEM((wide, ck), BF),
            pltpu.VMEM((wide, ck), BF),
            pltpu.VMEM((2, hid), F32),
            pltpu.VMEM((caps, quarter), BF),
            pltpu.VMEM((caps, quarter), BF),
            pltpu.VMEM((2, caps, width), BF),
            pltpu.VMEM((2, caps // 2, width), BF),
            pltpu.VMEM((3, 2, CAPS, width), BF),
            DMA((5,)), DMA((6, C, 4)), DMA((6, C, 4)), DMA((5,)), DMA((5,)),
            DMA((3, 3)), DMA((3, 3)), DMA((2, 4)), DMA((4,)), DMA((4,)), DMA((4,)),
        ],
        compiler_params=pltpu.CompilerParams(
            collective_id=0, has_side_effects=True, vmem_limit_bytes=67043328
        ),
        name="front",
    )(res, *small, up_bias, x, og, wqkv, wout, up, down)


def back_kernel(
    C, res_ref, vec, ub, x, og, fsum, bsum, proj_h, mixed_h, activ_h, wout, cgrads_h, grads_h,
    out_up, out_down, block, d_proj, d_after, vsum, gq,
    g, bx, by, bdx, bdy, bzu, bzd, cg, cbu, cbd, cgot, proj, mixed, activ, turned, capf, branch, d_mixed, d_branch, bias,
    full, split, got, lsem, ss, sr, cps, cpr, czs, czr, ps, pr,
):
    p = Place()
    n, width = x.shape
    res = res_ref[0]
    loads = load_all(
        [(grads_h, g), (proj_h, proj), (mixed_h, mixed), (cgrads_h, cg), (activ_h, activ)], lsem
    )
    p.barrier()

    def write(c, v):
        at = pl.ds(pl.multiple_of(c * (g.shape[2] // C), 128), g.shape[2] // C)
        out_up[1, :, at] = v[0]
        out_down[1, :, at] = v[1]

    def caption_out(q, up, down):
        quarter = cg.shape[2]
        at = pl.ds(pl.multiple_of(q * quarter, 128), quarter)
        out_up[0, :, at] = up
        out_down[0, :, at] = down

    rs = RS(p, g, (bx, by, bdx, bdy, bzu, bzd), ss, sr, C, write, (0, 2, 4, 5))
    cap = CaptionScatter(p, cg, cbu, cbd, cgot, cps, cpr, czs, czr, caption_out)
    loads[0].wait()
    rs.tick(0)
    loads[3].wait()
    cap.stage(0)
    loads[1].wait()
    loads[2].wait()
    loads[4].wait()
    fill_bias(res, bias)
    half = 256

    @pl.loop(0, width // half)
    def _(j):
        at = pl.ds(pl.multiple_of(j * half, 128), half)
        branch[:, at] = jnp.dot(mixed[...], wout[:, at], preferred_element_type=F32)

    rs.tick(1)
    vsum[...] = jnp.zeros(vsum.shape, F32)
    vsum[G_UB:G_UB + 8, :] = ub[...]
    pad = jnp.zeros((128 - CAPS, width), BF)
    for i, ref in enumerate((fsum, bsum)):
        capf[i] = jnp.concatenate([ref[n:, :], pad], axis=0)

    def add(row, v):
        vsum[row:row + 1, :] += colsum(v)

    @pl.loop(0, n // CHUNK)
    def _(r):
        @pl.when(r == 2)
        def _():
            rs.tick(2)

        base = pl.multiple_of(r * CHUNK, CHUNK)
        at = pl.ds(base, CHUNK)
        for i, ref in enumerate((activ, mixed)):
            turned[i, :, at] = ref[at, :].T
        pos = iota((CHUNK, 1), 0) + base
        kind = kind_of(res, pos)[0]
        live = (kind < 2).astype(F32)
        vis = kind == 1
        cap = kind == 0
        pick = (pos == caption_place(res, iota((1, 128), 1))).astype(F32).astype(BF)
        from_cap = jnp.dot(pick, capf[0], preferred_element_type=F32)
        d_cap = jnp.dot(pick, capf[1], preferred_element_type=F32)
        from_img = fsum[at, :].astype(F32)
        d_img = bsum[at, :].astype(F32)
        grad = og[at, :].astype(F32)
        row_branch = branch[at, :] + vec[V_OB:V_OB + 1, :]
        scale = live * vec[V_AS:V_AS + 1, :]
        after = x[at, :].astype(F32) + scale * row_branch
        expert = jnp.where(
            cap, from_cap + vec[V_DB:V_DB + 1, :], from_img + vec[V_DB + 1:V_DB + 2, :]
        ).astype(BF).astype(F32)
        ffn_scale = live * vec[V_FS:V_FS + 1, :]
        block[at, :] = (after + ffn_scale * expert).astype(BF)
        add(G_FS, live * expert * grad)
        d_expert = (ffn_scale * grad).astype(BF).astype(F32)
        add(G_DB, jnp.where(cap, d_expert, 0.0))
        add(G_DB + 1, jnp.where(vis, d_expert, 0.0))
        d_ffn = jnp.where(cap, d_cap, d_img)
        hat, inv = norm_parts(after)
        d_gain = d_ffn * hat
        add(G_FG, jnp.where(cap, d_gain, 0.0))
        add(G_FG + 1, jnp.where(vis, d_gain, 0.0))
        add(G_FB, jnp.where(cap, d_ffn, 0.0))
        add(G_FB + 1, jnp.where(vis, d_ffn, 0.0))
        gain = jnp.where(vis, vec[V_FG + 1:V_FG + 2, :], vec[V_FG:V_FG + 1, :])
        da = grad + norm_back(hat, inv, d_ffn * gain)
        d_after[at, :] = da
        add(G_AS, live * row_branch * da)
        db = (scale * da).astype(BF)
        d_branch[at, :] = db
        add(G_OB, db.astype(F32))

    rs.tick(3)
    cap.stage(1)
    rows = width // 32

    def pair(j):
        return remote(split.at[p.other, j], got.at[j], ps.at[j], pr.at[j], p.dp, p.other)

    def weight_part(j):
        if j < 3:
            right = d_proj[:, j * width:(j + 1) * width]
        else:
            right = d_branch[...]
        full[...] = jnp.dot(turned[j // 3], right, preferred_element_type=F32)

        @pl.loop(0, 16)
        def _(o):
            for core in range(2):
                at = pl.ds(pl.multiple_of((2 * o + core) * rows, 8), rows)
                split[core, j, o] = full[at, :].astype(BF)

        pair(j).start()

    def weight_sum(j):
        pair(j).wait()

        @pl.loop(0, 16)
        def _(o):
            v = split[p.mp, j, o].astype(F32) + got[j, o].astype(F32)
            gq[j // 2, o, :, (j % 2) * width:(j % 2 + 1) * width] = v.astype(BF)

    @pl.loop(0, width // half)
    def _(j):
        at = pl.ds(pl.multiple_of(j * half, 128), half)
        v = lax.dot_general(d_branch[...], wout[at, :], NT, preferred_element_type=F32)
        d_mixed[:, at] = v.astype(BF)

    rs.tick(4)
    weight_part(3)

    ones = [half_mask(0, 1.0), half_mask(1, 1.0)]
    scaled = [half_mask(0, 0.125), half_mask(1, 0.125)]
    first = iota((1, 128), 1) < 64

    @pl.loop(0, width // 128)
    def _(h):
        rs.tick(5 + h)
        for i, m in ((1, 2), (3, 3)):
            @pl.when(h == i)
            def _():
                cap.stage(m)

        def cols(base):
            return pl.ds(pl.multiple_of(base + h * 128, 128), 128)

        q, k, v = proj[:, cols(0)], proj[:, cols(width)], proj[:, cols(2 * width)]
        do = d_mixed[:, cols(0)]
        q_scaled = q * jnp.full((1, 128), 0.125, BF)
        k_turned = (k.astype(F32) * 0.125).T.astype(BF)
        dq, dk, dv = [], [], []
        for hh in range(2):
            s = lax.dot_general(k * scaled[hh], q, NT, preferred_element_type=F32) + bias[...]
            e = jnp.exp(s - jnp.max(s, axis=0, keepdims=True))
            pt = e * (1.0 / jnp.sum(e, axis=0, keepdims=True))
            dpt = lax.dot_general(v * ones[hh], do, NT, preferred_element_type=F32)
            delta = jnp.sum(pt * dpt, axis=0, keepdims=True)
            dst = (pt * (dpt - delta)).astype(BF)
            dv.append(jnp.dot(pt.astype(BF), do, preferred_element_type=F32))
            dk.append(jnp.dot(dst, q_scaled, preferred_element_type=F32))
            dq.append(jnp.dot(k_turned[64 * hh:64 * hh + 64], dst, preferred_element_type=F32))
        dq_all = jnp.concatenate(dq, axis=0).T.astype(BF)
        dv_all = jnp.where(first, dv[0], dv[1]).astype(BF)
        d_proj[:, cols(0)] = dq_all
        d_proj[:, cols(width)] = jnp.where(first, dk[0], dk[1]).astype(BF)
        d_proj[:, cols(2 * width)] = dv_all
        vsum[G_QB:G_QB + 1, cols(0)] = colsum(dq_all.astype(F32))
        vsum[G_VB:G_VB + 1, cols(0)] = colsum(dv_all.astype(F32))

    rs.tick(11)
    cap.stage(4)
    weight_part(0)
    weight_sum(3)
    rs.tick(12)
    weight_part(1)
    weight_sum(0)
    rs.tick(13)
    weight_part(2)
    weight_sum(1)
    rs.tick(14)
    rs.tick(15)
    rs.tick(16)
    cap.finish()
    weight_sum(2)
    pl.loop(0, 4 * C)(rs.finish)


def back(res, vec, ub, x, og, fsum, bsum, proj, mixed, activ, wout, cgrads, grads, C=3):
    quarter = cgrads.shape[2]
    n, width = x.shape
    M, rows, hid = grads.shape[0], grads.shape[1] // 16, grads.shape[2]
    own = width // 32
    sds = jax.ShapeDtypeStruct
    full = pltpu.VMEM((4, M, rows, hid), BF)
    part = pltpu.VMEM((4, M // 2, rows, hid), BF)
    return pl.pallas_call(
        functools.partial(back_kernel, C),
        out_shape=(
            sds((2, rows, hid), F32),
            sds((2, rows, hid), F32),
            sds((n, width), BF),
            sds((n, 3 * width), BF),
            sds((n, width), F32),
            sds((24, width), F32),
            sds((2, 16, own, 2 * width), BF),
        ),
        in_specs=[SM] + [VM] * 6 + [ANY, ANY, ANY, VM, ANY, ANY],
        out_specs=(VM,) * 7,
        scratch_shapes=[
            pltpu.VMEM((M, 16 * rows, hid), BF),
            full, full, part, part, full, full,
            pltpu.VMEM((M, 16 * rows, quarter), BF),
            pltpu.VMEM((4, M, 4 * rows, quarter), BF),
            pltpu.VMEM((4, M, 4 * rows, quarter), BF),
            pltpu.VMEM((3, M, rows, quarter), BF),
            pltpu.VMEM((n, 3 * width), BF),
            pltpu.VMEM((n, width), BF),
            pltpu.VMEM((n, width), BF),
            pltpu.VMEM((2, width, n), BF),
            pltpu.VMEM((2, 128, width), BF),
            pltpu.VMEM((n, width), F32),
            pltpu.VMEM((n, width), BF),
            pltpu.VMEM((n, width), BF),
            pltpu.VMEM((n, n), F32),
            pltpu.VMEM((width, width), F32),
            pltpu.VMEM((2, 4, 16, own, width), BF),
            pltpu.VMEM((4, 16, own, width), BF),
            DMA((5,)), DMA((6, C, 4)), DMA((6, C, 4)), DMA((3,)), DMA((3,)), DMA((2, 4)), DMA((2, 4)),
            DMA((4,)), DMA((4,)),
        ],
        compiler_params=pltpu.CompilerParams(
            collective_id=1, has_side_effects=True, vmem_limit_bytes=63 << 20
        ),
        name="back",
    )(res, vec, ub, x, og, fsum, bsum, proj, mixed, activ, wout, cgrads, grads)


def tail_kernel(
    C, vec, x, d_proj, d_after, wqkv, vin, gq,
    qkv_out, out_out, d_in, vout,
    g, bx, by, bdx, bdy, bzu, bzd, dn, vs, vr, ws, wr, wo,
    lsem, ss, sr, vss, vsr,
):
    p = Place()
    n, width = x.shape
    load = pltpu.make_async_copy(gq, g, lsem)
    load.start()
    p.barrier(far=True)

    def write(c, v):
        at = pl.ds(pl.multiple_of(c * width, 128), width)
        qkv_out[:, at] = v[0]
        if isinstance(c, int):
            if c == 0:
                qkv_out[:, 2 * width:] = v[1]
            else:
                out_out[...] = v[1]
            return

        @pl.when(c == 0)
        def _():
            qkv_out[:, 2 * width:] = v[1]

        @pl.when(c == 1)
        def _():
            out_out[...] = v[1]

    rs = RS(p, g, (bx, by, bdx, bdy, bzu, bzd), ss, sr, C, write, (None, 1, 3, 4))
    steps = [(p.dp, p.other), (p.xn, p.mp), (p.yn, p.mp), (p.z1, p.mp), (p.z2, p.mp)]

    def early(i):
        return remote(vs.at[i], vr.at[i], vss.at[0, i], vsr.at[0, i], *steps[i])

    def late(i):
        return remote(ws.at[i], wr.at[i], vss.at[1, i], vsr.at[1, i], *steps[i])

    def advance(i, hop, sent, got, out):
        hop(i).wait()
        v = sent[i] + got[i]
        if i < 4:
            sent[i + 1] = v
            hop(i + 1).start()
        else:
            out[...] = v

    vs[0] = vin[...]
    ws[0] = jnp.zeros((8, width), F32)
    early(0).start()
    load.wait()
    for t in range(4 * C):
        rs.s1(t)
    third = width // 3
    for j in range(3):
        at = slice(j * third, (j + 1) * third)
        dn[:, at] = lax.dot_general(d_proj[...], wqkv[at, :], NT, preferred_element_type=F32)
        rs.tick(1 + j)
        advance(j, early, vs, vr, vout)

    @pl.loop(0, n // CHUNK)
    def _(r):
        at = pl.ds(pl.multiple_of(r * CHUNK, CHUNK), CHUNK)
        hat, inv = norm_parts(x[at, :].astype(F32))
        d = dn[at, :]
        ws[0, G_AG:G_AG + 1, :] += colsum(d * hat)
        ws[0, G_AB:G_AB + 1, :] += colsum(d)
        d_in[at, :] = (d_after[at, :] + norm_back(hat, inv, d * vec[V_AG:V_AG + 1, :])).astype(BF)

    late(0).start()
    advance(3, early, vs, vr, vout)
    rs.tick(4)
    for i in range(5):
        rs.tick(5 + i)
        if i == 1:
            advance(4, early, vs, vr, vout)
        advance(i, late, ws, wr, wo)
    vout[:2, :] = wo[:2, :]
    for t in range(10, 4 * C + 4):
        rs.tick(t)
    pl.loop(0, 4 * C)(rs.finish)


def tail(vec, x, d_proj, d_after, wqkv, vsum, gq, C=2):
    n, width = x.shape
    rows = width // 32
    sds = jax.ShapeDtypeStruct
    full = pltpu.VMEM((4, 2, rows, 2 * width), BF)
    part = pltpu.VMEM((4, 1, rows, 2 * width), BF)
    return pl.pallas_call(
        functools.partial(tail_kernel, C),
        out_shape=(
            sds((rows, 3 * width), F32),
            sds((rows, width), F32),
            sds((n, width), BF),
            sds((24, width), F32),
        ),
        in_specs=[VM] * 6 + [ANY],
        out_specs=(VM,) * 4,
        scratch_shapes=[
            pltpu.VMEM((2, 16, rows, 2 * width), BF),
            full, full, part, part, full, full,
            pltpu.VMEM((n, width), F32),
            pltpu.VMEM((5, 24, width), F32),
            pltpu.VMEM((5, 24, width), F32),
            pltpu.VMEM((5, 8, width), F32),
            pltpu.VMEM((5, 8, width), F32),
            pltpu.VMEM((8, width), F32),
            DMA, DMA((6, C, 4)), DMA((6, C, 4)), DMA((2, 5)), DMA((2, 5)),
        ],
        compiler_params=pltpu.CompilerParams(
            collective_id=2, has_side_effects=True, vmem_limit_bytes=60 << 20
        ),
        name="tail",
    )(vec, x, d_proj, d_after, wqkv, vsum, gq)


def deliver_kernel(
    v_h, block, d_in, qkv, out, up, down,
    block_o, d_in_o, ag_o, ab_o, qkv_o, qv_o, out_o, ob_o, as_o, fs_o, fg_o, fb_o,
    up_o, ub_o, down_o, db_o, v, sem,
):
    width = v.shape[1]
    for copy in load_all(
        [
            (v_h, v), (block, block_o), (d_in, d_in_o), (qkv, qkv_o), (out, out_o),
            (up, up_o), (down, down_o),
        ],
        sem,
    ):
        copy.wait()
    for row, dst in ((G_AG, ag_o), (G_AB, ab_o), (G_OB, ob_o), (G_AS, as_o), (G_FS, fs_o)):
        dst[...] = v[row:row + 1, :].reshape(width)
    for row, dst in ((G_QB, qv_o), (G_FG, fg_o), (G_FB, fb_o), (G_DB, db_o)):
        dst[...] = v[row:row + 2, :]
    for e in range(2):
        for j in range(4):
            row = G_UB + 4 * e + j
            ub_o[e:e + 1, j * width:(j + 1) * width] = v[row:row + 1, :]


def deliver(v, block, d_in, qkv, out, up, down):
    width = v.shape[1]
    like = lambda a: jax.ShapeDtypeStruct(a.shape, a.dtype)
    one = jax.ShapeDtypeStruct((width,), F32)
    two = jax.ShapeDtypeStruct((2, width), F32)
    wide = jax.ShapeDtypeStruct((2, 4 * width), F32)
    return pl.pallas_call(
        deliver_kernel,
        out_shape=(
            like(block), like(d_in), one, one, like(qkv), two, like(out), one, one, one,
            two, two, like(up), wide, like(down), two,
        ),
        in_specs=[ANY] * 7,
        out_specs=(VM,) * 16,
        scratch_shapes=[pltpu.VMEM(v.shape, F32), DMA((7,))],
        compiler_params=pltpu.CompilerParams(vmem_limit_bytes=62 << 20),
        name="deliver",
    )(v, block, d_in, qkv, out, up, down)


def local_shards(
    layer_input_rows,
    resolution,
    attn_gain,
    attn_bias,
    qkv_weight,
    qv_bias,
    out_weight,
    out_bias,
    attn_scale,
    ffn_scale,
    ffn_gain,
    ffn_bias,
    up_weight,
    up_bias,
    down_weight,
    down_bias,
    output_gradient,
):
    x, og = layer_input_rows, output_gradient
    width = x.shape[1]
    small = (
        attn_gain, attn_bias, qv_bias, out_bias, attn_scale, ffn_scale, ffn_gain, ffn_bias, down_bias
    )
    proj, activ, mixed, vec, ub, fsum, bsum, cgrads, grads = front(
        resolution, small, up_bias, x, og, qkv_weight, out_weight, up_weight, down_weight
    )
    up_weight_grad, down_weight_grad, block_output, d_proj, d_after, vsum, gq = back(
        resolution, vec, ub, x, og, fsum, bsum, proj, mixed, activ, out_weight, cgrads, grads
    )
    qkv_out, out_out, input_grad, v = tail(
        vec, x, d_proj, d_after, qkv_weight, vsum, gq
    )
    return deliver(
        v, block_output, input_grad, qkv_out, out_out, up_weight_grad, down_weight_grad
    )


def solution(mesh):
    placed = (
        P(("dp", "mp"), None),
        P(("dp", "mp")),
        P(),
        P(),
        P(),
        P(),
        P(),
        P(),
        P(),
        P(),
        P(),
        P(),
        P(None, "dp", "mp"),
        P(None, "mp"),
        P(None, "dp", "mp"),
        P(),
        P(("dp", "mp"), None),
    )
    fast = mesh.shape["dp"] == 16 and mesh.shape["mp"] == 2
    return jax.shard_map(
        local_shards if fast else shards,
        mesh=mesh,
        in_specs=placed,
        out_specs=(
            P(("dp", "mp"), None),
            P(("dp", "mp"), None),
            P(),
            P(),
            P(("dp", "mp"), None),
            P(),
            P(("dp", "mp"), None),
            P(),
            P(),
            P(),
            P(),
            P(),
            P(None, "dp", "mp"),
            P(),
            P(None, "dp", "mp"),
            P(),
        ),
        check_vma=False,
    )
```
